128 devices in a mesh: scan: 64 (over x, y, z_lo, core), mode: 2 (over z_hi).
Axes of the slice: x: 4, y: 4, z: 4 (z_hi: 2, z_lo: 2; z = z_hi * 2 + z_lo), core: 2. Of those that a mesh axis runs over, the one named last changes fastest.
Arguments:
- object_tiles: float32 [64, 2, 512, 512], P('scan'), may hold values from -5 to 5
- probe_modes: float32 [4, 2, 512, 512], P('mode'), may hold values from -5 to 5
- amplitudes: float32 [64, 3, 512, 512], P('scan'), may hold values from 0.5 to 3
- offsets: int32 [64, 3, 2], P('scan'), may hold values from 1 to 511, as said below
- counts: int32 [64], P('scan'), may hold values from 1 to 3, as said below
Outputs:
- object_grad: float32 [64, 2, 512, 512], P('scan', 'mode')
- probe_grad: float32 [4, 2, 512, 512], P('mode')
- position_grad: float32 [64, 3, 2], P('scan')
The draws below stay inside these ranges and needn't reach their ends.
Inputs may be any that keep to these rules, and one draw needn't show every extreme that they name: `offsets`: A slot's window lies within its device's 2 x 2 arrangement of tiles. Slots s >= counts[d] of device d are empty.
All inputs are finite; a program needn't handle non-finite values.
Results may differ from the reference program's by a relative error of at most 0.006.
The reference program's roundings to bfloat16 on the way count: a program that leaves them out, or rounds other values in their place, can miss the bound.
Values sent between devices are 32-bit elements; how exact they have to be, the bound alone decides.
A program may use at most 192 MiB of HBM per device.

```python
import math
import jax
import jax.numpy as jnp
from jax import lax

PATCH = 512
MODES = 4
TILE = 512
GCOLS = 8
CAP = 3
N_SCAN = 64


def draw_offsets(key, part):
    key_values, key_high, key_low, key_first = jax.random.split(key, 4)
    values = jax.random.randint(key_values, (N_SCAN, CAP, 2), 1, TILE, dtype=jnp.int32)
    first = jax.random.randint(key_first, (N_SCAN, 2), TILE // 2, TILE, dtype=jnp.int32)
    values = values.at[:, 0, :].set(first)
    high_device = jax.random.randint(key_high, (), 0, N_SCAN, dtype=jnp.int32)
    low_device = jax.random.randint(key_low, (), 0, N_SCAN, dtype=jnp.int32)
    values = values.at[low_device, CAP - 1, 1].set(1)
    values = values.at[high_device, 0, 0].set(TILE - 1)
    return values


def draw_counts(key, part):
    key_values, key_high, key_low = jax.random.split(jax.random.fold_in(key, 7), 3)
    values = jax.random.randint(key_values, (N_SCAN,), 1, CAP + 1, dtype=jnp.int32)
    high_device = jax.random.randint(key_high, (), 0, N_SCAN, dtype=jnp.int32)
    low_device = jax.random.randint(key_low, (), 0, N_SCAN, dtype=jnp.int32)
    values = values.at[low_device].set(1)
    values = values.at[high_device].set(CAP)
    return values


def steps_of(stream_key, dims, cuts, least, high):
    def one(axis_at, parts):
        steps = jax.random.uniform(jax.random.fold_in(jax.random.fold_in(stream_key, 6), axis_at), (parts,), jnp.float32, least / len(cuts), high / len(cuts))
        return jnp.repeat(jnp.exp(steps), dims[axis_at] // parts).reshape((-1,) + (1,) * (len(dims) - axis_at - 1))

    gain = one(*cuts[0])
    for cut in cuts[1:]:
        gain = gain * one(*cut)
    return gain


def noise(key, dims, spread, reach, cuts=(), held_as=jnp.bfloat16):
    factor_of = steps_of(key, dims, cuts, -0.22, 0.18) if cuts else 1.0
    entries = jax.random.normal(key, dims, jnp.float32) * spread * factor_of
    return jnp.minimum(jnp.maximum(entries, -reach), reach).astype(held_as)


def setup_inputs(seed: int = 0) -> dict:
    splits = jax.random.split(jax.random.key(seed), 6)
    object_tiles = noise(splits[0], (N_SCAN, 2, TILE, TILE), 0.7, 5.0, ((0, 64),), jnp.float32)
    probe_modes = noise(splits[1], (MODES, 2, PATCH, PATCH), 0.7, 5.0, ((0, 2),), jnp.float32)
    amplitudes = jnp.clip(0.5 + 2.5 * jax.random.uniform(splits[2], (N_SCAN, CAP, PATCH, PATCH), jnp.float32) ** steps_of(splits[2], (N_SCAN, CAP, PATCH, PATCH), ((0, 64),), -0.2, 0.2), 0.5, 3.0)
    offsets = draw_offsets(jax.random.fold_in(splits[5], 71), 0)
    counts = draw_counts(jax.random.fold_in(splits[5], 71), 0)
    return dict(object_tiles=object_tiles, probe_modes=probe_modes, amplitudes=amplitudes, offsets=offsets, counts=counts)


amp_floor = 1.0

def dft_tables(length_side, direction_sign):
    index_row = jnp.arange(length_side, dtype=jnp.int32)
    product = index_row[:, None] * index_row[None, :] % length_side
    angles = product.astype(jnp.float32) * (2.0 * math.pi / length_side)
    scale_factor = 1.0 / math.sqrt(length_side)
    real_part = jnp.cos(angles) * scale_factor
    imag_part = direction_sign * jnp.sin(angles) * scale_factor
    matrix_table = jnp.stack([jnp.stack([real_part, -imag_part]), jnp.stack([imag_part, real_part])])
    return matrix_table.astype(jnp.bfloat16)

def transform(field, matrix_table):
    table_wide = matrix_table.astype(jnp.float32)
    first_section = jnp.einsum('dcpq,bcqk->bdpk', table_wide, field.astype(jnp.float32)).astype(jnp.bfloat16)
    return jnp.einsum('bcpq,dcqk->bdpk', first_section.astype(jnp.float32), table_wide)

def slot_terms(windows, probe_modes, device_amplitudes, device_count, forward_table, inverse_table):
    slots = windows.shape[0]
    modes_here = probe_modes.shape[0]
    side = probe_modes.shape[-1]
    patch = windows[:, :, 1:-1, 1:-1]
    grad_y = (windows[:, :, 2:, 1:-1] - windows[:, :, :-2, 1:-1]) * 0.5
    grad_x = (windows[:, :, 1:-1, 2:] - windows[:, :, 1:-1, :-2]) * 0.5
    obj_real = patch[:, 0][:, None]
    obj_imag = patch[:, 1][:, None]
    probe_real = probe_modes[:, 0][None]
    probe_imag = probe_modes[:, 1][None]
    exit_real = obj_real * probe_real - obj_imag * probe_imag
    exit_imag = obj_real * probe_imag + obj_imag * probe_real
    exit_wave = jnp.stack([exit_real, exit_imag], axis=2).astype(jnp.bfloat16)
    far_field = transform(exit_wave.reshape(slots * modes_here, 2, side, side), forward_table)
    far_field = far_field.reshape(slots, modes_here, 2, side, side)
    intensity = lax.optimization_barrier(jnp.sum(far_field * far_field, axis=(1, 2)))
    ratio = device_amplitudes / jnp.maximum(jnp.sqrt(intensity), amp_floor)
    correction = (far_field * (ratio - 1.0)[:, None, None]).astype(jnp.bfloat16)
    back_wave = transform(correction.reshape(slots * modes_here, 2, side, side), inverse_table)
    back_wave = back_wave.reshape(slots, modes_here, 2, side, side)
    live_slots = (jnp.arange(slots, dtype=jnp.int32) < device_count).astype(jnp.float32)
    back_wave = back_wave * live_slots[:, None, None, None, None]
    back_real = back_wave[:, :, 0]
    back_imag = back_wave[:, :, 1]
    grad_real = lax.optimization_barrier(jnp.sum(probe_real * back_real + probe_imag * back_imag, axis=1))
    grad_imag = lax.optimization_barrier(jnp.sum(probe_real * back_imag - probe_imag * back_real, axis=1))
    probe_real_grad = lax.optimization_barrier(jnp.sum(obj_real * back_real + obj_imag * back_imag, axis=0))
    probe_imag_grad = lax.optimization_barrier(jnp.sum(obj_real * back_imag - obj_imag * back_real, axis=0))
    position_y = lax.optimization_barrier(jnp.sum(grad_real * grad_y[:, 0] + grad_imag * grad_y[:, 1], axis=(1, 2)))
    position_x = lax.optimization_barrier(jnp.sum(grad_real * grad_x[:, 0] + grad_imag * grad_x[:, 1], axis=(1, 2)))
    positions = jnp.stack([position_y, position_x], axis=1) / side
    return (jnp.stack([grad_real, grad_imag], axis=1), jnp.stack([probe_real_grad, probe_imag_grad], axis=1), positions)

def reference(object_tiles, probe_modes, amplitudes, offsets, counts):
    forward_table = dft_tables(PATCH, -1.0)
    inverse_table = dft_tables(PATCH, 1.0)

    def neighbour_ids(device):
        return [device % N_SCAN, (device + 1) % N_SCAN, (device + GCOLS) % N_SCAN, (device + GCOLS + 1) % N_SCAN]

    def per_device(carry, inputs):
        gradient_tiles, probe_total = carry
        device, device_offsets, device_amplitudes, device_count = inputs
        ids = neighbour_ids(device)
        quads = [object_tiles[ids[k]] for k in range(4)]
        upper = jnp.concatenate([quads[0], quads[1]], axis=2)
        lower = jnp.concatenate([quads[2], quads[3]], axis=2)
        extended = jnp.concatenate([upper, lower], axis=1)
        windows = jnp.stack([lax.dynamic_slice(extended, (jnp.int32(0), device_offsets[slot_id, 0] - 1, device_offsets[slot_id, 1] - 1), (2, PATCH + 2, PATCH + 2)) for slot_id in range(CAP)])
        patch_grad, probe_part, positions = slot_terms(windows, probe_modes, device_amplitudes, device_count, forward_table, inverse_table)
        plane = jnp.zeros((2, 2 * TILE, 2 * TILE), jnp.float32)
        for slot_id in range(CAP):
            start = (jnp.int32(0), device_offsets[slot_id, 0], device_offsets[slot_id, 1])
            current = lax.dynamic_slice(plane, start, (2, PATCH, PATCH))
            plane = lax.dynamic_update_slice(plane, current + patch_grad[slot_id], start)
        pieces = [plane[:, :TILE, :TILE], plane[:, :TILE, TILE:], plane[:, TILE:, :TILE], plane[:, TILE:, TILE:]]
        for k in range(4):
            gradient_tiles = gradient_tiles.at[ids[k]].add(pieces[k])
        return ((gradient_tiles, probe_total + probe_part), positions)
    initial = (jnp.zeros((N_SCAN, 2, TILE, TILE), jnp.float32), jnp.zeros((MODES, 2, PATCH, PATCH), jnp.float32))
    (object_grad, probe_grad), position_grad = lax.scan(per_device, initial, (jnp.arange(N_SCAN, dtype=jnp.int32), offsets, amplitudes, counts))
    return (object_grad, probe_grad, position_grad)
```

```python
import math

import jax
import jax.numpy as jnp
from jax import lax
from jax.sharding import PartitionSpec as P

GCOLS = 8
CORE = (1, 2)
ZLO = (2, 2)
YAX = (4, 4)
XAX = (16, 4)


amp_floor = 1.0


def from_behind(value, axis, steps):
    count = lax.axis_size(axis)
    pairs = [(source, (source + steps) % count) for source in range(count)]
    return lax.ppermute(value, axis, pairs)


def sub_shift(value, sub, shift):
    stride, size = sub
    count = lax.axis_size("scan")
    pairs = []
    for source in range(count):
        coord = (source // stride) % size
        pairs.append((source, source + (((coord + shift) % size) - coord) * stride))
    return lax.ppermute(value, "scan", pairs)


def sub_coord(sub):
    stride, size = sub
    return (lax.axis_index("scan") // stride) % size


def pair_reduce_scatter(data, sub):
    coord = sub_coord(sub)
    half = data.shape[0] // 2
    mine = lax.dynamic_slice_in_dim(data, coord * half, half, axis=0)
    other = lax.dynamic_slice_in_dim(data, (1 - coord) * half, half, axis=0)
    return mine + sub_shift(other, sub, 1)


def pair_all_gather(data, sub):
    coord = sub_coord(sub)
    got = sub_shift(data, sub, 1)
    first = jnp.where(coord == 0, data, got)
    second = jnp.where(coord == 0, got, data)
    return jnp.concatenate([first, second], axis=0)


def ring_reduce_scatter(data, sub):
    size = sub[1]
    coord = sub_coord(sub)
    rows = data.shape[0] // (2 * size)
    fwd = data[: rows * size].reshape(size, rows, -1)
    bwd = data[rows * size :].reshape(size, rows, -1)
    part_f = fwd[(coord - 1) % size]
    part_b = bwd[(coord + 1) % size]
    for step in range(size - 1):
        got_f = sub_shift(part_f, sub, 1)
        got_b = sub_shift(part_b, sub, -1)
        part_f = got_f + fwd[(coord - step - 2) % size]
        part_b = got_b + bwd[(coord + step + 2) % size]
    return jnp.concatenate([part_f, part_b], axis=0)


def ring_all_gather(data, sub):
    size = sub[1]
    coord = sub_coord(sub)
    rows = data.shape[0] // 2
    piece_f = data[:rows]
    piece_b = data[rows:]
    out_f = jnp.zeros((size, rows, data.shape[1]), data.dtype)
    out_b = jnp.zeros((size, rows, data.shape[1]), data.dtype)
    out_f = lax.dynamic_update_index_in_dim(out_f, piece_f, coord, 0)
    out_b = lax.dynamic_update_index_in_dim(out_b, piece_b, coord, 0)
    for step in range(size - 1):
        piece_f = sub_shift(piece_f, sub, 1)
        piece_b = sub_shift(piece_b, sub, -1)
        out_f = lax.dynamic_update_index_in_dim(out_f, piece_f, (coord - step - 1) % size, 0)
        out_b = lax.dynamic_update_index_in_dim(out_b, piece_b, (coord + step + 1) % size, 0)
    return jnp.concatenate([out_f.reshape(size * rows, -1), out_b.reshape(size * rows, -1)], axis=0)


def scan_all_reduce(value):
    shape = value.shape
    data = value.reshape(-1, shape[-1])
    data = pair_reduce_scatter(data, CORE)
    data = ring_reduce_scatter(data, XAX)
    data = ring_reduce_scatter(data, YAX)
    data = pair_reduce_scatter(data, ZLO)
    data = pair_all_gather(data, ZLO)
    data = ring_all_gather(data, YAX)
    data = ring_all_gather(data, XAX)
    data = pair_all_gather(data, CORE)
    return data.reshape(shape)


def dft_tables(length_side, direction_sign):
    index_row = jnp.arange(length_side, dtype=jnp.int32)
    product = index_row[:, None] * index_row[None, :] % length_side
    angles = product.astype(jnp.float32) * (2.0 * math.pi / length_side)
    scale_factor = 1.0 / math.sqrt(length_side)
    real_part = jnp.cos(angles) * scale_factor
    imag_part = direction_sign * jnp.sin(angles) * scale_factor
    matrix_table = jnp.stack(
        [jnp.stack([real_part, -imag_part]), jnp.stack([imag_part, real_part])]
    )
    return matrix_table.astype(jnp.bfloat16)


def transform(field, matrix_table):
    first_section = jnp.einsum(
        "dcpq,bcqk->bdpk", matrix_table, field, preferred_element_type=jnp.float32
    ).astype(jnp.bfloat16)
    return jnp.einsum(
        "bcpq,dcqk->bdpk", first_section, matrix_table, preferred_element_type=jnp.float32
    )


def shards(object_tiles, probe_modes, amplitudes, offsets, counts):
    side = probe_modes.shape[-1]
    tile_side = object_tiles.shape[-1]
    slots = offsets.shape[1]
    own_modes = probe_modes.shape[0]
    partner_modes = lax.ppermute(probe_modes, "mode", [(0, 1), (1, 0)])
    all_modes = jnp.concatenate([probe_modes, partner_modes], axis=0)
    modes_here = all_modes.shape[0]
    own_tile = object_tiles[0]
    east_tile = from_behind(own_tile, "scan", -1)
    south_tile = from_behind(own_tile, "scan", -GCOLS)
    corner_tile = from_behind(own_tile, "scan", -(GCOLS + 1))
    upper_band = jnp.concatenate([own_tile, east_tile], axis=2)
    lower_band = jnp.concatenate([south_tile, corner_tile], axis=2)
    extended = jnp.concatenate([upper_band, lower_band], axis=1)
    slot_offsets = offsets[0]
    windows = jnp.stack(
        [
            lax.dynamic_slice(
                extended,
                (0, slot_offsets[slot_id, 0] - 1, slot_offsets[slot_id, 1] - 1),
                (2, side + 2, side + 2),
            )
            for slot_id in range(slots)
        ]
    )
    patch = windows[:, :, 1:-1, 1:-1]
    grad_y = (windows[:, :, 2:, 1:-1] - windows[:, :, :-2, 1:-1]) * 0.5
    grad_x = (windows[:, :, 1:-1, 2:] - windows[:, :, 1:-1, :-2]) * 0.5
    obj_real = patch[:, 0][:, None]
    obj_imag = patch[:, 1][:, None]
    probe_real = all_modes[:, 0][None]
    probe_imag = all_modes[:, 1][None]
    exit_real = obj_real * probe_real - obj_imag * probe_imag
    exit_imag = obj_real * probe_imag + obj_imag * probe_real
    exit_wave = jnp.stack([exit_real, exit_imag], axis=2).astype(jnp.bfloat16)
    forward_table = dft_tables(side, -1.0)
    inverse_table = dft_tables(side, 1.0)
    far_field = transform(exit_wave.reshape(slots * modes_here, 2, side, side), forward_table)
    far_field = far_field.reshape(slots, modes_here, 2, side, side)
    intensity = jnp.sum(far_field * far_field, axis=(1, 2))
    ratio = amplitudes[0] / jnp.maximum(jnp.sqrt(intensity), amp_floor)
    correction = (far_field * (ratio - 1.0)[:, None, None]).astype(jnp.bfloat16)
    live_slots = (jnp.arange(slots, dtype=jnp.int32) < counts[0]).astype(jnp.float32)
    back_own = transform(
        correction[:, :own_modes].reshape(slots * own_modes, 2, side, side), inverse_table
    ).reshape(slots, own_modes, 2, side, side)
    back_own = back_own * live_slots[:, None, None, None, None]
    probe_real_grad = jnp.sum(obj_real * back_own[:, :, 0] + obj_imag * back_own[:, :, 1], axis=0)
    probe_imag_grad = jnp.sum(obj_real * back_own[:, :, 1] - obj_imag * back_own[:, :, 0], axis=0)
    probe_grad = scan_all_reduce(jnp.stack([probe_real_grad, probe_imag_grad], axis=1))
    back_other = transform(
        correction[:, own_modes:].reshape(slots * (modes_here - own_modes), 2, side, side),
        inverse_table,
    ).reshape(slots, modes_here - own_modes, 2, side, side)
    back_other = back_other * live_slots[:, None, None, None, None]
    back_wave = jnp.concatenate([back_own, back_other], axis=1)
    back_real = back_wave[:, :, 0]
    back_imag = back_wave[:, :, 1]
    grad_real = jnp.sum(probe_real * back_real + probe_imag * back_imag, axis=1)
    grad_imag = jnp.sum(probe_real * back_imag - probe_imag * back_real, axis=1)
    whole_grad = jnp.stack([grad_real, grad_imag], axis=1)
    component = lax.axis_index("mode")
    position_y = jnp.sum(whole_grad * grad_y, axis=(1, 2, 3))
    position_x = jnp.sum(whole_grad * grad_x, axis=(1, 2, 3))
    positions = jnp.stack([position_y, position_x], axis=1) / side
    mine = lax.dynamic_slice_in_dim(whole_grad, component, 1, axis=1)
    gradient_plane = jnp.zeros((2 * tile_side, 2 * tile_side), jnp.float32)
    for slot_id in range(slots):
        start = (slot_offsets[slot_id, 0], slot_offsets[slot_id, 1])
        current = lax.dynamic_slice(gradient_plane, start, (side, side))
        gradient_plane = lax.dynamic_update_slice(gradient_plane, current + mine[slot_id, 0], start)
    received_east = from_behind(gradient_plane[:tile_side, tile_side:], "scan", 1)
    received_south = from_behind(gradient_plane[tile_side:, :tile_side], "scan", GCOLS)
    received_corner = from_behind(gradient_plane[tile_side:, tile_side:], "scan", GCOLS + 1)
    total_grad = (
        gradient_plane[:tile_side, :tile_side] + received_east + received_south + received_corner
    )
    return (total_grad[None, None], probe_grad, positions[None])


def solution(mesh):
    return jax.shard_map(
        shards,
        mesh=mesh,
        in_specs=(
            P("scan", None, None, None),
            P("mode", None, None, None),
            P("scan", None, None, None),
            P("scan", None, None),
            P("scan"),
        ),
        out_specs=(
            P("scan", "mode", None, None),
            P("mode", None, None, None),
            P("scan", None, None),
        ),
        check_vma=False,
    )
```

```python
import math

import jax
import jax.numpy as jnp
from jax import lax
from jax.sharding import PartitionSpec as P

GCOLS = 8
CORE = (1, 2)
ZLO = (2, 2)
YAX = (4, 4)
XAX = (16, 4)


amp_floor = 1.0


def from_behind(value, axis, steps):
    count = lax.axis_size(axis)
    pairs = [(source, (source + steps) % count) for source in range(count)]
    return lax.ppermute(value, axis, pairs)


def sub_shift(value, sub, shift):
    stride, size = sub
    count = lax.axis_size("scan")
    pairs = []
    for source in range(count):
        coord = (source // stride) % size
        pairs.append((source, source + (((coord + shift) % size) - coord) * stride))
    return lax.ppermute(value, "scan", pairs)


def sub_coord(sub):
    stride, size = sub
    return (lax.axis_index("scan") // stride) % size


def pair_reduce_scatter(data, sub):
    coord = sub_coord(sub)
    half = data.shape[0] // 2
    mine = lax.dynamic_slice_in_dim(data, coord * half, half, axis=0)
    other = lax.dynamic_slice_in_dim(data, (1 - coord) * half, half, axis=0)
    return mine + sub_shift(other, sub, 1)


def pair_all_gather(data, sub):
    coord = sub_coord(sub)
    got = sub_shift(data, sub, 1)
    first = jnp.where(coord == 0, data, got)
    second = jnp.where(coord == 0, got, data)
    return jnp.concatenate([first, second], axis=0)


def direct_reduce_scatter(data, sub):
    size = sub[1]
    coord = sub_coord(sub)
    chunks = data.reshape(size, data.shape[0] // size, -1)
    total = chunks[coord]
    for shift in range(1, size):
        total = total + sub_shift(chunks[(coord + shift) % size], sub, shift)
    return total


def direct_all_gather(data, sub):
    size = sub[1]
    coord = sub_coord(sub)
    out = jnp.zeros((size,) + data.shape, data.dtype)
    out = lax.dynamic_update_index_in_dim(out, data, coord, 0)
    for shift in range(1, size):
        got = sub_shift(data, sub, shift)
        out = lax.dynamic_update_index_in_dim(out, got, (coord - shift) % size, 0)
    return out.reshape(size * data.shape[0], -1)


def ring_reduce_scatter(data, sub):
    size = sub[1]
    coord = sub_coord(sub)
    rows = data.shape[0] // (2 * size)
    fwd = data[: rows * size].reshape(size, rows, -1)
    bwd = data[rows * size :].reshape(size, rows, -1)
    part_f = fwd[(coord - 1) % size]
    part_b = bwd[(coord + 1) % size]
    for step in range(size - 1):
        got_f = sub_shift(part_f, sub, 1)
        got_b = sub_shift(part_b, sub, -1)
        part_f = got_f + fwd[(coord - step - 2) % size]
        part_b = got_b + bwd[(coord + step + 2) % size]
    return jnp.concatenate([part_f, part_b], axis=0)


def ring_all_gather(data, sub):
    size = sub[1]
    coord = sub_coord(sub)
    rows = data.shape[0] // 2
    piece_f = data[:rows]
    piece_b = data[rows:]
    out_f = jnp.zeros((size, rows, data.shape[1]), data.dtype)
    out_b = jnp.zeros((size, rows, data.shape[1]), data.dtype)
    out_f = lax.dynamic_update_index_in_dim(out_f, piece_f, coord, 0)
    out_b = lax.dynamic_update_index_in_dim(out_b, piece_b, coord, 0)
    for step in range(size - 1):
        piece_f = sub_shift(piece_f, sub, 1)
        piece_b = sub_shift(piece_b, sub, -1)
        out_f = lax.dynamic_update_index_in_dim(out_f, piece_f, (coord - step - 1) % size, 0)
        out_b = lax.dynamic_update_index_in_dim(out_b, piece_b, (coord + step + 1) % size, 0)
    return jnp.concatenate([out_f.reshape(size * rows, -1), out_b.reshape(size * rows, -1)], axis=0)


def scan_all_reduce(value, tied):
    shape = value.shape
    data = value.reshape(-1, shape[-1])
    data = pair_reduce_scatter(data, CORE)
    data = direct_reduce_scatter(data, XAX)
    data = direct_reduce_scatter(data, YAX)
    data = pair_reduce_scatter(data, ZLO)
    data, tied = lax.optimization_barrier((data, tied))
    data = pair_all_gather(data, ZLO)
    data = direct_all_gather(data, YAX)
    data = direct_all_gather(data, XAX)
    data = pair_all_gather(data, CORE)
    return data.reshape(shape), tied


def dft_tables(length_side, direction_sign):
    index_row = jnp.arange(length_side, dtype=jnp.int32)
    product = index_row[:, None] * index_row[None, :] % length_side
    angles = product.astype(jnp.float32) * (2.0 * math.pi / length_side)
    scale_factor = 1.0 / math.sqrt(length_side)
    real_part = jnp.cos(angles) * scale_factor
    imag_part = direction_sign * jnp.sin(angles) * scale_factor
    matrix_table = jnp.stack(
        [jnp.stack([real_part, -imag_part]), jnp.stack([imag_part, real_part])]
    )
    return matrix_table.astype(jnp.bfloat16)


def transform(field, matrix_table):
    first_section = jnp.einsum(
        "dcpq,bcqk->bdpk", matrix_table, field, preferred_element_type=jnp.float32
    ).astype(jnp.bfloat16)
    return jnp.einsum(
        "bcpq,dcqk->bdpk", first_section, matrix_table, preferred_element_type=jnp.float32
    )


def shards(object_tiles, probe_modes, amplitudes, offsets, counts):
    side = probe_modes.shape[-1]
    tile_side = object_tiles.shape[-1]
    slots = offsets.shape[1]
    own_modes = probe_modes.shape[0]
    count = lax.axis_size("scan")
    core = lax.axis_index("scan") % 2
    sent = lax.dynamic_index_in_dim(probe_modes, core, 0, keepdims=False)
    pairs = [(s * 2 + m, (s ^ 2) * 2 + 1 - m) for s in range(count) for m in range(2)]
    got = lax.ppermute(sent, ("scan", "mode"), pairs)
    mate = lax.ppermute(got, "scan", [(s, s ^ 1) for s in range(count)])
    partner_modes = jnp.stack([jnp.where(core == 0, got, mate), jnp.where(core == 0, mate, got)])
    component = lax.axis_index("mode")
    all_modes = jnp.where(
        component == 0,
        jnp.concatenate([probe_modes, partner_modes], axis=0),
        jnp.concatenate([partner_modes, probe_modes], axis=0),
    )
    modes_here = all_modes.shape[0]
    own_tile = object_tiles[0]
    east_tile = from_behind(own_tile, "scan", -1)
    south_tile = from_behind(own_tile, "scan", -GCOLS)
    far_corner = lax.ppermute(
        own_tile, "scan", [(s, s - GCOLS - 1) for s in range(count) if (s - GCOLS - 1) % 2 == 1 and s >= GCOLS + 1]
        + [(s, s - GCOLS - 1 + count) for s in range(count) if (s - GCOLS - 1) % 2 == 1 and s < GCOLS + 1]
    )
    near_corner = lax.ppermute(south_tile, "scan", [(s, s - 1) for s in range(count) if s % 2 == 1])
    corner_tile = jnp.where(lax.axis_index("scan") % 2 == 0, near_corner, far_corner)
    upper_band = jnp.concatenate([own_tile, east_tile], axis=2)
    lower_band = jnp.concatenate([south_tile, corner_tile], axis=2)
    extended = jnp.concatenate([upper_band, lower_band], axis=1)
    slot_offsets = offsets[0]
    windows = jnp.stack(
        [
            lax.dynamic_slice(
                extended,
                (0, slot_offsets[slot_id, 0] - 1, slot_offsets[slot_id, 1] - 1),
                (2, side + 2, side + 2),
            )
            for slot_id in range(slots)
        ]
    )
    patch = windows[:, :, 1:-1, 1:-1]
    grad_y = (windows[:, :, 2:, 1:-1] - windows[:, :, :-2, 1:-1]) * 0.5
    grad_x = (windows[:, :, 1:-1, 2:] - windows[:, :, 1:-1, :-2]) * 0.5
    obj_real = patch[:, 0][:, None]
    obj_imag = patch[:, 1][:, None]
    probe_real = all_modes[:, 0][None]
    probe_imag = all_modes[:, 1][None]
    exit_real = obj_real * probe_real - obj_imag * probe_imag
    exit_imag = obj_real * probe_imag + obj_imag * probe_real
    exit_wave = jnp.stack([exit_real, exit_imag], axis=2).astype(jnp.bfloat16)
    forward_table = dft_tables(side, -1.0)
    inverse_table = dft_tables(side, 1.0)
    far_field = transform(exit_wave.reshape(slots * modes_here, 2, side, side), forward_table)
    far_field = far_field.reshape(slots, modes_here, 2, side, side)
    intensity = jnp.sum(far_field * far_field, axis=(1, 2))
    ratio = amplitudes[0] / jnp.maximum(jnp.sqrt(intensity), amp_floor)
    correction = (far_field * (ratio - 1.0)[:, None, None]).astype(jnp.bfloat16)
    live_slots = (jnp.arange(slots, dtype=jnp.int32) < counts[0]).astype(jnp.float32)
    back_wave = transform(
        correction.reshape(slots * modes_here, 2, side, side), inverse_table
    ).reshape(slots, modes_here, 2, side, side)
    back_wave = back_wave * live_slots[:, None, None, None, None]
    back_own = lax.dynamic_slice_in_dim(back_wave, component * own_modes, own_modes, axis=1)
    probe_real_grad = jnp.sum(obj_real * back_own[:, :, 0] + obj_imag * back_own[:, :, 1], axis=0)
    probe_imag_grad = jnp.sum(obj_real * back_own[:, :, 1] - obj_imag * back_own[:, :, 0], axis=0)
    probe_partial = jnp.stack([probe_real_grad, probe_imag_grad], axis=1)
    back_real = back_wave[:, :, 0]
    back_imag = back_wave[:, :, 1]
    grad_real = jnp.sum(probe_real * back_real + probe_imag * back_imag, axis=1)
    grad_imag = jnp.sum(probe_real * back_imag - probe_imag * back_real, axis=1)
    whole_grad = jnp.stack([grad_real, grad_imag], axis=1)
    position_y = jnp.sum(whole_grad * grad_y, axis=(1, 2, 3))
    position_x = jnp.sum(whole_grad * grad_x, axis=(1, 2, 3))
    positions = jnp.stack([position_y, position_x], axis=1) / side
    mine = lax.dynamic_slice_in_dim(whole_grad, component, 1, axis=1)
    gradient_plane = jnp.zeros((2 * tile_side, 2 * tile_side), jnp.float32)
    for slot_id in range(slots):
        start = (slot_offsets[slot_id, 0], slot_offsets[slot_id, 1])
        current = lax.dynamic_slice(gradient_plane, start, (side, side))
        gradient_plane = lax.dynamic_update_slice(gradient_plane, current + mine[slot_id, 0], start)
    probe_partial, gradient_plane = lax.optimization_barrier((probe_partial, gradient_plane))
    received_east = from_behind(gradient_plane[:tile_side, tile_side:], "scan", 1)
    received_south = from_behind(gradient_plane[tile_side:, :tile_side], "scan", GCOLS)
    received_corner = from_behind(gradient_plane[tile_side:, tile_side:], "scan", GCOLS + 1)
    probe_grad, (received_east, received_south, received_corner) = scan_all_reduce(
        probe_partial, (received_east, received_south, received_corner)
    )
    total_grad = (
        gradient_plane[:tile_side, :tile_side] + received_east + received_south + received_corner
    )
    return (total_grad[None, None], probe_grad, positions[None])


def solution(mesh):
    return jax.shard_map(
        shards,
        mesh=mesh,
        in_specs=(
            P("scan", None, None, None),
            P("mode", None, None, None),
            P("scan", None, None, None),
            P("scan", None, None),
            P("scan"),
        ),
        out_specs=(
            P("scan", "mode", None, None),
            P("mode", None, None, None),
            P("scan", None, None),
        ),
        check_vma=False,
    )
```

```python
import math

import jax
import jax.numpy as jnp
from jax import lax
from jax.experimental import pallas as pl
from jax.experimental.pallas import tpu as pltpu
from jax.sharding import PartitionSpec as P

GCOLS = 8
CORE = (1, 2)
ZLO = (2, 2)
YAX = (4, 4)
XAX = (16, 4)


amp_floor = 1.0


def from_behind(value, axis, steps):
    count = lax.axis_size(axis)
    pairs = [(source, (source + steps) % count) for source in range(count)]
    return lax.ppermute(value, axis, pairs)


def sub_shift(value, sub, shift):
    stride, size = sub
    count = lax.axis_size("scan")
    pairs = []
    for source in range(count):
        coord = (source // stride) % size
        pairs.append((source, source + (((coord + shift) % size) - coord) * stride))
    return lax.ppermute(value, "scan", pairs)


def sub_coord(sub):
    stride, size = sub
    return (lax.axis_index("scan") // stride) % size


def pair_reduce_scatter(data, sub):
    coord = sub_coord(sub)
    half = data.shape[0] // 2
    mine = lax.dynamic_slice_in_dim(data, coord * half, half, axis=0)
    other = lax.dynamic_slice_in_dim(data, (1 - coord) * half, half, axis=0)
    return mine + sub_shift(other, sub, 1)


def pair_all_gather(data, sub):
    coord = sub_coord(sub)
    got = sub_shift(data, sub, 1)
    first = jnp.where(coord == 0, data, got)
    second = jnp.where(coord == 0, got, data)
    return jnp.concatenate([first, second], axis=0)


def direct_reduce_scatter(data, sub):
    size = sub[1]
    coord = sub_coord(sub)
    chunks = data.reshape(size, data.shape[0] // size, -1)
    total = chunks[coord]
    for shift in range(1, size):
        total = total + sub_shift(chunks[(coord + shift) % size], sub, shift)
    return total


def direct_all_gather(data, sub):
    size = sub[1]
    coord = sub_coord(sub)
    out = jnp.zeros((size,) + data.shape, data.dtype)
    out = lax.dynamic_update_index_in_dim(out, data, coord, 0)
    for shift in range(1, size):
        got = sub_shift(data, sub, shift)
        out = lax.dynamic_update_index_in_dim(out, got, (coord - shift) % size, 0)
    return out.reshape(size * data.shape[0], -1)


def ring_reduce_scatter(data, sub):
    size = sub[1]
    coord = sub_coord(sub)
    rows = data.shape[0] // (2 * size)
    fwd = data[: rows * size].reshape(size, rows, -1)
    bwd = data[rows * size :].reshape(size, rows, -1)
    part_f = fwd[(coord - 1) % size]
    part_b = bwd[(coord + 1) % size]
    for step in range(size - 1):
        got_f = sub_shift(part_f, sub, 1)
        got_b = sub_shift(part_b, sub, -1)
        part_f = got_f + fwd[(coord - step - 2) % size]
        part_b = got_b + bwd[(coord + step + 2) % size]
    return jnp.concatenate([part_f, part_b], axis=0)


def ring_all_gather(data, sub):
    size = sub[1]
    coord = sub_coord(sub)
    rows = data.shape[0] // 2
    piece_f = data[:rows]
    piece_b = data[rows:]
    out_f = jnp.zeros((size, rows, data.shape[1]), data.dtype)
    out_b = jnp.zeros((size, rows, data.shape[1]), data.dtype)
    out_f = lax.dynamic_update_index_in_dim(out_f, piece_f, coord, 0)
    out_b = lax.dynamic_update_index_in_dim(out_b, piece_b, coord, 0)
    for step in range(size - 1):
        piece_f = sub_shift(piece_f, sub, 1)
        piece_b = sub_shift(piece_b, sub, -1)
        out_f = lax.dynamic_update_index_in_dim(out_f, piece_f, (coord - step - 1) % size, 0)
        out_b = lax.dynamic_update_index_in_dim(out_b, piece_b, (coord + step + 1) % size, 0)
    return jnp.concatenate([out_f.reshape(size * rows, -1), out_b.reshape(size * rows, -1)], axis=0)


def scan_all_reduce(value, tied):
    shape = value.shape
    data = value.reshape(-1, shape[-1])
    data = pair_reduce_scatter(data, CORE)
    data = direct_reduce_scatter(data, XAX)
    data = direct_reduce_scatter(data, YAX)
    data = pair_reduce_scatter(data, ZLO)
    data, tied = lax.optimization_barrier((data, tied))
    data = pair_all_gather(data, ZLO)
    data = direct_all_gather(data, YAX)
    data = direct_all_gather(data, XAX)
    data = pair_all_gather(data, CORE)
    return data.reshape(shape), tied


def dft_tables(length_side, direction_sign):
    index_row = jnp.arange(length_side, dtype=jnp.int32)
    product = index_row[:, None] * index_row[None, :] % length_side
    angles = product.astype(jnp.float32) * (2.0 * math.pi / length_side)
    scale_factor = 1.0 / math.sqrt(length_side)
    real_part = jnp.cos(angles) * scale_factor
    imag_part = direction_sign * jnp.sin(angles) * scale_factor
    matrix_table = jnp.stack(
        [jnp.stack([real_part, -imag_part]), jnp.stack([imag_part, real_part])]
    )
    return matrix_table.astype(jnp.bfloat16)


def transform(field, matrix_table):
    first_section = jnp.einsum(
        "dcpq,bcqk->bdpk", matrix_table, field, preferred_element_type=jnp.float32
    ).astype(jnp.bfloat16)
    return jnp.einsum(
        "bcpq,dcqk->bdpk", first_section, matrix_table, preferred_element_type=jnp.float32
    )


def complex_table(matrix_table, transposed):
    if transposed:
        rows = [jnp.concatenate([matrix_table[0, c], matrix_table[1, c]], axis=1) for c in range(2)]
    else:
        rows = [jnp.concatenate([matrix_table[d, 0], matrix_table[d, 1]], axis=1) for d in range(2)]
    return jnp.concatenate(rows, axis=0)


def forward_kernel(patch_ref, probe_ref, amp_ref, left_ref, right_ref, out_ref, far_ref):
    side = patch_ref.shape[-1]
    modes = probe_ref.shape[0]
    obj_real = patch_ref[0, 0]
    obj_imag = patch_ref[0, 1]

    def one_mode(mode, intensity):
        probe_real = probe_ref[mode, 0]
        probe_imag = probe_ref[mode, 1]
        exit_real = (obj_real * probe_real - obj_imag * probe_imag).astype(jnp.bfloat16)
        exit_imag = (obj_real * probe_imag + obj_imag * probe_real).astype(jnp.bfloat16)
        stacked = jnp.concatenate([exit_real, exit_imag], axis=0)
        half = jnp.dot(left_ref[...], stacked, preferred_element_type=jnp.float32).astype(jnp.bfloat16)
        wide = jnp.concatenate([half[:side], half[side:]], axis=1)
        far = jnp.dot(wide, right_ref[...], preferred_element_type=jnp.float32)
        far_ref[mode] = far
        return intensity + far[:, :side] * far[:, :side] + far[:, side:] * far[:, side:]

    intensity = lax.fori_loop(0, modes, one_mode, jnp.zeros((side, side), jnp.float32))
    ratio = amp_ref[0] / jnp.maximum(jnp.sqrt(intensity), amp_floor) - 1.0

    def store(mode, carry):
        far = far_ref[mode]
        out_ref[0, mode, 0] = (far[:, :side] * ratio).astype(jnp.bfloat16)
        out_ref[0, mode, 1] = (far[:, side:] * ratio).astype(jnp.bfloat16)
        return carry

    lax.fori_loop(0, modes, store, 0)


def forward_correction(patch, all_modes, amplitudes, forward_table):
    slots, _, side, _ = patch.shape
    modes = all_modes.shape[0]
    left = complex_table(forward_table, False)
    right = complex_table(forward_table, True)
    return pl.pallas_call(
        forward_kernel,
        grid=(slots,),
        in_specs=[
            pl.BlockSpec((1, 2, side, side), lambda s: (s, 0, 0, 0)),
            pl.BlockSpec((modes, 2, side, side), lambda s: (0, 0, 0, 0), pipeline_mode=pl.Buffered(1)),
            pl.BlockSpec((1, side, side), lambda s: (s, 0, 0)),
            pl.BlockSpec((2 * side, 2 * side), lambda s: (0, 0), pipeline_mode=pl.Buffered(1)),
            pl.BlockSpec((2 * side, 2 * side), lambda s: (0, 0), pipeline_mode=pl.Buffered(1)),
        ],
        out_specs=pl.BlockSpec((1, modes, 2, side, side), lambda s: (s, 0, 0, 0, 0)),
        out_shape=jax.ShapeDtypeStruct((slots, modes, 2, side, side), jnp.bfloat16),
        scratch_shapes=[pltpu.VMEM((modes, side, 2 * side), jnp.float32)],
        compiler_params=pltpu.CompilerParams(vmem_limit_bytes=64 * 1024 * 1024),
        cost_estimate=pl.CostEstimate(
            flops=slots * modes * 4 * (2 * side) ** 2 * side,
            bytes_accessed=slots * (modes + 3) * 2 * side * side * 4,
            transcendentals=slots * side * side,
        ),
    )(patch, all_modes, amplitudes, left, right)


def shards(object_tiles, probe_modes, amplitudes, offsets, counts):
    side = probe_modes.shape[-1]
    tile_side = object_tiles.shape[-1]
    slots = offsets.shape[1]
    own_modes = probe_modes.shape[0]
    count = lax.axis_size("scan")
    core = lax.axis_index("scan") % 2
    sent = lax.dynamic_index_in_dim(probe_modes, core, 0, keepdims=False)
    pairs = [(s * 2 + m, (s ^ 2) * 2 + 1 - m) for s in range(count) for m in range(2)]
    got = lax.ppermute(sent, ("scan", "mode"), pairs)
    mate = lax.ppermute(got, "scan", [(s, s ^ 1) for s in range(count)])
    partner_modes = jnp.stack([jnp.where(core == 0, got, mate), jnp.where(core == 0, mate, got)])
    component = lax.axis_index("mode")
    all_modes = jnp.where(
        component == 0,
        jnp.concatenate([probe_modes, partner_modes], axis=0),
        jnp.concatenate([partner_modes, probe_modes], axis=0),
    )
    modes_here = all_modes.shape[0]
    own_tile = object_tiles[0]
    east_tile = from_behind(own_tile, "scan", -1)
    south_tile = from_behind(own_tile, "scan", -GCOLS)
    far_corner = lax.ppermute(
        own_tile, "scan", [(s, s - GCOLS - 1) for s in range(count) if (s - GCOLS - 1) % 2 == 1 and s >= GCOLS + 1]
        + [(s, s - GCOLS - 1 + count) for s in range(count) if (s - GCOLS - 1) % 2 == 1 and s < GCOLS + 1]
    )
    near_corner = lax.ppermute(south_tile, "scan", [(s, s - 1) for s in range(count) if s % 2 == 1])
    corner_tile = jnp.where(lax.axis_index("scan") % 2 == 0, near_corner, far_corner)
    upper_band = jnp.concatenate([own_tile, east_tile], axis=2)
    lower_band = jnp.concatenate([south_tile, corner_tile], axis=2)
    extended = jnp.concatenate([upper_band, lower_band], axis=1)
    slot_offsets = offsets[0]
    windows = jnp.stack(
        [
            lax.dynamic_slice(
                extended,
                (0, slot_offsets[slot_id, 0] - 1, slot_offsets[slot_id, 1] - 1),
                (2, side + 2, side + 2),
            )
            for slot_id in range(slots)
        ]
    )
    patch = windows[:, :, 1:-1, 1:-1]
    grad_y = (windows[:, :, 2:, 1:-1] - windows[:, :, :-2, 1:-1]) * 0.5
    grad_x = (windows[:, :, 1:-1, 2:] - windows[:, :, 1:-1, :-2]) * 0.5
    obj_real = patch[:, 0][:, None]
    obj_imag = patch[:, 1][:, None]
    probe_real = all_modes[:, 0][None]
    probe_imag = all_modes[:, 1][None]
    forward_table = dft_tables(side, -1.0)
    inverse_table = dft_tables(side, 1.0)
    correction = forward_correction(patch, all_modes, amplitudes[0], forward_table)
    live_slots = (jnp.arange(slots, dtype=jnp.int32) < counts[0]).astype(jnp.float32)
    back_wave = transform(
        correction.reshape(slots * modes_here, 2, side, side), inverse_table
    ).reshape(slots, modes_here, 2, side, side)
    back_wave = back_wave * live_slots[:, None, None, None, None]
    back_own = lax.dynamic_slice_in_dim(back_wave, component * own_modes, own_modes, axis=1)
    probe_real_grad = jnp.sum(obj_real * back_own[:, :, 0] + obj_imag * back_own[:, :, 1], axis=0)
    probe_imag_grad = jnp.sum(obj_real * back_own[:, :, 1] - obj_imag * back_own[:, :, 0], axis=0)
    probe_partial = jnp.stack([probe_real_grad, probe_imag_grad], axis=1)
    back_real = back_wave[:, :, 0]
    back_imag = back_wave[:, :, 1]
    grad_real = jnp.sum(probe_real * back_real + probe_imag * back_imag, axis=1)
    grad_imag = jnp.sum(probe_real * back_imag - probe_imag * back_real, axis=1)
    whole_grad = jnp.stack([grad_real, grad_imag], axis=1)
    position_y = jnp.sum(whole_grad * grad_y, axis=(1, 2, 3))
    position_x = jnp.sum(whole_grad * grad_x, axis=(1, 2, 3))
    positions = jnp.stack([position_y, position_x], axis=1) / side
    mine = lax.dynamic_slice_in_dim(whole_grad, component, 1, axis=1)
    gradient_plane = jnp.zeros((2 * tile_side, 2 * tile_side), jnp.float32)
    for slot_id in range(slots):
        start = (slot_offsets[slot_id, 0], slot_offsets[slot_id, 1])
        current = lax.dynamic_slice(gradient_plane, start, (side, side))
        gradient_plane = lax.dynamic_update_slice(gradient_plane, current + mine[slot_id, 0], start)
    probe_partial, gradient_plane = lax.optimization_barrier((probe_partial, gradient_plane))
    received_east = from_behind(gradient_plane[:tile_side, tile_side:], "scan", 1)
    received_south = from_behind(gradient_plane[tile_side:, :tile_side], "scan", GCOLS)
    received_corner = from_behind(gradient_plane[tile_side:, tile_side:], "scan", GCOLS + 1)
    probe_grad, (received_east, received_south, received_corner) = scan_all_reduce(
        probe_partial, (received_east, received_south, received_corner)
    )
    total_grad = (
        gradient_plane[:tile_side, :tile_side] + received_east + received_south + received_corner
    )
    return (total_grad[None, None], probe_grad, positions[None])


def solution(mesh):
    return jax.shard_map(
        shards,
        mesh=mesh,
        in_specs=(
            P("scan", None, None, None),
            P("mode", None, None, None),
            P("scan", None, None, None),
            P("scan", None, None),
            P("scan"),
        ),
        out_specs=(
            P("scan", "mode", None, None),
            P("mode", None, None, None),
            P("scan", None, None),
        ),
        check_vma=False,
    )
```

```python
import math

import jax
import jax.numpy as jnp
from jax import lax
from jax.experimental import pallas as pl
from jax.experimental.pallas import tpu as pltpu
from jax.sharding import PartitionSpec as P

GCOLS = 8
CORE = (1, 2)
ZLO = (2, 2)
YAX = (4, 4)
XAX = (16, 4)


amp_floor = 1.0


def from_behind(value, axis, steps):
    count = lax.axis_size(axis)
    pairs = [(source, (source + steps) % count) for source in range(count)]
    return lax.ppermute(value, axis, pairs)


def sub_shift(value, sub, shift):
    stride, size = sub
    count = lax.axis_size("scan")
    pairs = []
    for source in range(count):
        coord = (source // stride) % size
        pairs.append((source, source + (((coord + shift) % size) - coord) * stride))
    return lax.ppermute(value, "scan", pairs)


def sub_coord(sub):
    stride, size = sub
    return (lax.axis_index("scan") // stride) % size


def pair_reduce_scatter(data, sub):
    coord = sub_coord(sub)
    half = data.shape[0] // 2
    mine = lax.dynamic_slice_in_dim(data, coord * half, half, axis=0)
    other = lax.dynamic_slice_in_dim(data, (1 - coord) * half, half, axis=0)
    return mine + sub_shift(other, sub, 1)


def pair_all_gather(data, sub):
    coord = sub_coord(sub)
    got = sub_shift(data, sub, 1)
    first = jnp.where(coord == 0, data, got)
    second = jnp.where(coord == 0, got, data)
    return jnp.concatenate([first, second], axis=0)


def direct_reduce_scatter(data, sub):
    size = sub[1]
    coord = sub_coord(sub)
    chunks = data.reshape(size, data.shape[0] // size, -1)
    total = chunks[coord]
    for shift in range(1, size):
        total = total + sub_shift(chunks[(coord + shift) % size], sub, shift)
    return total


def direct_all_gather(data, sub):
    size = sub[1]
    coord = sub_coord(sub)
    out = jnp.zeros((size,) + data.shape, data.dtype)
    out = lax.dynamic_update_index_in_dim(out, data, coord, 0)
    for shift in range(1, size):
        got = sub_shift(data, sub, shift)
        out = lax.dynamic_update_index_in_dim(out, got, (coord - shift) % size, 0)
    return out.reshape(size * data.shape[0], -1)


def ring_reduce_scatter(data, sub):
    size = sub[1]
    coord = sub_coord(sub)
    rows = data.shape[0] // (2 * size)
    fwd = data[: rows * size].reshape(size, rows, -1)
    bwd = data[rows * size :].reshape(size, rows, -1)
    part_f = fwd[(coord - 1) % size]
    part_b = bwd[(coord + 1) % size]
    for step in range(size - 1):
        got_f = sub_shift(part_f, sub, 1)
        got_b = sub_shift(part_b, sub, -1)
        part_f = got_f + fwd[(coord - step - 2) % size]
        part_b = got_b + bwd[(coord + step + 2) % size]
    return jnp.concatenate([part_f, part_b], axis=0)


def ring_all_gather(data, sub):
    size = sub[1]
    coord = sub_coord(sub)
    rows = data.shape[0] // 2
    piece_f = data[:rows]
    piece_b = data[rows:]
    out_f = jnp.zeros((size, rows, data.shape[1]), data.dtype)
    out_b = jnp.zeros((size, rows, data.shape[1]), data.dtype)
    out_f = lax.dynamic_update_index_in_dim(out_f, piece_f, coord, 0)
    out_b = lax.dynamic_update_index_in_dim(out_b, piece_b, coord, 0)
    for step in range(size - 1):
        piece_f = sub_shift(piece_f, sub, 1)
        piece_b = sub_shift(piece_b, sub, -1)
        out_f = lax.dynamic_update_index_in_dim(out_f, piece_f, (coord - step - 1) % size, 0)
        out_b = lax.dynamic_update_index_in_dim(out_b, piece_b, (coord + step + 1) % size, 0)
    return jnp.concatenate([out_f.reshape(size * rows, -1), out_b.reshape(size * rows, -1)], axis=0)


def scan_all_reduce(value, tied):
    shape = value.shape
    data = value.reshape(-1, shape[-1])
    data = pair_reduce_scatter(data, CORE)
    data = direct_reduce_scatter(data, XAX)
    data = direct_reduce_scatter(data, YAX)
    data = pair_reduce_scatter(data, ZLO)
    data, tied = lax.optimization_barrier((data, tied))
    data = pair_all_gather(data, ZLO)
    data = direct_all_gather(data, YAX)
    data = direct_all_gather(data, XAX)
    data = pair_all_gather(data, CORE)
    return data.reshape(shape), tied


def dft_tables(length_side, direction_sign):
    index_row = jnp.arange(length_side, dtype=jnp.int32)
    product = index_row[:, None] * index_row[None, :] % length_side
    angles = product.astype(jnp.float32) * (2.0 * math.pi / length_side)
    scale_factor = 1.0 / math.sqrt(length_side)
    real_part = jnp.cos(angles) * scale_factor
    imag_part = direction_sign * jnp.sin(angles) * scale_factor
    matrix_table = jnp.stack(
        [jnp.stack([real_part, -imag_part]), jnp.stack([imag_part, real_part])]
    )
    return matrix_table.astype(jnp.bfloat16)


def transform(field, matrix_table):
    first_section = jnp.einsum(
        "dcpq,bcqk->bdpk", matrix_table, field, preferred_element_type=jnp.float32
    ).astype(jnp.bfloat16)
    return jnp.einsum(
        "bcpq,dcqk->bdpk", first_section, matrix_table, preferred_element_type=jnp.float32
    )


def complex_table(matrix_table, transposed):
    if transposed:
        rows = [jnp.concatenate([matrix_table[0, c], matrix_table[1, c]], axis=1) for c in range(2)]
    else:
        rows = [jnp.concatenate([matrix_table[d, 0], matrix_table[d, 1]], axis=1) for d in range(2)]
    return jnp.concatenate(rows, axis=0)


def forward_kernel(patch_ref, probe_ref, amp_ref, left_ref, right_ref, out_ref, far_ref):
    side = patch_ref.shape[-1]
    modes = probe_ref.shape[0]
    obj_real = patch_ref[0, 0]
    obj_imag = patch_ref[0, 1]

    def one_mode(mode, intensity):
        probe_real = probe_ref[mode, 0]
        probe_imag = probe_ref[mode, 1]
        exit_real = (obj_real * probe_real - obj_imag * probe_imag).astype(jnp.bfloat16)
        exit_imag = (obj_real * probe_imag + obj_imag * probe_real).astype(jnp.bfloat16)
        stacked = jnp.concatenate([exit_real, exit_imag], axis=0)
        half = jnp.dot(left_ref[...], stacked, preferred_element_type=jnp.float32).astype(jnp.bfloat16)
        wide = jnp.concatenate([half[:side], half[side:]], axis=1)
        far = jnp.dot(wide, right_ref[...], preferred_element_type=jnp.float32)
        far_ref[mode] = far
        return intensity + far[:, :side] * far[:, :side] + far[:, side:] * far[:, side:]

    intensity = lax.fori_loop(0, modes, one_mode, jnp.zeros((side, side), jnp.float32))
    ratio = amp_ref[0] / jnp.maximum(jnp.sqrt(intensity), amp_floor) - 1.0

    def store(mode, carry):
        far = far_ref[mode]
        out_ref[0, mode, 0] = (far[:, :side] * ratio).astype(jnp.bfloat16)
        out_ref[0, mode, 1] = (far[:, side:] * ratio).astype(jnp.bfloat16)
        return carry

    lax.fori_loop(0, modes, store, 0)


def forward_correction(patch, all_modes, amplitudes, forward_table):
    slots, _, side, _ = patch.shape
    modes = all_modes.shape[0]
    left = complex_table(forward_table, False)
    right = complex_table(forward_table, True)
    return pl.pallas_call(
        forward_kernel,
        grid=(slots,),
        in_specs=[
            pl.BlockSpec((1, 2, side, side), lambda s: (s, 0, 0, 0)),
            pl.BlockSpec((modes, 2, side, side), lambda s: (0, 0, 0, 0), pipeline_mode=pl.Buffered(1)),
            pl.BlockSpec((1, side, side), lambda s: (s, 0, 0)),
            pl.BlockSpec((2 * side, 2 * side), lambda s: (0, 0), pipeline_mode=pl.Buffered(1)),
            pl.BlockSpec((2 * side, 2 * side), lambda s: (0, 0), pipeline_mode=pl.Buffered(1)),
        ],
        out_specs=pl.BlockSpec((1, modes, 2, side, side), lambda s: (s, 0, 0, 0, 0)),
        out_shape=jax.ShapeDtypeStruct((slots, modes, 2, side, side), jnp.bfloat16),
        scratch_shapes=[pltpu.VMEM((modes, side, 2 * side), jnp.float32)],
        compiler_params=pltpu.CompilerParams(vmem_limit_bytes=64 * 1024 * 1024),
        cost_estimate=pl.CostEstimate(
            flops=slots * modes * 4 * (2 * side) ** 2 * side,
            bytes_accessed=slots * (modes + 3) * 2 * side * side * 4,
            transcendentals=slots * side * side,
        ),
    )(patch, all_modes, amplitudes, left, right)


def backward_kernel(comp_ref, count_ref, corr_ref, probe_ref, patch_ref, left_ref, right_ref, grad_ref, part_ref):
    side = patch_ref.shape[-1]
    modes = probe_ref.shape[0]
    own_modes = part_ref.shape[0]
    slot = pl.program_id(0)

    @pl.when(slot == 0)
    def _():
        part_ref[...] = jnp.zeros(part_ref.shape, part_ref.dtype)

    live = (slot < count_ref[0]).astype(jnp.float32)
    first_own = comp_ref[0] * own_modes
    obj_real = patch_ref[0, 0]
    obj_imag = patch_ref[0, 1]

    def one_mode(mode, carry):
        grad_real, grad_imag = carry
        stacked = jnp.concatenate([corr_ref[0, mode, 0], corr_ref[0, mode, 1]], axis=0)
        half = jnp.dot(left_ref[...], stacked, preferred_element_type=jnp.float32).astype(jnp.bfloat16)
        wide = jnp.concatenate([half[:side], half[side:]], axis=1)
        back = jnp.dot(wide, right_ref[...], preferred_element_type=jnp.float32) * live
        back_real = back[:, :side]
        back_imag = back[:, side:]
        probe_real = probe_ref[mode, 0]
        probe_imag = probe_ref[mode, 1]
        own = mode - first_own

        @pl.when((own >= 0) & (own < own_modes))
        def _():
            index = jnp.clip(own, 0, own_modes - 1)
            part_ref[index, 0] += obj_real * back_real + obj_imag * back_imag
            part_ref[index, 1] += obj_real * back_imag - obj_imag * back_real

        grad_real = grad_real + (probe_real * back_real + probe_imag * back_imag)
        grad_imag = grad_imag + (probe_real * back_imag - probe_imag * back_real)
        return grad_real, grad_imag

    zeros = jnp.zeros((side, side), jnp.float32)
    grad_real, grad_imag = lax.fori_loop(0, modes, one_mode, (zeros, zeros))
    grad_ref[0, 0] = grad_real
    grad_ref[0, 1] = grad_imag


def backward_gradients(correction, all_modes, patch, component, count, own_modes, inverse_table):
    slots, modes, _, side, _ = correction.shape
    left = complex_table(inverse_table, False)
    right = complex_table(inverse_table, True)
    grid_spec = pltpu.PrefetchScalarGridSpec(
        num_scalar_prefetch=2,
        grid=(slots,),
        in_specs=[
            pl.BlockSpec((1, modes, 2, side, side), lambda s, c, n: (s, 0, 0, 0, 0)),
            pl.BlockSpec((modes, 2, side, side), lambda s, c, n: (0, 0, 0, 0), pipeline_mode=pl.Buffered(1)),
            pl.BlockSpec((1, 2, side, side), lambda s, c, n: (s, 0, 0, 0)),
            pl.BlockSpec((2 * side, 2 * side), lambda s, c, n: (0, 0), pipeline_mode=pl.Buffered(1)),
            pl.BlockSpec((2 * side, 2 * side), lambda s, c, n: (0, 0), pipeline_mode=pl.Buffered(1)),
        ],
        out_specs=[
            pl.BlockSpec((1, 2, side, side), lambda s, c, n: (s, 0, 0, 0)),
            pl.BlockSpec((own_modes, 2, side, side), lambda s, c, n: (0, 0, 0, 0)),
        ],
    )
    return pl.pallas_call(
        backward_kernel,
        grid_spec=grid_spec,
        out_shape=[
            jax.ShapeDtypeStruct((slots, 2, side, side), jnp.float32),
            jax.ShapeDtypeStruct((own_modes, 2, side, side), jnp.float32),
        ],
        compiler_params=pltpu.CompilerParams(
            vmem_limit_bytes=64 * 1024 * 1024, dimension_semantics=("arbitrary",)
        ),
        cost_estimate=pl.CostEstimate(
            flops=slots * modes * 4 * (2 * side) ** 2 * side,
            bytes_accessed=slots * (modes + 4) * 2 * side * side * 4,
            transcendentals=0,
        ),
    )(
        jnp.reshape(component, (1,)).astype(jnp.int32),
        jnp.reshape(count, (1,)).astype(jnp.int32),
        correction,
        all_modes,
        patch,
        left,
        right,
    )


def shards(object_tiles, probe_modes, amplitudes, offsets, counts):
    side = probe_modes.shape[-1]
    tile_side = object_tiles.shape[-1]
    slots = offsets.shape[1]
    own_modes = probe_modes.shape[0]
    count = lax.axis_size("scan")
    core = lax.axis_index("scan") % 2
    sent = lax.dynamic_index_in_dim(probe_modes, core, 0, keepdims=False)
    pairs = [(s * 2 + m, (s ^ 2) * 2 + 1 - m) for s in range(count) for m in range(2)]
    got = lax.ppermute(sent, ("scan", "mode"), pairs)
    mate = lax.ppermute(got, "scan", [(s, s ^ 1) for s in range(count)])
    partner_modes = jnp.stack([jnp.where(core == 0, got, mate), jnp.where(core == 0, mate, got)])
    component = lax.axis_index("mode")
    all_modes = jnp.where(
        component == 0,
        jnp.concatenate([probe_modes, partner_modes], axis=0),
        jnp.concatenate([partner_modes, probe_modes], axis=0),
    )
    modes_here = all_modes.shape[0]
    own_tile = object_tiles[0]
    east_tile = from_behind(own_tile, "scan", -1)
    south_tile = from_behind(own_tile, "scan", -GCOLS)
    far_corner = lax.ppermute(
        own_tile, "scan", [(s, s - GCOLS - 1) for s in range(count) if (s - GCOLS - 1) % 2 == 1 and s >= GCOLS + 1]
        + [(s, s - GCOLS - 1 + count) for s in range(count) if (s - GCOLS - 1) % 2 == 1 and s < GCOLS + 1]
    )
    near_corner = lax.ppermute(south_tile, "scan", [(s, s - 1) for s in range(count) if s % 2 == 1])
    corner_tile = jnp.where(lax.axis_index("scan") % 2 == 0, near_corner, far_corner)
    upper_band = jnp.concatenate([own_tile, east_tile], axis=2)
    lower_band = jnp.concatenate([south_tile, corner_tile], axis=2)
    extended = jnp.concatenate([upper_band, lower_band], axis=1)
    slot_offsets = offsets[0]
    windows = jnp.stack(
        [
            lax.dynamic_slice(
                extended,
                (0, slot_offsets[slot_id, 0] - 1, slot_offsets[slot_id, 1] - 1),
                (2, side + 2, side + 2),
            )
            for slot_id in range(slots)
        ]
    )
    patch = windows[:, :, 1:-1, 1:-1]
    grad_y = (windows[:, :, 2:, 1:-1] - windows[:, :, :-2, 1:-1]) * 0.5
    grad_x = (windows[:, :, 1:-1, 2:] - windows[:, :, 1:-1, :-2]) * 0.5
    obj_real = patch[:, 0][:, None]
    obj_imag = patch[:, 1][:, None]
    probe_real = all_modes[:, 0][None]
    probe_imag = all_modes[:, 1][None]
    forward_table = dft_tables(side, -1.0)
    inverse_table = dft_tables(side, 1.0)
    correction = forward_correction(patch, all_modes, amplitudes[0], forward_table)
    whole_grad, probe_partial = backward_gradients(
        correction, all_modes, patch, component, counts[0], own_modes, inverse_table
    )
    position_y = jnp.sum(whole_grad * grad_y, axis=(1, 2, 3))
    position_x = jnp.sum(whole_grad * grad_x, axis=(1, 2, 3))
    positions = jnp.stack([position_y, position_x], axis=1) / side
    mine = lax.dynamic_slice_in_dim(whole_grad, component, 1, axis=1)
    gradient_plane = jnp.zeros((2 * tile_side, 2 * tile_side), jnp.float32)
    for slot_id in range(slots):
        start = (slot_offsets[slot_id, 0], slot_offsets[slot_id, 1])
        current = lax.dynamic_slice(gradient_plane, start, (side, side))
        gradient_plane = lax.dynamic_update_slice(gradient_plane, current + mine[slot_id, 0], start)
    probe_partial, gradient_plane = lax.optimization_barrier((probe_partial, gradient_plane))
    received_east = from_behind(gradient_plane[:tile_side, tile_side:], "scan", 1)
    received_south = from_behind(gradient_plane[tile_side:, :tile_side], "scan", GCOLS)
    received_corner = from_behind(gradient_plane[tile_side:, tile_side:], "scan", GCOLS + 1)
    probe_grad, (received_east, received_south, received_corner) = scan_all_reduce(
        probe_partial, (received_east, received_south, received_corner)
    )
    total_grad = (
        gradient_plane[:tile_side, :tile_side] + received_east + received_south + received_corner
    )
    return (total_grad[None, None], probe_grad, positions[None])


def solution(mesh):
    return jax.shard_map(
        shards,
        mesh=mesh,
        in_specs=(
            P("scan", None, None, None),
            P("mode", None, None, None),
            P("scan", None, None, None),
            P("scan", None, None),
            P("scan"),
        ),
        out_specs=(
            P("scan", "mode", None, None),
            P("mode", None, None, None),
            P("scan", None, None),
        ),
        check_vma=False,
    )
```

```python
import math

import jax
import jax.numpy as jnp
from jax import lax
from jax.experimental import pallas as pl
from jax.experimental.pallas import tpu as pltpu
from jax.sharding import PartitionSpec as P

GCOLS = 8
CORE = (1, 2)
ZLO = (2, 2)
YAX = (4, 4)
XAX = (16, 4)


amp_floor = 1.0


def from_behind(value, axis, steps):
    count = lax.axis_size(axis)
    pairs = [(source, (source + steps) % count) for source in range(count)]
    return lax.ppermute(value, axis, pairs)


def sub_shift(value, sub, shift):
    stride, size = sub
    count = lax.axis_size("scan")
    pairs = []
    for source in range(count):
        coord = (source // stride) % size
        pairs.append((source, source + (((coord + shift) % size) - coord) * stride))
    return lax.ppermute(value, "scan", pairs)


def sub_coord(sub):
    stride, size = sub
    return (lax.axis_index("scan") // stride) % size


def pair_reduce_scatter(data, sub):
    coord = sub_coord(sub)
    half = data.shape[0] // 2
    mine = lax.dynamic_slice_in_dim(data, coord * half, half, axis=0)
    other = lax.dynamic_slice_in_dim(data, (1 - coord) * half, half, axis=0)
    return mine + sub_shift(other, sub, 1)


def pair_all_gather(data, sub):
    coord = sub_coord(sub)
    got = sub_shift(data, sub, 1)
    first = jnp.where(coord == 0, data, got)
    second = jnp.where(coord == 0, got, data)
    return jnp.concatenate([first, second], axis=0)


def direct_reduce_scatter(data, sub):
    size = sub[1]
    coord = sub_coord(sub)
    chunks = data.reshape(size, data.shape[0] // size, -1)
    total = chunks[coord]
    for shift in range(1, size):
        total = total + sub_shift(chunks[(coord + shift) % size], sub, shift)
    return total


def direct_all_gather(data, sub):
    size = sub[1]
    coord = sub_coord(sub)
    out = jnp.zeros((size,) + data.shape, data.dtype)
    out = lax.dynamic_update_index_in_dim(out, data, coord, 0)
    for shift in range(1, size):
        got = sub_shift(data, sub, shift)
        out = lax.dynamic_update_index_in_dim(out, got, (coord - shift) % size, 0)
    return out.reshape(size * data.shape[0], -1)


def ring_reduce_scatter(data, sub):
    size = sub[1]
    coord = sub_coord(sub)
    rows = data.shape[0] // (2 * size)
    fwd = data[: rows * size].reshape(size, rows, -1)
    bwd = data[rows * size :].reshape(size, rows, -1)
    part_f = fwd[(coord - 1) % size]
    part_b = bwd[(coord + 1) % size]
    for step in range(size - 1):
        got_f = sub_shift(part_f, sub, 1)
        got_b = sub_shift(part_b, sub, -1)
        part_f = got_f + fwd[(coord - step - 2) % size]
        part_b = got_b + bwd[(coord + step + 2) % size]
    return jnp.concatenate([part_f, part_b], axis=0)


def ring_all_gather(data, sub):
    size = sub[1]
    coord = sub_coord(sub)
    rows = data.shape[0] // 2
    piece_f = data[:rows]
    piece_b = data[rows:]
    out_f = jnp.zeros((size, rows, data.shape[1]), data.dtype)
    out_b = jnp.zeros((size, rows, data.shape[1]), data.dtype)
    out_f = lax.dynamic_update_index_in_dim(out_f, piece_f, coord, 0)
    out_b = lax.dynamic_update_index_in_dim(out_b, piece_b, coord, 0)
    for step in range(size - 1):
        piece_f = sub_shift(piece_f, sub, 1)
        piece_b = sub_shift(piece_b, sub, -1)
        out_f = lax.dynamic_update_index_in_dim(out_f, piece_f, (coord - step - 1) % size, 0)
        out_b = lax.dynamic_update_index_in_dim(out_b, piece_b, (coord + step + 1) % size, 0)
    return jnp.concatenate([out_f.reshape(size * rows, -1), out_b.reshape(size * rows, -1)], axis=0)


def scan_all_reduce(value, early, tied):
    shape = value.shape
    data = value.reshape(-1, shape[-1])
    data = pair_reduce_scatter(data, CORE)
    data = direct_reduce_scatter(data, XAX)
    data = direct_reduce_scatter(data, YAX)
    data = pair_reduce_scatter(data, ZLO)
    data, early = lax.optimization_barrier((data, early))
    data = pair_all_gather(data, ZLO)
    data = direct_all_gather(data, YAX)
    data, tied = lax.optimization_barrier((data, tied))
    data = direct_all_gather(data, XAX)
    data = pair_all_gather(data, CORE)
    return data.reshape(shape), early, tied


def dft_tables(length_side, direction_sign):
    index_row = jnp.arange(length_side, dtype=jnp.int32)
    product = index_row[:, None] * index_row[None, :] % length_side
    angles = product.astype(jnp.float32) * (2.0 * math.pi / length_side)
    scale_factor = 1.0 / math.sqrt(length_side)
    real_part = jnp.cos(angles) * scale_factor
    imag_part = direction_sign * jnp.sin(angles) * scale_factor
    matrix_table = jnp.stack(
        [jnp.stack([real_part, -imag_part]), jnp.stack([imag_part, real_part])]
    )
    return matrix_table.astype(jnp.bfloat16)


def transform(field, matrix_table):
    first_section = jnp.einsum(
        "dcpq,bcqk->bdpk", matrix_table, field, preferred_element_type=jnp.float32
    ).astype(jnp.bfloat16)
    return jnp.einsum(
        "bcpq,dcqk->bdpk", first_section, matrix_table, preferred_element_type=jnp.float32
    )


def complex_table(matrix_table, transposed):
    if transposed:
        rows = [jnp.concatenate([matrix_table[0, c], matrix_table[1, c]], axis=1) for c in range(2)]
    else:
        rows = [jnp.concatenate([matrix_table[d, 0], matrix_table[d, 1]], axis=1) for d in range(2)]
    return jnp.concatenate(rows, axis=0)


def forward_kernel(patch_ref, probe_ref, amp_ref, left_ref, right_ref, out_ref, far_ref):
    side = patch_ref.shape[-1]
    modes = probe_ref.shape[0]
    obj_real = patch_ref[0, 0]
    obj_imag = patch_ref[0, 1]

    def one_mode(mode, intensity):
        probe_real = probe_ref[mode, 0]
        probe_imag = probe_ref[mode, 1]
        exit_real = (obj_real * probe_real - obj_imag * probe_imag).astype(jnp.bfloat16)
        exit_imag = (obj_real * probe_imag + obj_imag * probe_real).astype(jnp.bfloat16)
        stacked = jnp.concatenate([exit_real, exit_imag], axis=0)
        half = jnp.dot(left_ref[...], stacked, preferred_element_type=jnp.float32).astype(jnp.bfloat16)
        wide = jnp.concatenate([half[:side], half[side:]], axis=1)
        far = jnp.dot(wide, right_ref[...], preferred_element_type=jnp.float32)
        far_ref[mode] = far
        return intensity + far[:, :side] * far[:, :side] + far[:, side:] * far[:, side:]

    intensity = lax.fori_loop(0, modes, one_mode, jnp.zeros((side, side), jnp.float32))
    ratio = amp_ref[0] / jnp.maximum(jnp.sqrt(intensity), amp_floor) - 1.0

    def store(mode, carry):
        far = far_ref[mode]
        out_ref[0, mode, 0] = (far[:, :side] * ratio).astype(jnp.bfloat16)
        out_ref[0, mode, 1] = (far[:, side:] * ratio).astype(jnp.bfloat16)
        return carry

    lax.fori_loop(0, modes, store, 0)


def forward_correction(patch, all_modes, amplitudes, forward_table):
    slots, _, side, _ = patch.shape
    modes = all_modes.shape[0]
    left = complex_table(forward_table, False)
    right = complex_table(forward_table, True)
    return pl.pallas_call(
        forward_kernel,
        grid=(slots,),
        in_specs=[
            pl.BlockSpec((1, 2, side, side), lambda s: (s, 0, 0, 0)),
            pl.BlockSpec((modes, 2, side, side), lambda s: (0, 0, 0, 0), pipeline_mode=pl.Buffered(1)),
            pl.BlockSpec((1, side, side), lambda s: (s, 0, 0)),
            pl.BlockSpec((2 * side, 2 * side), lambda s: (0, 0), pipeline_mode=pl.Buffered(1)),
            pl.BlockSpec((2 * side, 2 * side), lambda s: (0, 0), pipeline_mode=pl.Buffered(1)),
        ],
        out_specs=pl.BlockSpec((1, modes, 2, side, side), lambda s: (s, 0, 0, 0, 0)),
        out_shape=jax.ShapeDtypeStruct((slots, modes, 2, side, side), jnp.bfloat16),
        scratch_shapes=[pltpu.VMEM((modes, side, 2 * side), jnp.float32)],
        compiler_params=pltpu.CompilerParams(vmem_limit_bytes=64 * 1024 * 1024),
        cost_estimate=pl.CostEstimate(
            flops=slots * modes * 4 * (2 * side) ** 2 * side,
            bytes_accessed=slots * (modes + 3) * 2 * side * side * 4,
            transcendentals=slots * side * side,
        ),
    )(patch, all_modes, amplitudes, left, right)


def backward_kernel(comp_ref, count_ref, corr_ref, probe_ref, patch_ref, left_ref, right_ref, grad_ref, part_ref):
    side = patch_ref.shape[-1]
    modes = probe_ref.shape[0]
    own_modes = part_ref.shape[0]
    slot = pl.program_id(0)

    @pl.when(slot == 0)
    def _():
        part_ref[...] = jnp.zeros(part_ref.shape, part_ref.dtype)

    live = (slot < count_ref[0]).astype(jnp.float32)
    first_own = comp_ref[0] * own_modes
    obj_real = patch_ref[0, 0]
    obj_imag = patch_ref[0, 1]

    def one_mode(mode, carry):
        grad_real, grad_imag = carry
        stacked = jnp.concatenate([corr_ref[0, mode, 0], corr_ref[0, mode, 1]], axis=0)
        half = jnp.dot(left_ref[...], stacked, preferred_element_type=jnp.float32).astype(jnp.bfloat16)
        wide = jnp.concatenate([half[:side], half[side:]], axis=1)
        back = jnp.dot(wide, right_ref[...], preferred_element_type=jnp.float32) * live
        back_real = back[:, :side]
        back_imag = back[:, side:]
        probe_real = probe_ref[mode, 0]
        probe_imag = probe_ref[mode, 1]
        own = mode - first_own

        @pl.when((own >= 0) & (own < own_modes))
        def _():
            index = jnp.clip(own, 0, own_modes - 1)
            part_ref[index, 0] += obj_real * back_real + obj_imag * back_imag
            part_ref[index, 1] += obj_real * back_imag - obj_imag * back_real

        grad_real = grad_real + (probe_real * back_real + probe_imag * back_imag)
        grad_imag = grad_imag + (probe_real * back_imag - probe_imag * back_real)
        return grad_real, grad_imag

    zeros = jnp.zeros((side, side), jnp.float32)
    grad_real, grad_imag = lax.fori_loop(0, modes, one_mode, (zeros, zeros))
    grad_ref[0, 0] = grad_real
    grad_ref[0, 1] = grad_imag


def backward_gradients(correction, all_modes, patch, component, count, own_modes, inverse_table):
    slots, modes, _, side, _ = correction.shape
    left = complex_table(inverse_table, False)
    right = complex_table(inverse_table, True)
    grid_spec = pltpu.PrefetchScalarGridSpec(
        num_scalar_prefetch=2,
        grid=(slots,),
        in_specs=[
            pl.BlockSpec((1, modes, 2, side, side), lambda s, c, n: (s, 0, 0, 0, 0)),
            pl.BlockSpec((modes, 2, side, side), lambda s, c, n: (0, 0, 0, 0), pipeline_mode=pl.Buffered(1)),
            pl.BlockSpec((1, 2, side, side), lambda s, c, n: (s, 0, 0, 0)),
            pl.BlockSpec((2 * side, 2 * side), lambda s, c, n: (0, 0), pipeline_mode=pl.Buffered(1)),
            pl.BlockSpec((2 * side, 2 * side), lambda s, c, n: (0, 0), pipeline_mode=pl.Buffered(1)),
        ],
        out_specs=[
            pl.BlockSpec((1, 2, side, side), lambda s, c, n: (s, 0, 0, 0)),
            pl.BlockSpec((own_modes, 2, side, side), lambda s, c, n: (0, 0, 0, 0)),
        ],
    )
    return pl.pallas_call(
        backward_kernel,
        grid_spec=grid_spec,
        out_shape=[
            jax.ShapeDtypeStruct((slots, 2, side, side), jnp.float32),
            jax.ShapeDtypeStruct((own_modes, 2, side, side), jnp.float32),
        ],
        compiler_params=pltpu.CompilerParams(
            vmem_limit_bytes=64 * 1024 * 1024, dimension_semantics=("arbitrary",)
        ),
        cost_estimate=pl.CostEstimate(
            flops=slots * modes * 4 * (2 * side) ** 2 * side,
            bytes_accessed=slots * (modes + 4) * 2 * side * side * 4,
            transcendentals=0,
        ),
    )(
        jnp.reshape(component, (1,)).astype(jnp.int32),
        jnp.reshape(count, (1,)).astype(jnp.int32),
        correction,
        all_modes,
        patch,
        left,
        right,
    )


def shards(object_tiles, probe_modes, amplitudes, offsets, counts):
    side = probe_modes.shape[-1]
    tile_side = object_tiles.shape[-1]
    slots = offsets.shape[1]
    own_modes = probe_modes.shape[0]
    count = lax.axis_size("scan")
    core = lax.axis_index("scan") % 2
    sent = lax.dynamic_index_in_dim(probe_modes, core, 0, keepdims=False)
    pairs = [(s * 2 + m, (s ^ 2) * 2 + 1 - m) for s in range(count) for m in range(2)]
    got = lax.ppermute(sent, ("scan", "mode"), pairs)
    mate = lax.ppermute(got, "scan", [(s, s ^ 1) for s in range(count)])
    partner_modes = jnp.stack([jnp.where(core == 0, got, mate), jnp.where(core == 0, mate, got)])
    component = lax.axis_index("mode")
    all_modes = jnp.where(
        component == 0,
        jnp.concatenate([probe_modes, partner_modes], axis=0),
        jnp.concatenate([partner_modes, probe_modes], axis=0),
    )
    modes_here = all_modes.shape[0]
    own_tile = object_tiles[0]
    east_tile = from_behind(own_tile, "scan", -1)
    south_tile = from_behind(own_tile, "scan", -GCOLS)
    far_corner = lax.ppermute(
        own_tile, "scan", [(s, s - GCOLS - 1) for s in range(count) if (s - GCOLS - 1) % 2 == 1 and s >= GCOLS + 1]
        + [(s, s - GCOLS - 1 + count) for s in range(count) if (s - GCOLS - 1) % 2 == 1 and s < GCOLS + 1]
    )
    near_corner = lax.ppermute(south_tile, "scan", [(s, s - 1) for s in range(count) if s % 2 == 1])
    corner_tile = jnp.where(lax.axis_index("scan") % 2 == 0, near_corner, far_corner)
    upper_band = jnp.concatenate([own_tile, east_tile], axis=2)
    lower_band = jnp.concatenate([south_tile, corner_tile], axis=2)
    extended = jnp.concatenate([upper_band, lower_band], axis=1)
    slot_offsets = offsets[0]
    windows = jnp.stack(
        [
            lax.dynamic_slice(
                extended,
                (0, slot_offsets[slot_id, 0] - 1, slot_offsets[slot_id, 1] - 1),
                (2, side + 2, side + 2),
            )
            for slot_id in range(slots)
        ]
    )
    patch = windows[:, :, 1:-1, 1:-1]
    grad_y = (windows[:, :, 2:, 1:-1] - windows[:, :, :-2, 1:-1]) * 0.5
    grad_x = (windows[:, :, 1:-1, 2:] - windows[:, :, 1:-1, :-2]) * 0.5
    obj_real = patch[:, 0][:, None]
    obj_imag = patch[:, 1][:, None]
    probe_real = all_modes[:, 0][None]
    probe_imag = all_modes[:, 1][None]
    forward_table = dft_tables(side, -1.0)
    inverse_table = dft_tables(side, 1.0)
    correction = forward_correction(patch, all_modes, amplitudes[0], forward_table)
    whole_grad, probe_partial = backward_gradients(
        correction, all_modes, patch, component, counts[0], own_modes, inverse_table
    )
    position_y = jnp.sum(whole_grad * grad_y, axis=(1, 2, 3))
    position_x = jnp.sum(whole_grad * grad_x, axis=(1, 2, 3))
    positions = jnp.stack([position_y, position_x], axis=1) / side
    mine = lax.dynamic_slice_in_dim(whole_grad, component, 1, axis=1)
    gradient_plane = jnp.zeros((2 * tile_side, 2 * tile_side), jnp.float32)
    for slot_id in range(slots):
        start = (slot_offsets[slot_id, 0], slot_offsets[slot_id, 1])
        current = lax.dynamic_slice(gradient_plane, start, (side, side))
        gradient_plane = lax.dynamic_update_slice(gradient_plane, current + mine[slot_id, 0], start)
    probe_partial, gradient_plane = lax.optimization_barrier((probe_partial, gradient_plane))
    received_east = from_behind(gradient_plane[:tile_side, tile_side:], "scan", 1)
    received_south = from_behind(gradient_plane[tile_side:, :tile_side], "scan", GCOLS)
    received_corner = from_behind(gradient_plane[tile_side:, tile_side:], "scan", GCOLS + 1)
    probe_grad, positions, (received_east, received_south, received_corner) = scan_all_reduce(
        probe_partial, positions, (received_east, received_south, received_corner)
    )
    total_grad = (
        gradient_plane[:tile_side, :tile_side] + received_east + received_south + received_corner
    )
    return (total_grad[None, None], probe_grad, positions[None])


def solution(mesh):
    return jax.shard_map(
        shards,
        mesh=mesh,
        in_specs=(
            P("scan", None, None, None),
            P("mode", None, None, None),
            P("scan", None, None, None),
            P("scan", None, None),
            P("scan"),
        ),
        out_specs=(
            P("scan", "mode", None, None),
            P("mode", None, None, None),
            P("scan", None, None),
        ),
        check_vma=False,
    )
```

```python
import math

import jax
import jax.numpy as jnp
from jax import lax
from jax.experimental import pallas as pl
from jax.experimental.pallas import tpu as pltpu
from jax.sharding import PartitionSpec as P

GCOLS = 8
CORE = (1, 2)
ZLO = (2, 2)
YAX = (4, 4)
XAX = (16, 4)


amp_floor = 1.0


def from_behind(value, axis, steps):
    count = lax.axis_size(axis)
    pairs = [(source, (source + steps) % count) for source in range(count)]
    return lax.ppermute(value, axis, pairs)


def sub_shift(value, sub, shift):
    stride, size = sub
    count = lax.axis_size("scan")
    pairs = []
    for source in range(count):
        coord = (source // stride) % size
        pairs.append((source, source + (((coord + shift) % size) - coord) * stride))
    return lax.ppermute(value, "scan", pairs)


def sub_coord(sub):
    stride, size = sub
    return (lax.axis_index("scan") // stride) % size


def pair_reduce_scatter(data, sub):
    coord = sub_coord(sub)
    half = data.shape[0] // 2
    mine = lax.dynamic_slice_in_dim(data, coord * half, half, axis=0)
    other = lax.dynamic_slice_in_dim(data, (1 - coord) * half, half, axis=0)
    return mine + sub_shift(other, sub, 1)


def pair_all_gather(data, sub):
    coord = sub_coord(sub)
    got = sub_shift(data, sub, 1)
    first = jnp.where(coord == 0, data, got)
    second = jnp.where(coord == 0, got, data)
    return jnp.concatenate([first, second], axis=0)


def direct_reduce_scatter(data, sub):
    size = sub[1]
    coord = sub_coord(sub)
    chunks = data.reshape(size, data.shape[0] // size, -1)
    total = chunks[coord]
    for shift in range(1, size):
        total = total + sub_shift(chunks[(coord + shift) % size], sub, shift)
    return total


def direct_all_gather(data, sub):
    size = sub[1]
    coord = sub_coord(sub)
    out = jnp.zeros((size,) + data.shape, data.dtype)
    out = lax.dynamic_update_index_in_dim(out, data, coord, 0)
    for shift in range(1, size):
        got = sub_shift(data, sub, shift)
        out = lax.dynamic_update_index_in_dim(out, got, (coord - shift) % size, 0)
    return out.reshape(size * data.shape[0], -1)


def ring_reduce_scatter(data, sub):
    size = sub[1]
    coord = sub_coord(sub)
    rows = data.shape[0] // (2 * size)
    fwd = data[: rows * size].reshape(size, rows, -1)
    bwd = data[rows * size :].reshape(size, rows, -1)
    part_f = fwd[(coord - 1) % size]
    part_b = bwd[(coord + 1) % size]
    for step in range(size - 1):
        got_f = sub_shift(part_f, sub, 1)
        got_b = sub_shift(part_b, sub, -1)
        part_f = got_f + fwd[(coord - step - 2) % size]
        part_b = got_b + bwd[(coord + step + 2) % size]
    return jnp.concatenate([part_f, part_b], axis=0)


def ring_all_gather(data, sub):
    size = sub[1]
    coord = sub_coord(sub)
    rows = data.shape[0] // 2
    piece_f = data[:rows]
    piece_b = data[rows:]
    out_f = jnp.zeros((size, rows, data.shape[1]), data.dtype)
    out_b = jnp.zeros((size, rows, data.shape[1]), data.dtype)
    out_f = lax.dynamic_update_index_in_dim(out_f, piece_f, coord, 0)
    out_b = lax.dynamic_update_index_in_dim(out_b, piece_b, coord, 0)
    for step in range(size - 1):
        piece_f = sub_shift(piece_f, sub, 1)
        piece_b = sub_shift(piece_b, sub, -1)
        out_f = lax.dynamic_update_index_in_dim(out_f, piece_f, (coord - step - 1) % size, 0)
        out_b = lax.dynamic_update_index_in_dim(out_b, piece_b, (coord + step + 1) % size, 0)
    return jnp.concatenate([out_f.reshape(size * rows, -1), out_b.reshape(size * rows, -1)], axis=0)


def scan_all_reduce(value, early, tied):
    shape = value.shape
    data = value.reshape(-1, shape[-1])
    data = pair_reduce_scatter(data, CORE)
    data = direct_reduce_scatter(data, XAX)
    data = direct_reduce_scatter(data, YAX)
    data = pair_reduce_scatter(data, ZLO)
    data, early, tied = lax.optimization_barrier((data, early, tied))
    data = pair_all_gather(data, ZLO)
    data = direct_all_gather(data, YAX)
    data = direct_all_gather(data, XAX)
    data = pair_all_gather(data, CORE)
    return data.reshape(shape), early, tied


def dft_tables(length_side, direction_sign):
    index_row = jnp.arange(length_side, dtype=jnp.int32)
    product = index_row[:, None] * index_row[None, :] % length_side
    angles = product.astype(jnp.float32) * (2.0 * math.pi / length_side)
    scale_factor = 1.0 / math.sqrt(length_side)
    real_part = jnp.cos(angles) * scale_factor
    imag_part = direction_sign * jnp.sin(angles) * scale_factor
    matrix_table = jnp.stack(
        [jnp.stack([real_part, -imag_part]), jnp.stack([imag_part, real_part])]
    )
    return matrix_table.astype(jnp.bfloat16)


def transform(field, matrix_table):
    first_section = jnp.einsum(
        "dcpq,bcqk->bdpk", matrix_table, field, preferred_element_type=jnp.float32
    ).astype(jnp.bfloat16)
    return jnp.einsum(
        "bcpq,dcqk->bdpk", first_section, matrix_table, preferred_element_type=jnp.float32
    )


def complex_table(matrix_table, transposed):
    if transposed:
        rows = [jnp.concatenate([matrix_table[0, c], matrix_table[1, c]], axis=1) for c in range(2)]
    else:
        rows = [jnp.concatenate([matrix_table[d, 0], matrix_table[d, 1]], axis=1) for d in range(2)]
    return jnp.concatenate(rows, axis=0)


def forward_kernel(patch_ref, probe_ref, amp_ref, left_ref, right_ref, out_ref, far_ref):
    side = patch_ref.shape[-1]
    modes = probe_ref.shape[0]
    obj_real = patch_ref[0, 0]
    obj_imag = patch_ref[0, 1]

    def one_mode(mode, intensity):
        probe_real = probe_ref[mode, 0]
        probe_imag = probe_ref[mode, 1]
        exit_real = (obj_real * probe_real - obj_imag * probe_imag).astype(jnp.bfloat16)
        exit_imag = (obj_real * probe_imag + obj_imag * probe_real).astype(jnp.bfloat16)
        stacked = jnp.concatenate([exit_real, exit_imag], axis=0)
        half = jnp.dot(left_ref[...], stacked, preferred_element_type=jnp.float32).astype(jnp.bfloat16)
        wide = jnp.concatenate([half[:side], half[side:]], axis=1)
        far = jnp.dot(wide, right_ref[...], preferred_element_type=jnp.float32)
        far_ref[mode] = far
        return intensity + far[:, :side] * far[:, :side] + far[:, side:] * far[:, side:]

    intensity = lax.fori_loop(0, modes, one_mode, jnp.zeros((side, side), jnp.float32))
    ratio = amp_ref[0] / jnp.maximum(jnp.sqrt(intensity), amp_floor) - 1.0

    def store(mode, carry):
        far = far_ref[mode]
        out_ref[0, mode, 0] = (far[:, :side] * ratio).astype(jnp.bfloat16)
        out_ref[0, mode, 1] = (far[:, side:] * ratio).astype(jnp.bfloat16)
        return carry

    lax.fori_loop(0, modes, store, 0)


def forward_correction(patch, all_modes, amplitudes, forward_table):
    slots, _, side, _ = patch.shape
    modes = all_modes.shape[0]
    left = complex_table(forward_table, False)
    right = complex_table(forward_table, True)
    return pl.pallas_call(
        forward_kernel,
        grid=(slots,),
        in_specs=[
            pl.BlockSpec((1, 2, side, side), lambda s: (s, 0, 0, 0)),
            pl.BlockSpec((modes, 2, side, side), lambda s: (0, 0, 0, 0), pipeline_mode=pl.Buffered(1)),
            pl.BlockSpec((1, side, side), lambda s: (s, 0, 0)),
            pl.BlockSpec((2 * side, 2 * side), lambda s: (0, 0), pipeline_mode=pl.Buffered(1)),
            pl.BlockSpec((2 * side, 2 * side), lambda s: (0, 0), pipeline_mode=pl.Buffered(1)),
        ],
        out_specs=pl.BlockSpec((1, modes, 2, side, side), lambda s: (s, 0, 0, 0, 0)),
        out_shape=jax.ShapeDtypeStruct((slots, modes, 2, side, side), jnp.bfloat16),
        scratch_shapes=[pltpu.VMEM((modes, side, 2 * side), jnp.float32)],
        compiler_params=pltpu.CompilerParams(vmem_limit_bytes=64 * 1024 * 1024),
        cost_estimate=pl.CostEstimate(
            flops=slots * modes * 4 * (2 * side) ** 2 * side,
            bytes_accessed=slots * (modes + 3) * 2 * side * side * 4,
            transcendentals=slots * side * side,
        ),
    )(patch, all_modes, amplitudes, left, right)


def backward_kernel(comp_ref, count_ref, corr_ref, probe_ref, patch_ref, left_ref, right_ref, grad_ref, part_ref):
    side = patch_ref.shape[-1]
    modes = probe_ref.shape[0]
    own_modes = part_ref.shape[0]
    slot = pl.program_id(0)

    @pl.when(slot == 0)
    def _():
        part_ref[...] = jnp.zeros(part_ref.shape, part_ref.dtype)

    live = (slot < count_ref[0]).astype(jnp.float32)
    first_own = comp_ref[0] * own_modes
    obj_real = patch_ref[0, 0]
    obj_imag = patch_ref[0, 1]

    def one_mode(mode, carry):
        grad_real, grad_imag = carry
        stacked = jnp.concatenate([corr_ref[0, mode, 0], corr_ref[0, mode, 1]], axis=0)
        half = jnp.dot(left_ref[...], stacked, preferred_element_type=jnp.float32).astype(jnp.bfloat16)
        wide = jnp.concatenate([half[:side], half[side:]], axis=1)
        back = jnp.dot(wide, right_ref[...], preferred_element_type=jnp.float32) * live
        back_real = back[:, :side]
        back_imag = back[:, side:]
        probe_real = probe_ref[mode, 0]
        probe_imag = probe_ref[mode, 1]
        own = mode - first_own

        @pl.when((own >= 0) & (own < own_modes))
        def _():
            index = jnp.clip(own, 0, own_modes - 1)
            part_ref[index, 0] += obj_real * back_real + obj_imag * back_imag
            part_ref[index, 1] += obj_real * back_imag - obj_imag * back_real

        grad_real = grad_real + (probe_real * back_real + probe_imag * back_imag)
        grad_imag = grad_imag + (probe_real * back_imag - probe_imag * back_real)
        return grad_real, grad_imag

    zeros = jnp.zeros((side, side), jnp.float32)
    grad_real, grad_imag = lax.fori_loop(0, modes, one_mode, (zeros, zeros))
    grad_ref[0, 0] = grad_real
    grad_ref[0, 1] = grad_imag


def backward_gradients(correction, all_modes, patch, component, count, own_modes, inverse_table):
    slots, modes, _, side, _ = correction.shape
    left = complex_table(inverse_table, False)
    right = complex_table(inverse_table, True)
    grid_spec = pltpu.PrefetchScalarGridSpec(
        num_scalar_prefetch=2,
        grid=(slots,),
        in_specs=[
            pl.BlockSpec((1, modes, 2, side, side), lambda s, c, n: (s, 0, 0, 0, 0)),
            pl.BlockSpec((modes, 2, side, side), lambda s, c, n: (0, 0, 0, 0), pipeline_mode=pl.Buffered(1)),
            pl.BlockSpec((1, 2, side, side), lambda s, c, n: (s, 0, 0, 0)),
            pl.BlockSpec((2 * side, 2 * side), lambda s, c, n: (0, 0), pipeline_mode=pl.Buffered(1)),
            pl.BlockSpec((2 * side, 2 * side), lambda s, c, n: (0, 0), pipeline_mode=pl.Buffered(1)),
        ],
        out_specs=[
            pl.BlockSpec((1, 2, side, side), lambda s, c, n: (s, 0, 0, 0)),
            pl.BlockSpec((own_modes, 2, side, side), lambda s, c, n: (0, 0, 0, 0)),
        ],
    )
    return pl.pallas_call(
        backward_kernel,
        grid_spec=grid_spec,
        out_shape=[
            jax.ShapeDtypeStruct((slots, 2, side, side), jnp.float32),
            jax.ShapeDtypeStruct((own_modes, 2, side, side), jnp.float32),
        ],
        compiler_params=pltpu.CompilerParams(
            vmem_limit_bytes=64 * 1024 * 1024, dimension_semantics=("arbitrary",)
        ),
        cost_estimate=pl.CostEstimate(
            flops=slots * modes * 4 * (2 * side) ** 2 * side,
            bytes_accessed=slots * (modes + 4) * 2 * side * side * 4,
            transcendentals=0,
        ),
    )(
        jnp.reshape(component, (1,)).astype(jnp.int32),
        jnp.reshape(count, (1,)).astype(jnp.int32),
        correction,
        all_modes,
        patch,
        left,
        right,
    )


def shards(object_tiles, probe_modes, amplitudes, offsets, counts):
    side = probe_modes.shape[-1]
    tile_side = object_tiles.shape[-1]
    slots = offsets.shape[1]
    own_modes = probe_modes.shape[0]
    count = lax.axis_size("scan")
    core = lax.axis_index("scan") % 2
    sent = lax.dynamic_index_in_dim(probe_modes, core, 0, keepdims=False)
    pairs = [(s * 2 + m, (s ^ 2) * 2 + 1 - m) for s in range(count) for m in range(2)]
    got = lax.ppermute(sent, ("scan", "mode"), pairs)
    mate = lax.ppermute(got, "scan", [(s, s ^ 1) for s in range(count)])
    partner_modes = jnp.stack([jnp.where(core == 0, got, mate), jnp.where(core == 0, mate, got)])
    component = lax.axis_index("mode")
    all_modes = jnp.where(
        component == 0,
        jnp.concatenate([probe_modes, partner_modes], axis=0),
        jnp.concatenate([partner_modes, probe_modes], axis=0),
    )
    modes_here = all_modes.shape[0]
    own_tile = object_tiles[0]
    east_tile = from_behind(own_tile, "scan", -1)
    south_tile = from_behind(own_tile, "scan", -GCOLS)
    far_corner = lax.ppermute(
        own_tile, "scan", [(s, s - GCOLS - 1) for s in range(count) if (s - GCOLS - 1) % 2 == 1 and s >= GCOLS + 1]
        + [(s, s - GCOLS - 1 + count) for s in range(count) if (s - GCOLS - 1) % 2 == 1 and s < GCOLS + 1]
    )
    near_corner = lax.ppermute(south_tile, "scan", [(s, s - 1) for s in range(count) if s % 2 == 1])
    corner_tile = jnp.where(lax.axis_index("scan") % 2 == 0, near_corner, far_corner)
    upper_band = jnp.concatenate([own_tile, east_tile], axis=2)
    lower_band = jnp.concatenate([south_tile, corner_tile], axis=2)
    extended = jnp.concatenate([upper_band, lower_band], axis=1)
    slot_offsets = offsets[0]
    windows = jnp.stack(
        [
            lax.dynamic_slice(
                extended,
                (0, slot_offsets[slot_id, 0] - 1, slot_offsets[slot_id, 1] - 1),
                (2, side + 2, side + 2),
            )
            for slot_id in range(slots)
        ]
    )
    patch = windows[:, :, 1:-1, 1:-1]
    grad_y = (windows[:, :, 2:, 1:-1] - windows[:, :, :-2, 1:-1]) * 0.5
    grad_x = (windows[:, :, 1:-1, 2:] - windows[:, :, 1:-1, :-2]) * 0.5
    obj_real = patch[:, 0][:, None]
    obj_imag = patch[:, 1][:, None]
    probe_real = all_modes[:, 0][None]
    probe_imag = all_modes[:, 1][None]
    forward_table = dft_tables(side, -1.0)
    inverse_table = dft_tables(side, 1.0)
    correction = forward_correction(patch, all_modes, amplitudes[0], forward_table)
    whole_grad, probe_partial = backward_gradients(
        correction, all_modes, patch, component, counts[0], own_modes, inverse_table
    )
    position_y = jnp.sum(whole_grad * grad_y, axis=(1, 2, 3))
    position_x = jnp.sum(whole_grad * grad_x, axis=(1, 2, 3))
    positions = jnp.stack([position_y, position_x], axis=1) / side
    mine = lax.dynamic_slice_in_dim(whole_grad, component, 1, axis=1)
    gradient_plane = jnp.zeros((2 * tile_side, 2 * tile_side), jnp.float32)
    for slot_id in range(slots):
        start = (slot_offsets[slot_id, 0], slot_offsets[slot_id, 1])
        current = lax.dynamic_slice(gradient_plane, start, (side, side))
        gradient_plane = lax.dynamic_update_slice(gradient_plane, current + mine[slot_id, 0], start)
    probe_partial, gradient_plane = lax.optimization_barrier((probe_partial, gradient_plane))
    received_east = from_behind(gradient_plane[:tile_side, tile_side:], "scan", 1)
    received_south = from_behind(gradient_plane[tile_side:, :tile_side], "scan", GCOLS)
    received_corner = from_behind(gradient_plane[tile_side:, tile_side:], "scan", GCOLS + 1)
    probe_grad, positions, (received_east, received_south, received_corner) = scan_all_reduce(
        probe_partial, positions, (received_east, received_south, received_corner)
    )
    total_grad = (
        gradient_plane[:tile_side, :tile_side] + received_east + received_south + received_corner
    )
    return (total_grad[None, None], probe_grad, positions[None])


def solution(mesh):
    return jax.shard_map(
        shards,
        mesh=mesh,
        in_specs=(
            P("scan", None, None, None),
            P("mode", None, None, None),
            P("scan", None, None, None),
            P("scan", None, None),
            P("scan"),
        ),
        out_specs=(
            P("scan", "mode", None, None),
            P("mode", None, None, None),
            P("scan", None, None),
        ),
        check_vma=False,
    )
```

```python
import math

import jax
import jax.numpy as jnp
from jax import lax
from jax.experimental import pallas as pl
from jax.experimental.pallas import tpu as pltpu
from jax.sharding import PartitionSpec as P

GCOLS = 8
CORE = (1, 2)
ZLO = (2, 2)
YAX = (4, 4)
XAX = (16, 4)


amp_floor = 1.0


def from_behind(value, axis, steps):
    count = lax.axis_size(axis)
    pairs = [(source, (source + steps) % count) for source in range(count)]
    return lax.ppermute(value, axis, pairs)


def sub_shift(value, sub, shift):
    stride, size = sub
    count = lax.axis_size("scan")
    pairs = []
    for source in range(count):
        coord = (source // stride) % size
        pairs.append((source, source + (((coord + shift) % size) - coord) * stride))
    return lax.ppermute(value, "scan", pairs)


def sub_coord(sub):
    stride, size = sub
    return (lax.axis_index("scan") // stride) % size


def pair_reduce_scatter(data, sub):
    coord = sub_coord(sub)
    half = data.shape[0] // 2
    mine = lax.dynamic_slice_in_dim(data, coord * half, half, axis=0)
    other = lax.dynamic_slice_in_dim(data, (1 - coord) * half, half, axis=0)
    return mine + sub_shift(other, sub, 1)


def pair_all_gather(data, sub):
    coord = sub_coord(sub)
    got = sub_shift(data, sub, 1)
    first = jnp.where(coord == 0, data, got)
    second = jnp.where(coord == 0, got, data)
    return jnp.concatenate([first, second], axis=0)


def direct_reduce_scatter(data, sub):
    size = sub[1]
    coord = sub_coord(sub)
    chunks = data.reshape(size, data.shape[0] // size, -1)
    total = chunks[coord]
    for shift in range(1, size):
        total = total + sub_shift(chunks[(coord + shift) % size], sub, shift)
    return total


def direct_all_gather(data, sub):
    size = sub[1]
    coord = sub_coord(sub)
    out = jnp.zeros((size,) + data.shape, data.dtype)
    out = lax.dynamic_update_index_in_dim(out, data, coord, 0)
    for shift in range(1, size):
        got = sub_shift(data, sub, shift)
        out = lax.dynamic_update_index_in_dim(out, got, (coord - shift) % size, 0)
    return out.reshape(size * data.shape[0], -1)


def ring_reduce_scatter(data, sub):
    size = sub[1]
    coord = sub_coord(sub)
    rows = data.shape[0] // (2 * size)
    fwd = data[: rows * size].reshape(size, rows, -1)
    bwd = data[rows * size :].reshape(size, rows, -1)
    part_f = fwd[(coord - 1) % size]
    part_b = bwd[(coord + 1) % size]
    for step in range(size - 1):
        got_f = sub_shift(part_f, sub, 1)
        got_b = sub_shift(part_b, sub, -1)
        part_f = got_f + fwd[(coord - step - 2) % size]
        part_b = got_b + bwd[(coord + step + 2) % size]
    return jnp.concatenate([part_f, part_b], axis=0)


def ring_all_gather(data, sub):
    size = sub[1]
    coord = sub_coord(sub)
    rows = data.shape[0] // 2
    piece_f = data[:rows]
    piece_b = data[rows:]
    out_f = jnp.zeros((size, rows, data.shape[1]), data.dtype)
    out_b = jnp.zeros((size, rows, data.shape[1]), data.dtype)
    out_f = lax.dynamic_update_index_in_dim(out_f, piece_f, coord, 0)
    out_b = lax.dynamic_update_index_in_dim(out_b, piece_b, coord, 0)
    for step in range(size - 1):
        piece_f = sub_shift(piece_f, sub, 1)
        piece_b = sub_shift(piece_b, sub, -1)
        out_f = lax.dynamic_update_index_in_dim(out_f, piece_f, (coord - step - 1) % size, 0)
        out_b = lax.dynamic_update_index_in_dim(out_b, piece_b, (coord + step + 1) % size, 0)
    return jnp.concatenate([out_f.reshape(size * rows, -1), out_b.reshape(size * rows, -1)], axis=0)


def scan_all_reduce(value, early, tied):
    shape = value.shape
    data = value.reshape(-1, shape[-1])
    data = pair_reduce_scatter(data, CORE)
    data = direct_reduce_scatter(data, XAX)
    data = direct_reduce_scatter(data, YAX)
    data = pair_reduce_scatter(data, ZLO)
    data, early, tied = lax.optimization_barrier((data, early, tied))
    data = pair_all_gather(data, ZLO)
    data = direct_all_gather(data, YAX)
    data = direct_all_gather(data, XAX)
    data = pair_all_gather(data, CORE)
    return data.reshape(shape), early, tied


def dft_tables(length_side, direction_sign):
    index_row = jnp.arange(length_side, dtype=jnp.int32)
    product = index_row[:, None] * index_row[None, :] % length_side
    angles = product.astype(jnp.float32) * (2.0 * math.pi / length_side)
    scale_factor = 1.0 / math.sqrt(length_side)
    real_part = jnp.cos(angles) * scale_factor
    imag_part = direction_sign * jnp.sin(angles) * scale_factor
    matrix_table = jnp.stack(
        [jnp.stack([real_part, -imag_part]), jnp.stack([imag_part, real_part])]
    )
    return matrix_table.astype(jnp.bfloat16)


def transform(field, matrix_table):
    first_section = jnp.einsum(
        "dcpq,bcqk->bdpk", matrix_table, field, preferred_element_type=jnp.float32
    ).astype(jnp.bfloat16)
    return jnp.einsum(
        "bcpq,dcqk->bdpk", first_section, matrix_table, preferred_element_type=jnp.float32
    )


def complex_table(matrix_table, transposed):
    if transposed:
        rows = [jnp.concatenate([matrix_table[0, c], matrix_table[1, c]], axis=1) for c in range(2)]
    else:
        rows = [jnp.concatenate([matrix_table[d, 0], matrix_table[d, 1]], axis=1) for d in range(2)]
    return jnp.concatenate(rows, axis=0)


def forward_kernel(patch_ref, probe_ref, amp_ref, left_ref, right_ref, out_ref, far_ref):
    side = patch_ref.shape[-1]
    modes = probe_ref.shape[0]
    obj_real = patch_ref[0, 0]
    obj_imag = patch_ref[0, 1]

    def one_mode(mode, intensity):
        probe_real = probe_ref[mode, 0]
        probe_imag = probe_ref[mode, 1]
        exit_real = (obj_real * probe_real - obj_imag * probe_imag).astype(jnp.bfloat16)
        exit_imag = (obj_real * probe_imag + obj_imag * probe_real).astype(jnp.bfloat16)
        stacked = jnp.concatenate([exit_real, exit_imag], axis=0)
        half = jnp.dot(left_ref[...], stacked, preferred_element_type=jnp.float32).astype(jnp.bfloat16)
        wide = jnp.concatenate([half[:side], half[side:]], axis=1)
        far = jnp.dot(wide, right_ref[...], preferred_element_type=jnp.float32)
        far_ref[mode] = far
        return intensity + far[:, :side] * far[:, :side] + far[:, side:] * far[:, side:]

    intensity = lax.fori_loop(0, modes, one_mode, jnp.zeros((side, side), jnp.float32))
    ratio = amp_ref[0] / jnp.maximum(jnp.sqrt(intensity), amp_floor) - 1.0

    def store(mode, carry):
        far = far_ref[mode]
        out_ref[0, mode, 0] = (far[:, :side] * ratio).astype(jnp.bfloat16)
        out_ref[0, mode, 1] = (far[:, side:] * ratio).astype(jnp.bfloat16)
        return carry

    lax.fori_loop(0, modes, store, 0)


def forward_correction(patch, all_modes, amplitudes, forward_table):
    slots, _, side, _ = patch.shape
    modes = all_modes.shape[0]
    left = complex_table(forward_table, False)
    right = complex_table(forward_table, True)
    return pl.pallas_call(
        forward_kernel,
        grid=(slots,),
        in_specs=[
            pl.BlockSpec((1, 2, side, side), lambda s: (s, 0, 0, 0)),
            pl.BlockSpec((modes, 2, side, side), lambda s: (0, 0, 0, 0), pipeline_mode=pl.Buffered(1)),
            pl.BlockSpec((1, side, side), lambda s: (s, 0, 0)),
            pl.BlockSpec((2 * side, 2 * side), lambda s: (0, 0), pipeline_mode=pl.Buffered(1)),
            pl.BlockSpec((2 * side, 2 * side), lambda s: (0, 0), pipeline_mode=pl.Buffered(1)),
        ],
        out_specs=pl.BlockSpec((1, modes, 2, side, side), lambda s: (s, 0, 0, 0, 0)),
        out_shape=jax.ShapeDtypeStruct((slots, modes, 2, side, side), jnp.bfloat16),
        scratch_shapes=[pltpu.VMEM((modes, side, 2 * side), jnp.float32)],
        compiler_params=pltpu.CompilerParams(vmem_limit_bytes=64 * 1024 * 1024),
        cost_estimate=pl.CostEstimate(
            flops=slots * modes * 4 * (2 * side) ** 2 * side,
            bytes_accessed=slots * (modes + 3) * 2 * side * side * 4,
            transcendentals=slots * side * side,
        ),
    )(patch, all_modes, amplitudes, left, right)


def backward_kernel(block_ref, count_ref, corr_ref, probe_ref, patch_ref, left_ref, right_ref, grad_ref, *part):
    side = patch_ref.shape[-1]
    modes = probe_ref.shape[0]
    slot = pl.program_id(0)
    if part:
        part_ref = part[0]

        @pl.when(slot == 0)
        def _():
            part_ref[...] = jnp.zeros(part_ref.shape, part_ref.dtype)

    live = (slot < count_ref[0]).astype(jnp.float32)
    obj_real = patch_ref[0, 0]
    obj_imag = patch_ref[0, 1]

    def one_mode(mode, carry):
        grad_real, grad_imag = carry
        stacked = jnp.concatenate([corr_ref[0, mode, 0], corr_ref[0, mode, 1]], axis=0)
        half = jnp.dot(left_ref[...], stacked, preferred_element_type=jnp.float32).astype(jnp.bfloat16)
        wide = jnp.concatenate([half[:side], half[side:]], axis=1)
        back = jnp.dot(wide, right_ref[...], preferred_element_type=jnp.float32) * live
        back_real = back[:, :side]
        back_imag = back[:, side:]
        probe_real = probe_ref[mode, 0]
        probe_imag = probe_ref[mode, 1]
        if part:
            part_ref[mode, 0] += obj_real * back_real + obj_imag * back_imag
            part_ref[mode, 1] += obj_real * back_imag - obj_imag * back_real

        grad_real = grad_real + (probe_real * back_real + probe_imag * back_imag)
        grad_imag = grad_imag + (probe_real * back_imag - probe_imag * back_real)
        return grad_real, grad_imag

    zeros = jnp.zeros((side, side), jnp.float32)
    grad_real, grad_imag = lax.fori_loop(0, modes, one_mode, (zeros, zeros))
    grad_ref[0, 0] = grad_real
    grad_ref[0, 1] = grad_imag


def backward_gradients(correction, all_modes, patch, block, count, block_modes, inverse_table, with_partial):
    slots, modes, _, side, _ = correction.shape
    left = complex_table(inverse_table, False)
    right = complex_table(inverse_table, True)
    out_specs = [pl.BlockSpec((1, 2, side, side), lambda s, b, n: (s, 0, 0, 0))]
    out_shape = [jax.ShapeDtypeStruct((slots, 2, side, side), jnp.float32)]
    if with_partial:
        out_specs.append(pl.BlockSpec((block_modes, 2, side, side), lambda s, b, n: (0, 0, 0, 0)))
        out_shape.append(jax.ShapeDtypeStruct((block_modes, 2, side, side), jnp.float32))
    grid_spec = pltpu.PrefetchScalarGridSpec(
        num_scalar_prefetch=2,
        grid=(slots,),
        in_specs=[
            pl.BlockSpec((1, block_modes, 2, side, side), lambda s, b, n: (s, b[0], 0, 0, 0)),
            pl.BlockSpec((block_modes, 2, side, side), lambda s, b, n: (b[0], 0, 0, 0), pipeline_mode=pl.Buffered(1)),
            pl.BlockSpec((1, 2, side, side), lambda s, b, n: (s, 0, 0, 0)),
            pl.BlockSpec((2 * side, 2 * side), lambda s, b, n: (0, 0), pipeline_mode=pl.Buffered(1)),
            pl.BlockSpec((2 * side, 2 * side), lambda s, b, n: (0, 0), pipeline_mode=pl.Buffered(1)),
        ],
        out_specs=out_specs,
    )
    return pl.pallas_call(
        backward_kernel,
        grid_spec=grid_spec,
        out_shape=out_shape,
        compiler_params=pltpu.CompilerParams(
            vmem_limit_bytes=64 * 1024 * 1024, dimension_semantics=("arbitrary",)
        ),
        cost_estimate=pl.CostEstimate(
            flops=slots * block_modes * 4 * (2 * side) ** 2 * side,
            bytes_accessed=slots * (block_modes + 4) * 2 * side * side * 4,
            transcendentals=0,
        ),
    )(
        jnp.reshape(block, (1,)).astype(jnp.int32),
        jnp.reshape(count, (1,)).astype(jnp.int32),
        correction,
        all_modes,
        patch,
        left,
        right,
    )


def shards(object_tiles, probe_modes, amplitudes, offsets, counts):
    side = probe_modes.shape[-1]
    tile_side = object_tiles.shape[-1]
    slots = offsets.shape[1]
    own_modes = probe_modes.shape[0]
    count = lax.axis_size("scan")
    core = lax.axis_index("scan") % 2
    sent = lax.dynamic_index_in_dim(probe_modes, core, 0, keepdims=False)
    pairs = [(s * 2 + m, (s ^ 2) * 2 + 1 - m) for s in range(count) for m in range(2)]
    got = lax.ppermute(sent, ("scan", "mode"), pairs)
    mate = lax.ppermute(got, "scan", [(s, s ^ 1) for s in range(count)])
    partner_modes = jnp.stack([jnp.where(core == 0, got, mate), jnp.where(core == 0, mate, got)])
    component = lax.axis_index("mode")
    all_modes = jnp.where(
        component == 0,
        jnp.concatenate([probe_modes, partner_modes], axis=0),
        jnp.concatenate([partner_modes, probe_modes], axis=0),
    )
    modes_here = all_modes.shape[0]
    own_tile = object_tiles[0]
    east_tile = from_behind(own_tile, "scan", -1)
    south_tile = from_behind(own_tile, "scan", -GCOLS)
    far_corner = lax.ppermute(
        own_tile, "scan", [(s, s - GCOLS - 1) for s in range(count) if (s - GCOLS - 1) % 2 == 1 and s >= GCOLS + 1]
        + [(s, s - GCOLS - 1 + count) for s in range(count) if (s - GCOLS - 1) % 2 == 1 and s < GCOLS + 1]
    )
    near_corner = lax.ppermute(south_tile, "scan", [(s, s - 1) for s in range(count) if s % 2 == 1])
    corner_tile = jnp.where(lax.axis_index("scan") % 2 == 0, near_corner, far_corner)
    upper_band = jnp.concatenate([own_tile, east_tile], axis=2)
    lower_band = jnp.concatenate([south_tile, corner_tile], axis=2)
    extended = jnp.concatenate([upper_band, lower_band], axis=1)
    slot_offsets = offsets[0]
    windows = jnp.stack(
        [
            lax.dynamic_slice(
                extended,
                (0, slot_offsets[slot_id, 0] - 1, slot_offsets[slot_id, 1] - 1),
                (2, side + 2, side + 2),
            )
            for slot_id in range(slots)
        ]
    )
    patch = windows[:, :, 1:-1, 1:-1]
    grad_y = (windows[:, :, 2:, 1:-1] - windows[:, :, :-2, 1:-1]) * 0.5
    grad_x = (windows[:, :, 1:-1, 2:] - windows[:, :, 1:-1, :-2]) * 0.5
    obj_real = patch[:, 0][:, None]
    obj_imag = patch[:, 1][:, None]
    probe_real = all_modes[:, 0][None]
    probe_imag = all_modes[:, 1][None]
    forward_table = dft_tables(side, -1.0)
    inverse_table = dft_tables(side, 1.0)
    correction = forward_correction(patch, all_modes, amplitudes[0], forward_table)
    own_grad, probe_partial = backward_gradients(
        correction, all_modes, patch, component, counts[0], own_modes, inverse_table, True
    )
    (partner_grad,) = backward_gradients(
        correction, all_modes, patch, 1 - component, counts[0], own_modes, inverse_table, False
    )
    whole_grad = own_grad + partner_grad
    position_y = jnp.sum(whole_grad * grad_y, axis=(1, 2, 3))
    position_x = jnp.sum(whole_grad * grad_x, axis=(1, 2, 3))
    positions = jnp.stack([position_y, position_x], axis=1) / side
    mine = lax.dynamic_slice_in_dim(whole_grad, component, 1, axis=1)
    gradient_plane = jnp.zeros((2 * tile_side, 2 * tile_side), jnp.float32)
    for slot_id in range(slots):
        start = (slot_offsets[slot_id, 0], slot_offsets[slot_id, 1])
        current = lax.dynamic_slice(gradient_plane, start, (side, side))
        gradient_plane = lax.dynamic_update_slice(gradient_plane, current + mine[slot_id, 0], start)
    received_east = from_behind(gradient_plane[:tile_side, tile_side:], "scan", 1)
    received_south = from_behind(gradient_plane[tile_side:, :tile_side], "scan", GCOLS)
    received_corner = from_behind(gradient_plane[tile_side:, tile_side:], "scan", GCOLS + 1)
    probe_grad, positions, (received_east, received_south, received_corner) = scan_all_reduce(
        probe_partial, positions, (received_east, received_south, received_corner)
    )
    total_grad = (
        gradient_plane[:tile_side, :tile_side] + received_east + received_south + received_corner
    )
    return (total_grad[None, None], probe_grad, positions[None])


def solution(mesh):
    return jax.shard_map(
        shards,
        mesh=mesh,
        in_specs=(
            P("scan", None, None, None),
            P("mode", None, None, None),
            P("scan", None, None, None),
            P("scan", None, None),
            P("scan"),
        ),
        out_specs=(
            P("scan", "mode", None, None),
            P("mode", None, None, None),
            P("scan", None, None),
        ),
        check_vma=False,
    )
```

```python
import math

import jax
import jax.numpy as jnp
from jax import lax
from jax.experimental import pallas as pl
from jax.experimental.pallas import tpu as pltpu
from jax.sharding import PartitionSpec as P

GCOLS = 8
CORE = (1, 2)
ZLO = (2, 2)
YAX = (4, 4)
XAX = (16, 4)


amp_floor = 1.0


def from_behind(value, axis, steps):
    count = lax.axis_size(axis)
    pairs = [(source, (source + steps) % count) for source in range(count)]
    return lax.ppermute(value, axis, pairs)


def sub_shift(value, sub, shift):
    stride, size = sub
    count = lax.axis_size("scan")
    pairs = []
    for source in range(count):
        coord = (source // stride) % size
        pairs.append((source, source + (((coord + shift) % size) - coord) * stride))
    return lax.ppermute(value, "scan", pairs)


def sub_coord(sub):
    stride, size = sub
    return (lax.axis_index("scan") // stride) % size


def pair_reduce_scatter(data, sub):
    coord = sub_coord(sub)
    half = data.shape[0] // 2
    mine = lax.dynamic_slice_in_dim(data, coord * half, half, axis=0)
    other = lax.dynamic_slice_in_dim(data, (1 - coord) * half, half, axis=0)
    return mine + sub_shift(other, sub, 1)


def pair_all_gather(data, sub):
    coord = sub_coord(sub)
    got = sub_shift(data, sub, 1)
    first = jnp.where(coord == 0, data, got)
    second = jnp.where(coord == 0, got, data)
    return jnp.concatenate([first, second], axis=0)


def direct_reduce_scatter(data, sub):
    size = sub[1]
    coord = sub_coord(sub)
    chunks = data.reshape(size, data.shape[0] // size, -1)
    total = chunks[coord]
    for shift in range(1, size):
        total = total + sub_shift(chunks[(coord + shift) % size], sub, shift)
    return total


def direct_all_gather(data, sub):
    size = sub[1]
    coord = sub_coord(sub)
    out = jnp.zeros((size,) + data.shape, data.dtype)
    out = lax.dynamic_update_index_in_dim(out, data, coord, 0)
    for shift in range(1, size):
        got = sub_shift(data, sub, shift)
        out = lax.dynamic_update_index_in_dim(out, got, (coord - shift) % size, 0)
    return out.reshape(size * data.shape[0], -1)


def ring_reduce_scatter(data, sub):
    size = sub[1]
    coord = sub_coord(sub)
    rows = data.shape[0] // (2 * size)
    fwd = data[: rows * size].reshape(size, rows, -1)
    bwd = data[rows * size :].reshape(size, rows, -1)
    part_f = fwd[(coord - 1) % size]
    part_b = bwd[(coord + 1) % size]
    for step in range(size - 1):
        got_f = sub_shift(part_f, sub, 1)
        got_b = sub_shift(part_b, sub, -1)
        part_f = got_f + fwd[(coord - step - 2) % size]
        part_b = got_b + bwd[(coord + step + 2) % size]
    return jnp.concatenate([part_f, part_b], axis=0)


def ring_all_gather(data, sub):
    size = sub[1]
    coord = sub_coord(sub)
    rows = data.shape[0] // 2
    piece_f = data[:rows]
    piece_b = data[rows:]
    out_f = jnp.zeros((size, rows, data.shape[1]), data.dtype)
    out_b = jnp.zeros((size, rows, data.shape[1]), data.dtype)
    out_f = lax.dynamic_update_index_in_dim(out_f, piece_f, coord, 0)
    out_b = lax.dynamic_update_index_in_dim(out_b, piece_b, coord, 0)
    for step in range(size - 1):
        piece_f = sub_shift(piece_f, sub, 1)
        piece_b = sub_shift(piece_b, sub, -1)
        out_f = lax.dynamic_update_index_in_dim(out_f, piece_f, (coord - step - 1) % size, 0)
        out_b = lax.dynamic_update_index_in_dim(out_b, piece_b, (coord + step + 1) % size, 0)
    return jnp.concatenate([out_f.reshape(size * rows, -1), out_b.reshape(size * rows, -1)], axis=0)


def scan_all_reduce(value, early, tied):
    shape = value.shape
    data = value.reshape(-1, shape[-1])
    data = pair_reduce_scatter(data, CORE)
    data = direct_reduce_scatter(data, XAX)
    data = direct_reduce_scatter(data, YAX)
    data = pair_reduce_scatter(data, ZLO)
    data, early, tied = lax.optimization_barrier((data, early, tied))
    data = pair_all_gather(data, ZLO)
    data = direct_all_gather(data, YAX)
    data = direct_all_gather(data, XAX)
    data = pair_all_gather(data, CORE)
    return data.reshape(shape), early, tied


def dft_tables(length_side, direction_sign):
    index_row = jnp.arange(length_side, dtype=jnp.int32)
    product = index_row[:, None] * index_row[None, :] % length_side
    angles = product.astype(jnp.float32) * (2.0 * math.pi / length_side)
    scale_factor = 1.0 / math.sqrt(length_side)
    real_part = jnp.cos(angles) * scale_factor
    imag_part = direction_sign * jnp.sin(angles) * scale_factor
    matrix_table = jnp.stack(
        [jnp.stack([real_part, -imag_part]), jnp.stack([imag_part, real_part])]
    )
    return matrix_table.astype(jnp.bfloat16)


def transform(field, matrix_table):
    first_section = jnp.einsum(
        "dcpq,bcqk->bdpk", matrix_table, field, preferred_element_type=jnp.float32
    ).astype(jnp.bfloat16)
    return jnp.einsum(
        "bcpq,dcqk->bdpk", first_section, matrix_table, preferred_element_type=jnp.float32
    )


def complex_table(matrix_table, transposed):
    if transposed:
        rows = [jnp.concatenate([matrix_table[0, c], matrix_table[1, c]], axis=1) for c in range(2)]
    else:
        rows = [jnp.concatenate([matrix_table[d, 0], matrix_table[d, 1]], axis=1) for d in range(2)]
    return jnp.concatenate(rows, axis=0)


def forward_kernel(patch_ref, probe_ref, amp_ref, left_ref, right_ref, out_ref, far_ref):
    side = patch_ref.shape[-1]
    modes = probe_ref.shape[0]
    obj_real = patch_ref[0, 0]
    obj_imag = patch_ref[0, 1]

    def one_mode(mode, intensity):
        probe_real = probe_ref[mode, 0]
        probe_imag = probe_ref[mode, 1]
        exit_real = (obj_real * probe_real - obj_imag * probe_imag).astype(jnp.bfloat16)
        exit_imag = (obj_real * probe_imag + obj_imag * probe_real).astype(jnp.bfloat16)
        stacked = jnp.concatenate([exit_real, exit_imag], axis=0)
        half = jnp.dot(left_ref[...], stacked, preferred_element_type=jnp.float32).astype(jnp.bfloat16)
        wide = jnp.concatenate([half[:side], half[side:]], axis=1)
        far = jnp.dot(wide, right_ref[...], preferred_element_type=jnp.float32)
        far_ref[mode] = far
        return intensity + far[:, :side] * far[:, :side] + far[:, side:] * far[:, side:]

    intensity = lax.fori_loop(0, modes, one_mode, jnp.zeros((side, side), jnp.float32))
    ratio = amp_ref[0] / jnp.maximum(jnp.sqrt(intensity), amp_floor) - 1.0

    def store(mode, carry):
        far = far_ref[mode]
        out_ref[0, mode, 0] = (far[:, :side] * ratio).astype(jnp.bfloat16)
        out_ref[0, mode, 1] = (far[:, side:] * ratio).astype(jnp.bfloat16)
        return carry

    lax.fori_loop(0, modes, store, 0)


def forward_correction(patch, all_modes, amplitudes, forward_table):
    slots, _, side, _ = patch.shape
    modes = all_modes.shape[0]
    left = complex_table(forward_table, False)
    right = complex_table(forward_table, True)
    return pl.pallas_call(
        forward_kernel,
        grid=(slots,),
        in_specs=[
            pl.BlockSpec((1, 2, side, side), lambda s: (s, 0, 0, 0)),
            pl.BlockSpec((modes, 2, side, side), lambda s: (0, 0, 0, 0), pipeline_mode=pl.Buffered(1)),
            pl.BlockSpec((1, side, side), lambda s: (s, 0, 0)),
            pl.BlockSpec((2 * side, 2 * side), lambda s: (0, 0), pipeline_mode=pl.Buffered(1)),
            pl.BlockSpec((2 * side, 2 * side), lambda s: (0, 0), pipeline_mode=pl.Buffered(1)),
        ],
        out_specs=pl.BlockSpec((1, modes, 2, side, side), lambda s: (s, 0, 0, 0, 0)),
        out_shape=jax.ShapeDtypeStruct((slots, modes, 2, side, side), jnp.bfloat16),
        scratch_shapes=[pltpu.VMEM((modes, side, 2 * side), jnp.float32)],
        compiler_params=pltpu.CompilerParams(vmem_limit_bytes=64 * 1024 * 1024),
        cost_estimate=pl.CostEstimate(
            flops=slots * modes * 4 * (2 * side) ** 2 * side,
            bytes_accessed=slots * (modes + 3) * 2 * side * side * 4,
            transcendentals=slots * side * side,
        ),
    )(patch, all_modes, amplitudes, left, right)


def backward_kernel(block_ref, count_ref, corr_ref, probe_ref, patch_ref, left_ref, right_ref, grad_ref, *part):
    side = patch_ref.shape[-1]
    modes = probe_ref.shape[0]
    slot = pl.program_id(0)
    if part:
        part_ref = part[0]

        @pl.when(slot == 0)
        def _():
            part_ref[...] = jnp.zeros(part_ref.shape, part_ref.dtype)

    live = (slot < count_ref[0]).astype(jnp.float32)
    obj_real = patch_ref[0, 0]
    obj_imag = patch_ref[0, 1]

    def one_mode(mode, carry):
        grad_real, grad_imag = carry
        stacked = jnp.concatenate([corr_ref[0, mode, 0], corr_ref[0, mode, 1]], axis=0)
        half = jnp.dot(left_ref[...], stacked, preferred_element_type=jnp.float32).astype(jnp.bfloat16)
        wide = jnp.concatenate([half[:side], half[side:]], axis=1)
        back = jnp.dot(wide, right_ref[...], preferred_element_type=jnp.float32) * live
        back_real = back[:, :side]
        back_imag = back[:, side:]
        probe_real = probe_ref[mode, 0]
        probe_imag = probe_ref[mode, 1]
        if part:
            part_ref[mode, 0] += obj_real * back_real + obj_imag * back_imag
            part_ref[mode, 1] += obj_real * back_imag - obj_imag * back_real

        grad_real = grad_real + (probe_real * back_real + probe_imag * back_imag)
        grad_imag = grad_imag + (probe_real * back_imag - probe_imag * back_real)
        return grad_real, grad_imag

    zeros = jnp.zeros((side, side), jnp.float32)
    grad_real, grad_imag = lax.fori_loop(0, modes, one_mode, (zeros, zeros))
    grad_ref[0, 0] = grad_real
    grad_ref[0, 1] = grad_imag


def backward_gradients(correction, all_modes, patch, block, count, block_modes, inverse_table, with_partial):
    slots, modes, _, side, _ = correction.shape
    left = complex_table(inverse_table, False)
    right = complex_table(inverse_table, True)
    out_specs = [pl.BlockSpec((1, 2, side, side), lambda s, b, n: (s, 0, 0, 0))]
    out_shape = [jax.ShapeDtypeStruct((slots, 2, side, side), jnp.float32)]
    if with_partial:
        out_specs.append(pl.BlockSpec((block_modes, 2, side, side), lambda s, b, n: (0, 0, 0, 0)))
        out_shape.append(jax.ShapeDtypeStruct((block_modes, 2, side, side), jnp.float32))
    grid_spec = pltpu.PrefetchScalarGridSpec(
        num_scalar_prefetch=2,
        grid=(slots,),
        in_specs=[
            pl.BlockSpec((1, block_modes, 2, side, side), lambda s, b, n: (s, b[0], 0, 0, 0)),
            pl.BlockSpec((block_modes, 2, side, side), lambda s, b, n: (b[0], 0, 0, 0), pipeline_mode=pl.Buffered(1)),
            pl.BlockSpec((1, 2, side, side), lambda s, b, n: (s, 0, 0, 0)),
            pl.BlockSpec((2 * side, 2 * side), lambda s, b, n: (0, 0), pipeline_mode=pl.Buffered(1)),
            pl.BlockSpec((2 * side, 2 * side), lambda s, b, n: (0, 0), pipeline_mode=pl.Buffered(1)),
        ],
        out_specs=out_specs,
    )
    return pl.pallas_call(
        backward_kernel,
        grid_spec=grid_spec,
        out_shape=out_shape,
        compiler_params=pltpu.CompilerParams(
            vmem_limit_bytes=64 * 1024 * 1024, dimension_semantics=("arbitrary",)
        ),
        cost_estimate=pl.CostEstimate(
            flops=slots * block_modes * 4 * (2 * side) ** 2 * side,
            bytes_accessed=slots * (block_modes + 4) * 2 * side * side * 4,
            transcendentals=0,
        ),
    )(
        jnp.reshape(block, (1,)).astype(jnp.int32),
        jnp.reshape(count, (1,)).astype(jnp.int32),
        correction,
        all_modes,
        patch,
        left,
        right,
    )


def shards(object_tiles, probe_modes, amplitudes, offsets, counts):
    side = probe_modes.shape[-1]
    tile_side = object_tiles.shape[-1]
    slots = offsets.shape[1]
    own_modes = probe_modes.shape[0]
    count = lax.axis_size("scan")
    core = lax.axis_index("scan") % 2
    sent = lax.dynamic_index_in_dim(probe_modes, core, 0, keepdims=False)
    pairs = [(s * 2 + m, (s ^ 2) * 2 + 1 - m) for s in range(count) for m in range(2)]
    got = lax.ppermute(sent, ("scan", "mode"), pairs)
    other = lax.dynamic_index_in_dim(probe_modes, 1 - core, 0, keepdims=False)
    mate = lax.ppermute(other, "mode", [(0, 1), (1, 0)])
    partner_modes = jnp.stack([jnp.where(core == 0, got, mate), jnp.where(core == 0, mate, got)])
    component = lax.axis_index("mode")
    all_modes = jnp.where(
        component == 0,
        jnp.concatenate([probe_modes, partner_modes], axis=0),
        jnp.concatenate([partner_modes, probe_modes], axis=0),
    )
    modes_here = all_modes.shape[0]
    own_tile = object_tiles[0]
    east_tile = from_behind(own_tile, "scan", -1)
    south_tile = from_behind(own_tile, "scan", -GCOLS)
    far_corner = lax.ppermute(
        own_tile, "scan", [(s, s - GCOLS - 1) for s in range(count) if (s - GCOLS - 1) % 2 == 1 and s >= GCOLS + 1]
        + [(s, s - GCOLS - 1 + count) for s in range(count) if (s - GCOLS - 1) % 2 == 1 and s < GCOLS + 1]
    )
    near_corner = lax.ppermute(south_tile, "scan", [(s, s - 1) for s in range(count) if s % 2 == 1])
    corner_tile = jnp.where(lax.axis_index("scan") % 2 == 0, near_corner, far_corner)
    upper_band = jnp.concatenate([own_tile, east_tile], axis=2)
    lower_band = jnp.concatenate([south_tile, corner_tile], axis=2)
    extended = jnp.concatenate([upper_band, lower_band], axis=1)
    slot_offsets = offsets[0]
    windows = jnp.stack(
        [
            lax.dynamic_slice(
                extended,
                (0, slot_offsets[slot_id, 0] - 1, slot_offsets[slot_id, 1] - 1),
                (2, side + 2, side + 2),
            )
            for slot_id in range(slots)
        ]
    )
    patch = windows[:, :, 1:-1, 1:-1]
    grad_y = (windows[:, :, 2:, 1:-1] - windows[:, :, :-2, 1:-1]) * 0.5
    grad_x = (windows[:, :, 1:-1, 2:] - windows[:, :, 1:-1, :-2]) * 0.5
    obj_real = patch[:, 0][:, None]
    obj_imag = patch[:, 1][:, None]
    probe_real = all_modes[:, 0][None]
    probe_imag = all_modes[:, 1][None]
    forward_table = dft_tables(side, -1.0)
    inverse_table = dft_tables(side, 1.0)
    correction = forward_correction(patch, all_modes, amplitudes[0], forward_table)
    own_grad, probe_partial = backward_gradients(
        correction, all_modes, patch, component, counts[0], own_modes, inverse_table, True
    )
    (partner_grad,) = backward_gradients(
        correction, all_modes, patch, 1 - component, counts[0], own_modes, inverse_table, False
    )
    whole_grad = own_grad + partner_grad
    position_y = jnp.sum(whole_grad * grad_y, axis=(1, 2, 3))
    position_x = jnp.sum(whole_grad * grad_x, axis=(1, 2, 3))
    positions = jnp.stack([position_y, position_x], axis=1) / side
    mine = lax.dynamic_slice_in_dim(whole_grad, component, 1, axis=1)
    gradient_plane = jnp.zeros((2 * tile_side, 2 * tile_side), jnp.float32)
    for slot_id in range(slots):
        start = (slot_offsets[slot_id, 0], slot_offsets[slot_id, 1])
        current = lax.dynamic_slice(gradient_plane, start, (side, side))
        gradient_plane = lax.dynamic_update_slice(gradient_plane, current + mine[slot_id, 0], start)
    received_east = from_behind(gradient_plane[:tile_side, tile_side:], "scan", 1)
    received_south = from_behind(gradient_plane[tile_side:, :tile_side], "scan", GCOLS)
    received_corner = from_behind(gradient_plane[tile_side:, tile_side:], "scan", GCOLS + 1)
    probe_grad, positions, (received_east, received_south, received_corner) = scan_all_reduce(
        probe_partial, positions, (received_east, received_south, received_corner)
    )
    total_grad = (
        gradient_plane[:tile_side, :tile_side] + received_east + received_south + received_corner
    )
    return (total_grad[None, None], probe_grad, positions[None])


def solution(mesh):
    return jax.shard_map(
        shards,
        mesh=mesh,
        in_specs=(
            P("scan", None, None, None),
            P("mode", None, None, None),
            P("scan", None, None, None),
            P("scan", None, None),
            P("scan"),
        ),
        out_specs=(
            P("scan", "mode", None, None),
            P("mode", None, None, None),
            P("scan", None, None),
        ),
        check_vma=False,
    )
```

```python
import math

import jax
import jax.numpy as jnp
from jax import lax
from jax.experimental import pallas as pl
from jax.experimental.pallas import tpu as pltpu
from jax.sharding import PartitionSpec as P

GCOLS = 8
CORE = (1, 2)
ZLO = (2, 2)
YAX = (4, 4)
XAX = (16, 4)


amp_floor = 1.0


def from_behind(value, axis, steps):
    count = lax.axis_size(axis)
    pairs = [(source, (source + steps) % count) for source in range(count)]
    return lax.ppermute(value, axis, pairs)


def sub_shift(value, sub, shift):
    stride, size = sub
    count = lax.axis_size("scan")
    pairs = []
    for source in range(count):
        coord = (source // stride) % size
        pairs.append((source, source + (((coord + shift) % size) - coord) * stride))
    return lax.ppermute(value, "scan", pairs)


def sub_coord(sub):
    stride, size = sub
    return (lax.axis_index("scan") // stride) % size


def pair_reduce_scatter(data, sub):
    coord = sub_coord(sub)
    half = data.shape[0] // 2
    mine = lax.dynamic_slice_in_dim(data, coord * half, half, axis=0)
    other = lax.dynamic_slice_in_dim(data, (1 - coord) * half, half, axis=0)
    return mine + sub_shift(other, sub, 1)


def pair_all_gather(data, sub):
    coord = sub_coord(sub)
    got = sub_shift(data, sub, 1)
    first = jnp.where(coord == 0, data, got)
    second = jnp.where(coord == 0, got, data)
    return jnp.concatenate([first, second], axis=0)


def direct_reduce_scatter(data, sub):
    size = sub[1]
    coord = sub_coord(sub)
    chunks = data.reshape(size, data.shape[0] // size, -1)
    total = chunks[coord]
    for shift in range(1, size):
        total = total + sub_shift(chunks[(coord + shift) % size], sub, shift)
    return total


def direct_all_gather(data, sub):
    size = sub[1]
    coord = sub_coord(sub)
    out = jnp.zeros((size,) + data.shape, data.dtype)
    out = lax.dynamic_update_index_in_dim(out, data, coord, 0)
    for shift in range(1, size):
        got = sub_shift(data, sub, shift)
        out = lax.dynamic_update_index_in_dim(out, got, (coord - shift) % size, 0)
    return out.reshape(size * data.shape[0], -1)


def ring_reduce_scatter(data, sub):
    size = sub[1]
    coord = sub_coord(sub)
    rows = data.shape[0] // (2 * size)
    fwd = data[: rows * size].reshape(size, rows, -1)
    bwd = data[rows * size :].reshape(size, rows, -1)
    part_f = fwd[(coord - 1) % size]
    part_b = bwd[(coord + 1) % size]
    for step in range(size - 1):
        got_f = sub_shift(part_f, sub, 1)
        got_b = sub_shift(part_b, sub, -1)
        part_f = got_f + fwd[(coord - step - 2) % size]
        part_b = got_b + bwd[(coord + step + 2) % size]
    return jnp.concatenate([part_f, part_b], axis=0)


def ring_all_gather(data, sub):
    size = sub[1]
    coord = sub_coord(sub)
    rows = data.shape[0] // 2
    piece_f = data[:rows]
    piece_b = data[rows:]
    out_f = jnp.zeros((size, rows, data.shape[1]), data.dtype)
    out_b = jnp.zeros((size, rows, data.shape[1]), data.dtype)
    out_f = lax.dynamic_update_index_in_dim(out_f, piece_f, coord, 0)
    out_b = lax.dynamic_update_index_in_dim(out_b, piece_b, coord, 0)
    for step in range(size - 1):
        piece_f = sub_shift(piece_f, sub, 1)
        piece_b = sub_shift(piece_b, sub, -1)
        out_f = lax.dynamic_update_index_in_dim(out_f, piece_f, (coord - step - 1) % size, 0)
        out_b = lax.dynamic_update_index_in_dim(out_b, piece_b, (coord + step + 1) % size, 0)
    return jnp.concatenate([out_f.reshape(size * rows, -1), out_b.reshape(size * rows, -1)], axis=0)


def scan_all_reduce(value, early, tied):
    shape = value.shape
    data = value.reshape(-1, shape[-1])
    data = pair_reduce_scatter(data, CORE)
    data = direct_reduce_scatter(data, XAX)
    data = direct_reduce_scatter(data, YAX)
    data = pair_reduce_scatter(data, ZLO)
    data, early, tied = lax.optimization_barrier((data, early, tied))
    data = pair_all_gather(data, ZLO)
    data = direct_all_gather(data, YAX)
    data = direct_all_gather(data, XAX)
    data = pair_all_gather(data, CORE)
    return data.reshape(shape), early, tied


def dft_tables(length_side, direction_sign):
    index_row = jnp.arange(length_side, dtype=jnp.int32)
    product = index_row[:, None] * index_row[None, :] % length_side
    angles = product.astype(jnp.float32) * (2.0 * math.pi / length_side)
    scale_factor = 1.0 / math.sqrt(length_side)
    real_part = jnp.cos(angles) * scale_factor
    imag_part = direction_sign * jnp.sin(angles) * scale_factor
    matrix_table = jnp.stack(
        [jnp.stack([real_part, -imag_part]), jnp.stack([imag_part, real_part])]
    )
    return matrix_table.astype(jnp.bfloat16)


def transform(field, matrix_table):
    first_section = jnp.einsum(
        "dcpq,bcqk->bdpk", matrix_table, field, preferred_element_type=jnp.float32
    ).astype(jnp.bfloat16)
    return jnp.einsum(
        "bcpq,dcqk->bdpk", first_section, matrix_table, preferred_element_type=jnp.float32
    )


def complex_table(matrix_table, transposed):
    if transposed:
        rows = [jnp.concatenate([matrix_table[0, c], matrix_table[1, c]], axis=1) for c in range(2)]
    else:
        rows = [jnp.concatenate([matrix_table[d, 0], matrix_table[d, 1]], axis=1) for d in range(2)]
    return jnp.concatenate(rows, axis=0)


def forward_kernel(patch_ref, probe_ref, amp_ref, left_ref, right_ref, out_ref, far_ref):
    side = patch_ref.shape[-1]
    modes = probe_ref.shape[0]
    obj_real = patch_ref[0, 0]
    obj_imag = patch_ref[0, 1]

    def one_mode(mode, intensity):
        probe_real = probe_ref[mode, 0]
        probe_imag = probe_ref[mode, 1]
        exit_real = (obj_real * probe_real - obj_imag * probe_imag).astype(jnp.bfloat16)
        exit_imag = (obj_real * probe_imag + obj_imag * probe_real).astype(jnp.bfloat16)
        stacked = jnp.concatenate([exit_real, exit_imag], axis=0)
        half = jnp.dot(left_ref[...], stacked, preferred_element_type=jnp.float32).astype(jnp.bfloat16)
        wide = jnp.concatenate([half[:side], half[side:]], axis=1)
        far = jnp.dot(wide, right_ref[...], preferred_element_type=jnp.float32)
        far_ref[mode] = far
        return intensity + far[:, :side] * far[:, :side] + far[:, side:] * far[:, side:]

    intensity = lax.fori_loop(0, modes, one_mode, jnp.zeros((side, side), jnp.float32))
    ratio = amp_ref[0] / jnp.maximum(jnp.sqrt(intensity), amp_floor) - 1.0

    def store(mode, carry):
        far = far_ref[mode]
        out_ref[0, mode, 0] = (far[:, :side] * ratio).astype(jnp.bfloat16)
        out_ref[0, mode, 1] = (far[:, side:] * ratio).astype(jnp.bfloat16)
        return carry

    lax.fori_loop(0, modes, store, 0)


def forward_correction(patch, all_modes, amplitudes, forward_table):
    slots, _, side, _ = patch.shape
    modes = all_modes.shape[0]
    left = complex_table(forward_table, False)
    right = complex_table(forward_table, True)
    return pl.pallas_call(
        forward_kernel,
        grid=(slots,),
        in_specs=[
            pl.BlockSpec((1, 2, side, side), lambda s: (s, 0, 0, 0)),
            pl.BlockSpec((modes, 2, side, side), lambda s: (0, 0, 0, 0), pipeline_mode=pl.Buffered(1)),
            pl.BlockSpec((1, side, side), lambda s: (s, 0, 0)),
            pl.BlockSpec((2 * side, 2 * side), lambda s: (0, 0), pipeline_mode=pl.Buffered(1)),
            pl.BlockSpec((2 * side, 2 * side), lambda s: (0, 0), pipeline_mode=pl.Buffered(1)),
        ],
        out_specs=pl.BlockSpec((1, modes, 2, side, side), lambda s: (s, 0, 0, 0, 0)),
        out_shape=jax.ShapeDtypeStruct((slots, modes, 2, side, side), jnp.bfloat16),
        scratch_shapes=[pltpu.VMEM((modes, side, 2 * side), jnp.float32)],
        compiler_params=pltpu.CompilerParams(vmem_limit_bytes=64 * 1024 * 1024),
        cost_estimate=pl.CostEstimate(
            flops=slots * modes * 4 * (2 * side) ** 2 * side,
            bytes_accessed=slots * (modes + 3) * 2 * side * side * 4,
            transcendentals=slots * side * side,
        ),
    )(patch, all_modes, amplitudes, left, right)


def backward_kernel(block_ref, count_ref, corr_ref, probe_ref, patch_ref, left_ref, right_ref, grad_ref, *part):
    side = patch_ref.shape[-1]
    modes = probe_ref.shape[0]
    slot = pl.program_id(0)
    if part:
        part_ref = part[0]

        @pl.when(slot == 0)
        def _():
            part_ref[...] = jnp.zeros(part_ref.shape, part_ref.dtype)

    live = (slot < count_ref[0]).astype(jnp.float32)
    obj_real = patch_ref[0, 0]
    obj_imag = patch_ref[0, 1]

    def one_mode(mode, carry):
        grad_real, grad_imag = carry
        stacked = jnp.concatenate([corr_ref[0, mode, 0], corr_ref[0, mode, 1]], axis=0)
        half = jnp.dot(left_ref[...], stacked, preferred_element_type=jnp.float32).astype(jnp.bfloat16)
        wide = jnp.concatenate([half[:side], half[side:]], axis=1)
        back = jnp.dot(wide, right_ref[...], preferred_element_type=jnp.float32) * live
        back_real = back[:, :side]
        back_imag = back[:, side:]
        probe_real = probe_ref[mode, 0]
        probe_imag = probe_ref[mode, 1]
        if part:
            part_ref[mode, 0] += obj_real * back_real + obj_imag * back_imag
            part_ref[mode, 1] += obj_real * back_imag - obj_imag * back_real

        grad_real = grad_real + (probe_real * back_real + probe_imag * back_imag)
        grad_imag = grad_imag + (probe_real * back_imag - probe_imag * back_real)
        return grad_real, grad_imag

    zeros = jnp.zeros((side, side), jnp.float32)
    grad_real, grad_imag = lax.fori_loop(0, modes, one_mode, (zeros, zeros))
    grad_ref[0, 0] = grad_real
    grad_ref[0, 1] = grad_imag


def backward_gradients(correction, all_modes, patch, block, count, block_modes, inverse_table, with_partial):
    slots, modes, _, side, _ = correction.shape
    left = complex_table(inverse_table, False)
    right = complex_table(inverse_table, True)
    out_specs = [pl.BlockSpec((1, 2, side, side), lambda s, b, n: (s, 0, 0, 0))]
    out_shape = [jax.ShapeDtypeStruct((slots, 2, side, side), jnp.float32)]
    if with_partial:
        out_specs.append(pl.BlockSpec((block_modes, 2, side, side), lambda s, b, n: (0, 0, 0, 0)))
        out_shape.append(jax.ShapeDtypeStruct((block_modes, 2, side, side), jnp.float32))
    grid_spec = pltpu.PrefetchScalarGridSpec(
        num_scalar_prefetch=2,
        grid=(slots,),
        in_specs=[
            pl.BlockSpec((1, block_modes, 2, side, side), lambda s, b, n: (s, b[0], 0, 0, 0)),
            pl.BlockSpec((block_modes, 2, side, side), lambda s, b, n: (b[0], 0, 0, 0), pipeline_mode=pl.Buffered(1)),
            pl.BlockSpec((1, 2, side, side), lambda s, b, n: (s, 0, 0, 0)),
            pl.BlockSpec((2 * side, 2 * side), lambda s, b, n: (0, 0), pipeline_mode=pl.Buffered(1)),
            pl.BlockSpec((2 * side, 2 * side), lambda s, b, n: (0, 0), pipeline_mode=pl.Buffered(1)),
        ],
        out_specs=out_specs,
    )
    return pl.pallas_call(
        backward_kernel,
        grid_spec=grid_spec,
        out_shape=out_shape,
        compiler_params=pltpu.CompilerParams(
            vmem_limit_bytes=64 * 1024 * 1024, dimension_semantics=("arbitrary",)
        ),
        cost_estimate=pl.CostEstimate(
            flops=slots * block_modes * 4 * (2 * side) ** 2 * side,
            bytes_accessed=slots * (block_modes + 4) * 2 * side * side * 4,
            transcendentals=0,
        ),
    )(
        jnp.reshape(block, (1,)).astype(jnp.int32),
        jnp.reshape(count, (1,)).astype(jnp.int32),
        correction,
        all_modes,
        patch,
        left,
        right,
    )


def shards(object_tiles, probe_modes, amplitudes, offsets, counts):
    side = probe_modes.shape[-1]
    tile_side = object_tiles.shape[-1]
    slots = offsets.shape[1]
    own_modes = probe_modes.shape[0]
    count = lax.axis_size("scan")
    core = lax.axis_index("scan") % 2
    sent = lax.dynamic_index_in_dim(probe_modes, core, 0, keepdims=False)
    pairs = [(s * 2 + m, (s ^ 2) * 2 + 1 - m) for s in range(count) for m in range(2)]
    got = lax.ppermute(sent, ("scan", "mode"), pairs)
    other = lax.dynamic_index_in_dim(probe_modes, 1 - core, 0, keepdims=False)
    mate = lax.ppermute(other, "mode", [(0, 1), (1, 0)])
    partner_modes = jnp.stack([jnp.where(core == 0, got, mate), jnp.where(core == 0, mate, got)])
    component = lax.axis_index("mode")
    all_modes = jnp.where(
        component == 0,
        jnp.concatenate([probe_modes, partner_modes], axis=0),
        jnp.concatenate([partner_modes, probe_modes], axis=0),
    )
    modes_here = all_modes.shape[0]
    own_tile = object_tiles[0]
    east_tile = from_behind(own_tile, "scan", -1)
    south_tile = from_behind(own_tile, "scan", -GCOLS)
    corner_tile = from_behind(own_tile, "scan", -(GCOLS + 1))
    upper_band = jnp.concatenate([own_tile, east_tile], axis=2)
    lower_band = jnp.concatenate([south_tile, corner_tile], axis=2)
    extended = jnp.concatenate([upper_band, lower_band], axis=1)
    slot_offsets = offsets[0]
    windows = jnp.stack(
        [
            lax.dynamic_slice(
                extended,
                (0, slot_offsets[slot_id, 0] - 1, slot_offsets[slot_id, 1] - 1),
                (2, side + 2, side + 2),
            )
            for slot_id in range(slots)
        ]
    )
    patch = windows[:, :, 1:-1, 1:-1]
    grad_y = (windows[:, :, 2:, 1:-1] - windows[:, :, :-2, 1:-1]) * 0.5
    grad_x = (windows[:, :, 1:-1, 2:] - windows[:, :, 1:-1, :-2]) * 0.5
    obj_real = patch[:, 0][:, None]
    obj_imag = patch[:, 1][:, None]
    probe_real = all_modes[:, 0][None]
    probe_imag = all_modes[:, 1][None]
    forward_table = dft_tables(side, -1.0)
    inverse_table = dft_tables(side, 1.0)
    correction = forward_correction(patch, all_modes, amplitudes[0], forward_table)
    own_grad, probe_partial = backward_gradients(
        correction, all_modes, patch, component, counts[0], own_modes, inverse_table, True
    )
    (partner_grad,) = backward_gradients(
        correction, all_modes, patch, 1 - component, counts[0], own_modes, inverse_table, False
    )
    whole_grad = own_grad + partner_grad
    position_y = jnp.sum(whole_grad * grad_y, axis=(1, 2, 3))
    position_x = jnp.sum(whole_grad * grad_x, axis=(1, 2, 3))
    positions = jnp.stack([position_y, position_x], axis=1) / side
    mine = lax.dynamic_slice_in_dim(whole_grad, component, 1, axis=1)
    gradient_plane = jnp.zeros((2 * tile_side, 2 * tile_side), jnp.float32)
    for slot_id in range(slots):
        start = (slot_offsets[slot_id, 0], slot_offsets[slot_id, 1])
        current = lax.dynamic_slice(gradient_plane, start, (side, side))
        gradient_plane = lax.dynamic_update_slice(gradient_plane, current + mine[slot_id, 0], start)
    received_east = from_behind(gradient_plane[:tile_side, tile_side:], "scan", 1)
    received_south = from_behind(gradient_plane[tile_side:, :tile_side], "scan", GCOLS)
    received_corner = from_behind(gradient_plane[tile_side:, tile_side:], "scan", GCOLS + 1)
    probe_grad, positions, (received_east, received_south, received_corner) = scan_all_reduce(
        probe_partial, positions, (received_east, received_south, received_corner)
    )
    total_grad = (
        gradient_plane[:tile_side, :tile_side] + received_east + received_south + received_corner
    )
    return (total_grad[None, None], probe_grad, positions[None])


def solution(mesh):
    return jax.shard_map(
        shards,
        mesh=mesh,
        in_specs=(
            P("scan", None, None, None),
            P("mode", None, None, None),
            P("scan", None, None, None),
            P("scan", None, None),
            P("scan"),
        ),
        out_specs=(
            P("scan", "mode", None, None),
            P("mode", None, None, None),
            P("scan", None, None),
        ),
        check_vma=False,
    )
```

```python
import math

import jax
import jax.numpy as jnp
from jax import lax
from jax.experimental import pallas as pl
from jax.experimental.pallas import tpu as pltpu
from jax.sharding import PartitionSpec as P

GCOLS = 8
CORE = (1, 2)
ZLO = (2, 2)
YAX = (4, 4)
XAX = (16, 4)


amp_floor = 1.0


def from_behind(value, axis, steps):
    count = lax.axis_size(axis)
    pairs = [(source, (source + steps) % count) for source in range(count)]
    return lax.ppermute(value, axis, pairs)


def sub_shift(value, sub, shift):
    stride, size = sub
    count = lax.axis_size("scan")
    pairs = []
    for source in range(count):
        coord = (source // stride) % size
        pairs.append((source, source + (((coord + shift) % size) - coord) * stride))
    return lax.ppermute(value, "scan", pairs)


def sub_coord(sub):
    stride, size = sub
    return (lax.axis_index("scan") // stride) % size


def pair_reduce_scatter(data, sub):
    coord = sub_coord(sub)
    half = data.shape[0] // 2
    mine = lax.dynamic_slice_in_dim(data, coord * half, half, axis=0)
    other = lax.dynamic_slice_in_dim(data, (1 - coord) * half, half, axis=0)
    return mine + sub_shift(other, sub, 1)


def pair_all_gather(data, sub):
    coord = sub_coord(sub)
    got = sub_shift(data, sub, 1)
    first = jnp.where(coord == 0, data, got)
    second = jnp.where(coord == 0, got, data)
    return jnp.concatenate([first, second], axis=0)


def direct_reduce_scatter(data, sub):
    size = sub[1]
    coord = sub_coord(sub)
    chunks = data.reshape(size, data.shape[0] // size, -1)
    total = chunks[coord]
    for shift in range(1, size):
        total = total + sub_shift(chunks[(coord + shift) % size], sub, shift)
    return total


def direct_all_gather(data, sub):
    size = sub[1]
    coord = sub_coord(sub)
    out = jnp.zeros((size,) + data.shape, data.dtype)
    out = lax.dynamic_update_index_in_dim(out, data, coord, 0)
    for shift in range(1, size):
        got = sub_shift(data, sub, shift)
        out = lax.dynamic_update_index_in_dim(out, got, (coord - shift) % size, 0)
    return out.reshape(size * data.shape[0], -1)


def ring_reduce_scatter(data, sub):
    size = sub[1]
    coord = sub_coord(sub)
    rows = data.shape[0] // (2 * size)
    fwd = data[: rows * size].reshape(size, rows, -1)
    bwd = data[rows * size :].reshape(size, rows, -1)
    part_f = fwd[(coord - 1) % size]
    part_b = bwd[(coord + 1) % size]
    for step in range(size - 1):
        got_f = sub_shift(part_f, sub, 1)
        got_b = sub_shift(part_b, sub, -1)
        part_f = got_f + fwd[(coord - step - 2) % size]
        part_b = got_b + bwd[(coord + step + 2) % size]
    return jnp.concatenate([part_f, part_b], axis=0)


def ring_all_gather(data, sub):
    size = sub[1]
    coord = sub_coord(sub)
    rows = data.shape[0] // 2
    piece_f = data[:rows]
    piece_b = data[rows:]
    out_f = jnp.zeros((size, rows, data.shape[1]), data.dtype)
    out_b = jnp.zeros((size, rows, data.shape[1]), data.dtype)
    out_f = lax.dynamic_update_index_in_dim(out_f, piece_f, coord, 0)
    out_b = lax.dynamic_update_index_in_dim(out_b, piece_b, coord, 0)
    for step in range(size - 1):
        piece_f = sub_shift(piece_f, sub, 1)
        piece_b = sub_shift(piece_b, sub, -1)
        out_f = lax.dynamic_update_index_in_dim(out_f, piece_f, (coord - step - 1) % size, 0)
        out_b = lax.dynamic_update_index_in_dim(out_b, piece_b, (coord + step + 1) % size, 0)
    return jnp.concatenate([out_f.reshape(size * rows, -1), out_b.reshape(size * rows, -1)], axis=0)


def scan_all_reduce(value, early_inputs, early_work, tied):
    shape = value.shape
    data = value.reshape(-1, shape[-1])
    data = pair_reduce_scatter(data, CORE)
    data = direct_reduce_scatter(data, XAX)
    data, early_inputs = lax.optimization_barrier((data, early_inputs))
    early = early_work(*early_inputs)
    data = direct_reduce_scatter(data, YAX)
    data = pair_reduce_scatter(data, ZLO)
    data, early, tied = lax.optimization_barrier((data, early, tied))
    data = pair_all_gather(data, ZLO)
    data = direct_all_gather(data, YAX)
    data = direct_all_gather(data, XAX)
    data = pair_all_gather(data, CORE)
    return data.reshape(shape), early, tied


def dft_tables(length_side, direction_sign):
    index_row = jnp.arange(length_side, dtype=jnp.int32)
    product = index_row[:, None] * index_row[None, :] % length_side
    angles = product.astype(jnp.float32) * (2.0 * math.pi / length_side)
    scale_factor = 1.0 / math.sqrt(length_side)
    real_part = jnp.cos(angles) * scale_factor
    imag_part = direction_sign * jnp.sin(angles) * scale_factor
    matrix_table = jnp.stack(
        [jnp.stack([real_part, -imag_part]), jnp.stack([imag_part, real_part])]
    )
    return matrix_table.astype(jnp.bfloat16)


def transform(field, matrix_table):
    first_section = jnp.einsum(
        "dcpq,bcqk->bdpk", matrix_table, field, preferred_element_type=jnp.float32
    ).astype(jnp.bfloat16)
    return jnp.einsum(
        "bcpq,dcqk->bdpk", first_section, matrix_table, preferred_element_type=jnp.float32
    )


def complex_table(matrix_table, transposed):
    if transposed:
        rows = [jnp.concatenate([matrix_table[0, c], matrix_table[1, c]], axis=1) for c in range(2)]
    else:
        rows = [jnp.concatenate([matrix_table[d, 0], matrix_table[d, 1]], axis=1) for d in range(2)]
    return jnp.concatenate(rows, axis=0)


def forward_kernel(patch_ref, probe_ref, amp_ref, left_ref, right_ref, out_ref, far_ref):
    side = patch_ref.shape[-1]
    modes = probe_ref.shape[0]
    obj_real = patch_ref[0, 0]
    obj_imag = patch_ref[0, 1]

    def one_mode(mode, intensity):
        probe_real = probe_ref[mode, 0]
        probe_imag = probe_ref[mode, 1]
        exit_real = (obj_real * probe_real - obj_imag * probe_imag).astype(jnp.bfloat16)
        exit_imag = (obj_real * probe_imag + obj_imag * probe_real).astype(jnp.bfloat16)
        stacked = jnp.concatenate([exit_real, exit_imag], axis=0)
        half = jnp.dot(left_ref[...], stacked, preferred_element_type=jnp.float32).astype(jnp.bfloat16)
        wide = jnp.concatenate([half[:side], half[side:]], axis=1)
        far = jnp.dot(wide, right_ref[...], preferred_element_type=jnp.float32)
        far_ref[mode] = far
        return intensity + far[:, :side] * far[:, :side] + far[:, side:] * far[:, side:]

    intensity = lax.fori_loop(0, modes, one_mode, jnp.zeros((side, side), jnp.float32))
    ratio = amp_ref[0] / jnp.maximum(jnp.sqrt(intensity), amp_floor) - 1.0

    def store(mode, carry):
        far = far_ref[mode]
        out_ref[0, mode, 0] = (far[:, :side] * ratio).astype(jnp.bfloat16)
        out_ref[0, mode, 1] = (far[:, side:] * ratio).astype(jnp.bfloat16)
        return carry

    lax.fori_loop(0, modes, store, 0)


def forward_correction(patch, all_modes, amplitudes, forward_table):
    slots, _, side, _ = patch.shape
    modes = all_modes.shape[0]
    left = complex_table(forward_table, False)
    right = complex_table(forward_table, True)
    return pl.pallas_call(
        forward_kernel,
        grid=(slots,),
        in_specs=[
            pl.BlockSpec((1, 2, side, side), lambda s: (s, 0, 0, 0)),
            pl.BlockSpec((modes, 2, side, side), lambda s: (0, 0, 0, 0), pipeline_mode=pl.Buffered(1)),
            pl.BlockSpec((1, side, side), lambda s: (s, 0, 0)),
            pl.BlockSpec((2 * side, 2 * side), lambda s: (0, 0), pipeline_mode=pl.Buffered(1)),
            pl.BlockSpec((2 * side, 2 * side), lambda s: (0, 0), pipeline_mode=pl.Buffered(1)),
        ],
        out_specs=pl.BlockSpec((1, modes, 2, side, side), lambda s: (s, 0, 0, 0, 0)),
        out_shape=jax.ShapeDtypeStruct((slots, modes, 2, side, side), jnp.bfloat16),
        scratch_shapes=[pltpu.VMEM((modes, side, 2 * side), jnp.float32)],
        compiler_params=pltpu.CompilerParams(vmem_limit_bytes=64 * 1024 * 1024),
        cost_estimate=pl.CostEstimate(
            flops=slots * modes * 4 * (2 * side) ** 2 * side,
            bytes_accessed=slots * (modes + 3) * 2 * side * side * 4,
            transcendentals=slots * side * side,
        ),
    )(patch, all_modes, amplitudes, left, right)


def backward_kernel(block_ref, count_ref, corr_ref, probe_ref, patch_ref, left_ref, right_ref, grad_ref, *part):
    side = patch_ref.shape[-1]
    modes = probe_ref.shape[0]
    slot = pl.program_id(0)
    if part:
        part_ref = part[0]

        @pl.when(slot == 0)
        def _():
            part_ref[...] = jnp.zeros(part_ref.shape, part_ref.dtype)

    live = (slot < count_ref[0]).astype(jnp.float32)
    obj_real = patch_ref[0, 0]
    obj_imag = patch_ref[0, 1]

    def one_mode(mode, carry):
        grad_real, grad_imag = carry
        stacked = jnp.concatenate([corr_ref[0, mode, 0], corr_ref[0, mode, 1]], axis=0)
        half = jnp.dot(left_ref[...], stacked, preferred_element_type=jnp.float32).astype(jnp.bfloat16)
        wide = jnp.concatenate([half[:side], half[side:]], axis=1)
        back = jnp.dot(wide, right_ref[...], preferred_element_type=jnp.float32) * live
        back_real = back[:, :side]
        back_imag = back[:, side:]
        probe_real = probe_ref[mode, 0]
        probe_imag = probe_ref[mode, 1]
        if part:
            part_ref[mode, 0] += obj_real * back_real + obj_imag * back_imag
            part_ref[mode, 1] += obj_real * back_imag - obj_imag * back_real

        grad_real = grad_real + (probe_real * back_real + probe_imag * back_imag)
        grad_imag = grad_imag + (probe_real * back_imag - probe_imag * back_real)
        return grad_real, grad_imag

    zeros = jnp.zeros((side, side), jnp.float32)
    grad_real, grad_imag = lax.fori_loop(0, modes, one_mode, (zeros, zeros))
    grad_ref[0, 0] = grad_real
    grad_ref[0, 1] = grad_imag


def backward_gradients(correction, all_modes, patch, block, count, block_modes, inverse_table, with_partial):
    slots, modes, _, side, _ = correction.shape
    left = complex_table(inverse_table, False)
    right = complex_table(inverse_table, True)
    out_specs = [pl.BlockSpec((1, 2, side, side), lambda s, b, n: (s, 0, 0, 0))]
    out_shape = [jax.ShapeDtypeStruct((slots, 2, side, side), jnp.float32)]
    if with_partial:
        out_specs.append(pl.BlockSpec((block_modes, 2, side, side), lambda s, b, n: (0, 0, 0, 0)))
        out_shape.append(jax.ShapeDtypeStruct((block_modes, 2, side, side), jnp.float32))
    grid_spec = pltpu.PrefetchScalarGridSpec(
        num_scalar_prefetch=2,
        grid=(slots,),
        in_specs=[
            pl.BlockSpec((1, block_modes, 2, side, side), lambda s, b, n: (s, b[0], 0, 0, 0)),
            pl.BlockSpec((block_modes, 2, side, side), lambda s, b, n: (b[0], 0, 0, 0), pipeline_mode=pl.Buffered(1)),
            pl.BlockSpec((1, 2, side, side), lambda s, b, n: (s, 0, 0, 0)),
            pl.BlockSpec((2 * side, 2 * side), lambda s, b, n: (0, 0), pipeline_mode=pl.Buffered(1)),
            pl.BlockSpec((2 * side, 2 * side), lambda s, b, n: (0, 0), pipeline_mode=pl.Buffered(1)),
        ],
        out_specs=out_specs,
    )
    return pl.pallas_call(
        backward_kernel,
        grid_spec=grid_spec,
        out_shape=out_shape,
        compiler_params=pltpu.CompilerParams(
            vmem_limit_bytes=64 * 1024 * 1024, dimension_semantics=("arbitrary",)
        ),
        cost_estimate=pl.CostEstimate(
            flops=slots * block_modes * 4 * (2 * side) ** 2 * side,
            bytes_accessed=slots * (block_modes + 4) * 2 * side * side * 4,
            transcendentals=0,
        ),
    )(
        jnp.reshape(block, (1,)).astype(jnp.int32),
        jnp.reshape(count, (1,)).astype(jnp.int32),
        correction,
        all_modes,
        patch,
        left,
        right,
    )


def shards(object_tiles, probe_modes, amplitudes, offsets, counts):
    side = probe_modes.shape[-1]
    tile_side = object_tiles.shape[-1]
    slots = offsets.shape[1]
    own_modes = probe_modes.shape[0]
    count = lax.axis_size("scan")
    core = lax.axis_index("scan") % 2
    sent = lax.dynamic_index_in_dim(probe_modes, core, 0, keepdims=False)
    pairs = [(s * 2 + m, (s ^ 2) * 2 + 1 - m) for s in range(count) for m in range(2)]
    got = lax.ppermute(sent, ("scan", "mode"), pairs)
    other = lax.dynamic_index_in_dim(probe_modes, 1 - core, 0, keepdims=False)
    mate = lax.ppermute(other, "mode", [(0, 1), (1, 0)])
    partner_modes = jnp.stack([jnp.where(core == 0, got, mate), jnp.where(core == 0, mate, got)])
    component = lax.axis_index("mode")
    all_modes = jnp.where(
        component == 0,
        jnp.concatenate([probe_modes, partner_modes], axis=0),
        jnp.concatenate([partner_modes, probe_modes], axis=0),
    )
    modes_here = all_modes.shape[0]
    own_tile = object_tiles[0]
    east_tile = from_behind(own_tile, "scan", -1)
    south_tile = from_behind(own_tile, "scan", -GCOLS)
    far_corner = lax.ppermute(
        own_tile, "scan", [(s, s - GCOLS - 1) for s in range(count) if (s - GCOLS - 1) % 2 == 1 and s >= GCOLS + 1]
        + [(s, s - GCOLS - 1 + count) for s in range(count) if (s - GCOLS - 1) % 2 == 1 and s < GCOLS + 1]
    )
    near_corner = lax.ppermute(south_tile, "scan", [(s, s - 1) for s in range(count) if s % 2 == 1])
    corner_tile = jnp.where(lax.axis_index("scan") % 2 == 0, near_corner, far_corner)
    upper_band = jnp.concatenate([own_tile, east_tile], axis=2)
    lower_band = jnp.concatenate([south_tile, corner_tile], axis=2)
    extended = jnp.concatenate([upper_band, lower_band], axis=1)
    slot_offsets = offsets[0]
    windows = jnp.stack(
        [
            lax.dynamic_slice(
                extended,
                (0, slot_offsets[slot_id, 0] - 1, slot_offsets[slot_id, 1] - 1),
                (2, side + 2, side + 2),
            )
            for slot_id in range(slots)
        ]
    )
    patch = windows[:, :, 1:-1, 1:-1]
    grad_y = (windows[:, :, 2:, 1:-1] - windows[:, :, :-2, 1:-1]) * 0.5
    grad_x = (windows[:, :, 1:-1, 2:] - windows[:, :, 1:-1, :-2]) * 0.5
    obj_real = patch[:, 0][:, None]
    obj_imag = patch[:, 1][:, None]
    probe_real = all_modes[:, 0][None]
    probe_imag = all_modes[:, 1][None]
    forward_table = dft_tables(side, -1.0)
    inverse_table = dft_tables(side, 1.0)
    correction = forward_correction(patch, all_modes, amplitudes[0], forward_table)
    own_grad, probe_partial = backward_gradients(
        correction, all_modes, patch, component, counts[0], own_modes, inverse_table, True
    )
    (partner_grad,) = backward_gradients(
        correction, all_modes, patch, 1 - component, counts[0], own_modes, inverse_table, False
    )
    whole_grad = own_grad + partner_grad
    def position_work(whole_grad, grad_y, grad_x):
        position_y = jnp.sum(whole_grad * grad_y, axis=(1, 2, 3))
        position_x = jnp.sum(whole_grad * grad_x, axis=(1, 2, 3))
        return jnp.stack([position_y, position_x], axis=1) / side

    mine = lax.dynamic_slice_in_dim(whole_grad, component, 1, axis=1)
    gradient_plane = jnp.zeros((2 * tile_side, 2 * tile_side), jnp.float32)
    for slot_id in range(slots):
        start = (slot_offsets[slot_id, 0], slot_offsets[slot_id, 1])
        current = lax.dynamic_slice(gradient_plane, start, (side, side))
        gradient_plane = lax.dynamic_update_slice(gradient_plane, current + mine[slot_id, 0], start)
    received_east = from_behind(gradient_plane[:tile_side, tile_side:], "scan", 1)
    received_south = from_behind(gradient_plane[tile_side:, :tile_side], "scan", GCOLS)
    received_corner = from_behind(gradient_plane[tile_side:, tile_side:], "scan", GCOLS + 1)
    probe_grad, positions, (received_east, received_south, received_corner) = scan_all_reduce(
        probe_partial, (whole_grad, grad_y, grad_x), position_work, (received_east, received_south, received_corner)
    )
    total_grad = (
        gradient_plane[:tile_side, :tile_side] + received_east + received_south + received_corner
    )
    return (total_grad[None, None], probe_grad, positions[None])


def solution(mesh):
    return jax.shard_map(
        shards,
        mesh=mesh,
        in_specs=(
            P("scan", None, None, None),
            P("mode", None, None, None),
            P("scan", None, None, None),
            P("scan", None, None),
            P("scan"),
        ),
        out_specs=(
            P("scan", "mode", None, None),
            P("mode", None, None, None),
            P("scan", None, None),
        ),
        check_vma=False,
    )
```

```python
import math

import jax
import jax.numpy as jnp
from jax import lax
from jax.experimental import pallas as pl
from jax.experimental.pallas import tpu as pltpu
from jax.sharding import PartitionSpec as P

GCOLS = 8
CORE = (1, 2)
ZLO = (2, 2)
YAX = (4, 4)
XAX = (16, 4)


amp_floor = 1.0


def from_behind(value, axis, steps):
    count = lax.axis_size(axis)
    pairs = [(source, (source + steps) % count) for source in range(count)]
    return lax.ppermute(value, axis, pairs)


def sub_shift(value, sub, shift):
    stride, size = sub
    count = lax.axis_size("scan")
    pairs = []
    for source in range(count):
        coord = (source // stride) % size
        pairs.append((source, source + (((coord + shift) % size) - coord) * stride))
    return lax.ppermute(value, "scan", pairs)


def sub_coord(sub):
    stride, size = sub
    return (lax.axis_index("scan") // stride) % size


def pair_reduce_scatter(data, sub):
    coord = sub_coord(sub)
    half = data.shape[0] // 2
    mine = lax.dynamic_slice_in_dim(data, coord * half, half, axis=0)
    other = lax.dynamic_slice_in_dim(data, (1 - coord) * half, half, axis=0)
    return mine + sub_shift(other, sub, 1)


def pair_all_gather(data, sub):
    coord = sub_coord(sub)
    got = sub_shift(data, sub, 1)
    first = jnp.where(coord == 0, data, got)
    second = jnp.where(coord == 0, got, data)
    return jnp.concatenate([first, second], axis=0)


def direct_reduce_scatter(data, sub):
    size = sub[1]
    coord = sub_coord(sub)
    chunks = data.reshape(size, data.shape[0] // size, -1)
    total = chunks[coord]
    for shift in range(1, size):
        total = total + sub_shift(chunks[(coord + shift) % size], sub, shift)
    return total


def direct_all_gather(data, sub):
    size = sub[1]
    coord = sub_coord(sub)
    out = jnp.zeros((size,) + data.shape, data.dtype)
    out = lax.dynamic_update_index_in_dim(out, data, coord, 0)
    for shift in range(1, size):
        got = sub_shift(data, sub, shift)
        out = lax.dynamic_update_index_in_dim(out, got, (coord - shift) % size, 0)
    return out.reshape(size * data.shape[0], -1)


def ring_reduce_scatter(data, sub):
    size = sub[1]
    coord = sub_coord(sub)
    rows = data.shape[0] // (2 * size)
    fwd = data[: rows * size].reshape(size, rows, -1)
    bwd = data[rows * size :].reshape(size, rows, -1)
    part_f = fwd[(coord - 1) % size]
    part_b = bwd[(coord + 1) % size]
    for step in range(size - 1):
        got_f = sub_shift(part_f, sub, 1)
        got_b = sub_shift(part_b, sub, -1)
        part_f = got_f + fwd[(coord - step - 2) % size]
        part_b = got_b + bwd[(coord + step + 2) % size]
    return jnp.concatenate([part_f, part_b], axis=0)


def ring_all_gather(data, sub):
    size = sub[1]
    coord = sub_coord(sub)
    rows = data.shape[0] // 2
    piece_f = data[:rows]
    piece_b = data[rows:]
    out_f = jnp.zeros((size, rows, data.shape[1]), data.dtype)
    out_b = jnp.zeros((size, rows, data.shape[1]), data.dtype)
    out_f = lax.dynamic_update_index_in_dim(out_f, piece_f, coord, 0)
    out_b = lax.dynamic_update_index_in_dim(out_b, piece_b, coord, 0)
    for step in range(size - 1):
        piece_f = sub_shift(piece_f, sub, 1)
        piece_b = sub_shift(piece_b, sub, -1)
        out_f = lax.dynamic_update_index_in_dim(out_f, piece_f, (coord - step - 1) % size, 0)
        out_b = lax.dynamic_update_index_in_dim(out_b, piece_b, (coord + step + 1) % size, 0)
    return jnp.concatenate([out_f.reshape(size * rows, -1), out_b.reshape(size * rows, -1)], axis=0)


def scan_all_reduce(value, early, tied):
    shape = value.shape
    data = value.reshape(-1, shape[-1])
    data = pair_reduce_scatter(data, CORE)
    data = ring_reduce_scatter(data, XAX)
    data = direct_reduce_scatter(data, YAX)
    data = pair_reduce_scatter(data, ZLO)
    data, early, tied = lax.optimization_barrier((data, early, tied))
    data = pair_all_gather(data, ZLO)
    data = direct_all_gather(data, YAX)
    data = ring_all_gather(data, XAX)
    data = pair_all_gather(data, CORE)
    return data.reshape(shape), early, tied


def dft_tables(length_side, direction_sign):
    index_row = jnp.arange(length_side, dtype=jnp.int32)
    product = index_row[:, None] * index_row[None, :] % length_side
    angles = product.astype(jnp.float32) * (2.0 * math.pi / length_side)
    scale_factor = 1.0 / math.sqrt(length_side)
    real_part = jnp.cos(angles) * scale_factor
    imag_part = direction_sign * jnp.sin(angles) * scale_factor
    matrix_table = jnp.stack(
        [jnp.stack([real_part, -imag_part]), jnp.stack([imag_part, real_part])]
    )
    return matrix_table.astype(jnp.bfloat16)


def transform(field, matrix_table):
    first_section = jnp.einsum(
        "dcpq,bcqk->bdpk", matrix_table, field, preferred_element_type=jnp.float32
    ).astype(jnp.bfloat16)
    return jnp.einsum(
        "bcpq,dcqk->bdpk", first_section, matrix_table, preferred_element_type=jnp.float32
    )


def complex_table(matrix_table, transposed):
    if transposed:
        rows = [jnp.concatenate([matrix_table[0, c], matrix_table[1, c]], axis=1) for c in range(2)]
    else:
        rows = [jnp.concatenate([matrix_table[d, 0], matrix_table[d, 1]], axis=1) for d in range(2)]
    return jnp.concatenate(rows, axis=0)


def forward_kernel(patch_ref, probe_ref, amp_ref, left_ref, right_ref, out_ref, far_ref):
    side = patch_ref.shape[-1]
    modes = probe_ref.shape[0]
    obj_real = patch_ref[0, 0]
    obj_imag = patch_ref[0, 1]

    def one_mode(mode, intensity):
        probe_real = probe_ref[mode, 0]
        probe_imag = probe_ref[mode, 1]
        exit_real = (obj_real * probe_real - obj_imag * probe_imag).astype(jnp.bfloat16)
        exit_imag = (obj_real * probe_imag + obj_imag * probe_real).astype(jnp.bfloat16)
        stacked = jnp.concatenate([exit_real, exit_imag], axis=0)
        half = jnp.dot(left_ref[...], stacked, preferred_element_type=jnp.float32).astype(jnp.bfloat16)
        wide = jnp.concatenate([half[:side], half[side:]], axis=1)
        far = jnp.dot(wide, right_ref[...], preferred_element_type=jnp.float32)
        far_ref[mode] = far
        return intensity + far[:, :side] * far[:, :side] + far[:, side:] * far[:, side:]

    intensity = lax.fori_loop(0, modes, one_mode, jnp.zeros((side, side), jnp.float32))
    ratio = amp_ref[0] / jnp.maximum(jnp.sqrt(intensity), amp_floor) - 1.0

    def store(mode, carry):
        far = far_ref[mode]
        out_ref[0, mode, 0] = (far[:, :side] * ratio).astype(jnp.bfloat16)
        out_ref[0, mode, 1] = (far[:, side:] * ratio).astype(jnp.bfloat16)
        return carry

    lax.fori_loop(0, modes, store, 0)


def forward_correction(patch, all_modes, amplitudes, forward_table):
    slots, _, side, _ = patch.shape
    modes = all_modes.shape[0]
    left = complex_table(forward_table, False)
    right = complex_table(forward_table, True)
    return pl.pallas_call(
        forward_kernel,
        grid=(slots,),
        in_specs=[
            pl.BlockSpec((1, 2, side, side), lambda s: (s, 0, 0, 0)),
            pl.BlockSpec((modes, 2, side, side), lambda s: (0, 0, 0, 0), pipeline_mode=pl.Buffered(1)),
            pl.BlockSpec((1, side, side), lambda s: (s, 0, 0)),
            pl.BlockSpec((2 * side, 2 * side), lambda s: (0, 0), pipeline_mode=pl.Buffered(1)),
            pl.BlockSpec((2 * side, 2 * side), lambda s: (0, 0), pipeline_mode=pl.Buffered(1)),
        ],
        out_specs=pl.BlockSpec((1, modes, 2, side, side), lambda s: (s, 0, 0, 0, 0)),
        out_shape=jax.ShapeDtypeStruct((slots, modes, 2, side, side), jnp.bfloat16),
        scratch_shapes=[pltpu.VMEM((modes, side, 2 * side), jnp.float32)],
        compiler_params=pltpu.CompilerParams(vmem_limit_bytes=64 * 1024 * 1024),
        cost_estimate=pl.CostEstimate(
            flops=slots * modes * 4 * (2 * side) ** 2 * side,
            bytes_accessed=slots * (modes + 3) * 2 * side * side * 4,
            transcendentals=slots * side * side,
        ),
    )(patch, all_modes, amplitudes, left, right)


def backward_kernel(block_ref, count_ref, corr_ref, probe_ref, patch_ref, left_ref, right_ref, grad_ref, *part):
    side = patch_ref.shape[-1]
    modes = probe_ref.shape[0]
    slot = pl.program_id(0)
    if part:
        part_ref = part[0]

        @pl.when(slot == 0)
        def _():
            part_ref[...] = jnp.zeros(part_ref.shape, part_ref.dtype)

    live = (slot < count_ref[0]).astype(jnp.float32)
    obj_real = patch_ref[0, 0]
    obj_imag = patch_ref[0, 1]

    def one_mode(mode, carry):
        grad_real, grad_imag = carry
        stacked = jnp.concatenate([corr_ref[0, mode, 0], corr_ref[0, mode, 1]], axis=0)
        half = jnp.dot(left_ref[...], stacked, preferred_element_type=jnp.float32).astype(jnp.bfloat16)
        wide = jnp.concatenate([half[:side], half[side:]], axis=1)
        back = jnp.dot(wide, right_ref[...], preferred_element_type=jnp.float32) * live
        back_real = back[:, :side]
        back_imag = back[:, side:]
        probe_real = probe_ref[mode, 0]
        probe_imag = probe_ref[mode, 1]
        if part:
            part_ref[mode, 0] += obj_real * back_real + obj_imag * back_imag
            part_ref[mode, 1] += obj_real * back_imag - obj_imag * back_real

        grad_real = grad_real + (probe_real * back_real + probe_imag * back_imag)
        grad_imag = grad_imag + (probe_real * back_imag - probe_imag * back_real)
        return grad_real, grad_imag

    zeros = jnp.zeros((side, side), jnp.float32)
    grad_real, grad_imag = lax.fori_loop(0, modes, one_mode, (zeros, zeros))
    grad_ref[0, 0] = grad_real
    grad_ref[0, 1] = grad_imag


def backward_gradients(correction, all_modes, patch, block, count, block_modes, inverse_table, with_partial):
    slots, modes, _, side, _ = correction.shape
    left = complex_table(inverse_table, False)
    right = complex_table(inverse_table, True)
    out_specs = [pl.BlockSpec((1, 2, side, side), lambda s, b, n: (s, 0, 0, 0))]
    out_shape = [jax.ShapeDtypeStruct((slots, 2, side, side), jnp.float32)]
    if with_partial:
        out_specs.append(pl.BlockSpec((block_modes, 2, side, side), lambda s, b, n: (0, 0, 0, 0)))
        out_shape.append(jax.ShapeDtypeStruct((block_modes, 2, side, side), jnp.float32))
    grid_spec = pltpu.PrefetchScalarGridSpec(
        num_scalar_prefetch=2,
        grid=(slots,),
        in_specs=[
            pl.BlockSpec((1, block_modes, 2, side, side), lambda s, b, n: (s, b[0], 0, 0, 0)),
            pl.BlockSpec((block_modes, 2, side, side), lambda s, b, n: (b[0], 0, 0, 0), pipeline_mode=pl.Buffered(1)),
            pl.BlockSpec((1, 2, side, side), lambda s, b, n: (s, 0, 0, 0)),
            pl.BlockSpec((2 * side, 2 * side), lambda s, b, n: (0, 0), pipeline_mode=pl.Buffered(1)),
            pl.BlockSpec((2 * side, 2 * side), lambda s, b, n: (0, 0), pipeline_mode=pl.Buffered(1)),
        ],
        out_specs=out_specs,
    )
    return pl.pallas_call(
        backward_kernel,
        grid_spec=grid_spec,
        out_shape=out_shape,
        compiler_params=pltpu.CompilerParams(
            vmem_limit_bytes=64 * 1024 * 1024, dimension_semantics=("arbitrary",)
        ),
        cost_estimate=pl.CostEstimate(
            flops=slots * block_modes * 4 * (2 * side) ** 2 * side,
            bytes_accessed=slots * (block_modes + 4) * 2 * side * side * 4,
            transcendentals=0,
        ),
    )(
        jnp.reshape(block, (1,)).astype(jnp.int32),
        jnp.reshape(count, (1,)).astype(jnp.int32),
        correction,
        all_modes,
        patch,
        left,
        right,
    )


def shards(object_tiles, probe_modes, amplitudes, offsets, counts):
    side = probe_modes.shape[-1]
    tile_side = object_tiles.shape[-1]
    slots = offsets.shape[1]
    own_modes = probe_modes.shape[0]
    count = lax.axis_size("scan")
    core = lax.axis_index("scan") % 2
    sent = lax.dynamic_index_in_dim(probe_modes, core, 0, keepdims=False)
    pairs = [(s * 2 + m, (s ^ 2) * 2 + 1 - m) for s in range(count) for m in range(2)]
    got = lax.ppermute(sent, ("scan", "mode"), pairs)
    other = lax.dynamic_index_in_dim(probe_modes, 1 - core, 0, keepdims=False)
    mate = lax.ppermute(other, "mode", [(0, 1), (1, 0)])
    partner_modes = jnp.stack([jnp.where(core == 0, got, mate), jnp.where(core == 0, mate, got)])
    component = lax.axis_index("mode")
    all_modes = jnp.where(
        component == 0,
        jnp.concatenate([probe_modes, partner_modes], axis=0),
        jnp.concatenate([partner_modes, probe_modes], axis=0),
    )
    modes_here = all_modes.shape[0]
    own_tile = object_tiles[0]
    east_tile = from_behind(own_tile, "scan", -1)
    south_tile = from_behind(own_tile, "scan", -GCOLS)
    far_corner = lax.ppermute(
        own_tile, "scan", [(s, s - GCOLS - 1) for s in range(count) if (s - GCOLS - 1) % 2 == 1 and s >= GCOLS + 1]
        + [(s, s - GCOLS - 1 + count) for s in range(count) if (s - GCOLS - 1) % 2 == 1 and s < GCOLS + 1]
    )
    near_corner = lax.ppermute(south_tile, "scan", [(s, s - 1) for s in range(count) if s % 2 == 1])
    corner_tile = jnp.where(lax.axis_index("scan") % 2 == 0, near_corner, far_corner)
    upper_band = jnp.concatenate([own_tile, east_tile], axis=2)
    lower_band = jnp.concatenate([south_tile, corner_tile], axis=2)
    extended = jnp.concatenate([upper_band, lower_band], axis=1)
    slot_offsets = offsets[0]
    windows = jnp.stack(
        [
            lax.dynamic_slice(
                extended,
                (0, slot_offsets[slot_id, 0] - 1, slot_offsets[slot_id, 1] - 1),
                (2, side + 2, side + 2),
            )
            for slot_id in range(slots)
        ]
    )
    patch = windows[:, :, 1:-1, 1:-1]
    grad_y = (windows[:, :, 2:, 1:-1] - windows[:, :, :-2, 1:-1]) * 0.5
    grad_x = (windows[:, :, 1:-1, 2:] - windows[:, :, 1:-1, :-2]) * 0.5
    obj_real = patch[:, 0][:, None]
    obj_imag = patch[:, 1][:, None]
    probe_real = all_modes[:, 0][None]
    probe_imag = all_modes[:, 1][None]
    forward_table = dft_tables(side, -1.0)
    inverse_table = dft_tables(side, 1.0)
    correction = forward_correction(patch, all_modes, amplitudes[0], forward_table)
    own_grad, probe_partial = backward_gradients(
        correction, all_modes, patch, component, counts[0], own_modes, inverse_table, True
    )
    (partner_grad,) = backward_gradients(
        correction, all_modes, patch, 1 - component, counts[0], own_modes, inverse_table, False
    )
    whole_grad = own_grad + partner_grad
    position_y = jnp.sum(whole_grad * grad_y, axis=(1, 2, 3))
    position_x = jnp.sum(whole_grad * grad_x, axis=(1, 2, 3))
    positions = jnp.stack([position_y, position_x], axis=1) / side
    mine = lax.dynamic_slice_in_dim(whole_grad, component, 1, axis=1)
    gradient_plane = jnp.zeros((2 * tile_side, 2 * tile_side), jnp.float32)
    for slot_id in range(slots):
        start = (slot_offsets[slot_id, 0], slot_offsets[slot_id, 1])
        current = lax.dynamic_slice(gradient_plane, start, (side, side))
        gradient_plane = lax.dynamic_update_slice(gradient_plane, current + mine[slot_id, 0], start)
    received_east = from_behind(gradient_plane[:tile_side, tile_side:], "scan", 1)
    received_south = from_behind(gradient_plane[tile_side:, :tile_side], "scan", GCOLS)
    received_corner = from_behind(gradient_plane[tile_side:, tile_side:], "scan", GCOLS + 1)
    probe_grad, positions, (received_east, received_south, received_corner) = scan_all_reduce(
        probe_partial, positions, (received_east, received_south, received_corner)
    )
    total_grad = (
        gradient_plane[:tile_side, :tile_side] + received_east + received_south + received_corner
    )
    return (total_grad[None, None], probe_grad, positions[None])


def solution(mesh):
    return jax.shard_map(
        shards,
        mesh=mesh,
        in_specs=(
            P("scan", None, None, None),
            P("mode", None, None, None),
            P("scan", None, None, None),
            P("scan", None, None),
            P("scan"),
        ),
        out_specs=(
            P("scan", "mode", None, None),
            P("mode", None, None, None),
            P("scan", None, None),
        ),
        check_vma=False,
    )
```

```python
import math

import jax
import jax.numpy as jnp
from jax import lax
from jax.experimental import pallas as pl
from jax.experimental.pallas import tpu as pltpu
from jax.sharding import PartitionSpec as P

GCOLS = 8
CORE = (1, 2)
ZLO = (2, 2)
YAX = (4, 4)
XAX = (16, 4)


amp_floor = 1.0


def from_behind(value, axis, steps):
    count = lax.axis_size(axis)
    pairs = [(source, (source + steps) % count) for source in range(count)]
    return lax.ppermute(value, axis, pairs)


def sub_shift(value, sub, shift):
    stride, size = sub
    count = lax.axis_size("scan")
    pairs = []
    for source in range(count):
        coord = (source // stride) % size
        pairs.append((source, source + (((coord + shift) % size) - coord) * stride))
    return lax.ppermute(value, "scan", pairs)


def sub_coord(sub):
    stride, size = sub
    return (lax.axis_index("scan") // stride) % size


def pair_reduce_scatter(data, sub):
    coord = sub_coord(sub)
    half = data.shape[0] // 2
    mine = lax.dynamic_slice_in_dim(data, coord * half, half, axis=0)
    other = lax.dynamic_slice_in_dim(data, (1 - coord) * half, half, axis=0)
    return mine + sub_shift(other, sub, 1)


def pair_all_gather(data, sub):
    coord = sub_coord(sub)
    got = sub_shift(data, sub, 1)
    first = jnp.where(coord == 0, data, got)
    second = jnp.where(coord == 0, got, data)
    return jnp.concatenate([first, second], axis=0)


def direct_reduce_scatter(data, sub):
    size = sub[1]
    coord = sub_coord(sub)
    chunks = data.reshape(size, data.shape[0] // size, -1)
    total = chunks[coord]
    for shift in range(1, size):
        total = total + sub_shift(chunks[(coord + shift) % size], sub, shift)
    return total


def direct_all_gather(data, sub):
    size = sub[1]
    coord = sub_coord(sub)
    out = jnp.zeros((size,) + data.shape, data.dtype)
    out = lax.dynamic_update_index_in_dim(out, data, coord, 0)
    for shift in range(1, size):
        got = sub_shift(data, sub, shift)
        out = lax.dynamic_update_index_in_dim(out, got, (coord - shift) % size, 0)
    return out.reshape(size * data.shape[0], -1)


def ring_reduce_scatter(data, sub):
    size = sub[1]
    coord = sub_coord(sub)
    rows = data.shape[0] // (2 * size)
    fwd = data[: rows * size].reshape(size, rows, -1)
    bwd = data[rows * size :].reshape(size, rows, -1)
    part_f = fwd[(coord - 1) % size]
    part_b = bwd[(coord + 1) % size]
    for step in range(size - 1):
        got_f = sub_shift(part_f, sub, 1)
        got_b = sub_shift(part_b, sub, -1)
        part_f = got_f + fwd[(coord - step - 2) % size]
        part_b = got_b + bwd[(coord + step + 2) % size]
    return jnp.concatenate([part_f, part_b], axis=0)


def ring_all_gather(data, sub):
    size = sub[1]
    coord = sub_coord(sub)
    rows = data.shape[0] // 2
    piece_f = data[:rows]
    piece_b = data[rows:]
    out_f = jnp.zeros((size, rows, data.shape[1]), data.dtype)
    out_b = jnp.zeros((size, rows, data.shape[1]), data.dtype)
    out_f = lax.dynamic_update_index_in_dim(out_f, piece_f, coord, 0)
    out_b = lax.dynamic_update_index_in_dim(out_b, piece_b, coord, 0)
    for step in range(size - 1):
        piece_f = sub_shift(piece_f, sub, 1)
        piece_b = sub_shift(piece_b, sub, -1)
        out_f = lax.dynamic_update_index_in_dim(out_f, piece_f, (coord - step - 1) % size, 0)
        out_b = lax.dynamic_update_index_in_dim(out_b, piece_b, (coord + step + 1) % size, 0)
    return jnp.concatenate([out_f.reshape(size * rows, -1), out_b.reshape(size * rows, -1)], axis=0)


def scan_all_reduce(value, early, tied):
    shape = value.shape
    data = value.reshape(-1, shape[-1])
    data = pair_reduce_scatter(data, CORE)
    data = direct_reduce_scatter(data, XAX)
    data = direct_reduce_scatter(data, YAX)
    data = data + sub_shift(data, ZLO, 1)
    data, early, tied = lax.optimization_barrier((data, early, tied))
    data = direct_all_gather(data, YAX)
    data = direct_all_gather(data, XAX)
    data = pair_all_gather(data, CORE)
    return data.reshape(shape), early, tied


def dft_tables(length_side, direction_sign):
    index_row = jnp.arange(length_side, dtype=jnp.int32)
    product = index_row[:, None] * index_row[None, :] % length_side
    angles = product.astype(jnp.float32) * (2.0 * math.pi / length_side)
    scale_factor = 1.0 / math.sqrt(length_side)
    real_part = jnp.cos(angles) * scale_factor
    imag_part = direction_sign * jnp.sin(angles) * scale_factor
    matrix_table = jnp.stack(
        [jnp.stack([real_part, -imag_part]), jnp.stack([imag_part, real_part])]
    )
    return matrix_table.astype(jnp.bfloat16)


def transform(field, matrix_table):
    first_section = jnp.einsum(
        "dcpq,bcqk->bdpk", matrix_table, field, preferred_element_type=jnp.float32
    ).astype(jnp.bfloat16)
    return jnp.einsum(
        "bcpq,dcqk->bdpk", first_section, matrix_table, preferred_element_type=jnp.float32
    )


def complex_table(matrix_table, transposed):
    if transposed:
        rows = [jnp.concatenate([matrix_table[0, c], matrix_table[1, c]], axis=1) for c in range(2)]
    else:
        rows = [jnp.concatenate([matrix_table[d, 0], matrix_table[d, 1]], axis=1) for d in range(2)]
    return jnp.concatenate(rows, axis=0)


def forward_kernel(patch_ref, probe_ref, amp_ref, left_ref, right_ref, out_ref, far_ref):
    side = patch_ref.shape[-1]
    modes = probe_ref.shape[0]
    obj_real = patch_ref[0, 0]
    obj_imag = patch_ref[0, 1]

    def one_mode(mode, intensity):
        probe_real = probe_ref[mode, 0]
        probe_imag = probe_ref[mode, 1]
        exit_real = (obj_real * probe_real - obj_imag * probe_imag).astype(jnp.bfloat16)
        exit_imag = (obj_real * probe_imag + obj_imag * probe_real).astype(jnp.bfloat16)
        stacked = jnp.concatenate([exit_real, exit_imag], axis=0)
        half = jnp.dot(left_ref[...], stacked, preferred_element_type=jnp.float32).astype(jnp.bfloat16)
        wide = jnp.concatenate([half[:side], half[side:]], axis=1)
        far = jnp.dot(wide, right_ref[...], preferred_element_type=jnp.float32)
        far_ref[mode] = far
        return intensity + far[:, :side] * far[:, :side] + far[:, side:] * far[:, side:]

    intensity = lax.fori_loop(0, modes, one_mode, jnp.zeros((side, side), jnp.float32))
    ratio = amp_ref[0] / jnp.maximum(jnp.sqrt(intensity), amp_floor) - 1.0

    def store(mode, carry):
        far = far_ref[mode]
        out_ref[0, mode, 0] = (far[:, :side] * ratio).astype(jnp.bfloat16)
        out_ref[0, mode, 1] = (far[:, side:] * ratio).astype(jnp.bfloat16)
        return carry

    lax.fori_loop(0, modes, store, 0)


def forward_correction(patch, all_modes, amplitudes, forward_table):
    slots, _, side, _ = patch.shape
    modes = all_modes.shape[0]
    left = complex_table(forward_table, False)
    right = complex_table(forward_table, True)
    return pl.pallas_call(
        forward_kernel,
        grid=(slots,),
        in_specs=[
            pl.BlockSpec((1, 2, side, side), lambda s: (s, 0, 0, 0)),
            pl.BlockSpec((modes, 2, side, side), lambda s: (0, 0, 0, 0), pipeline_mode=pl.Buffered(1)),
            pl.BlockSpec((1, side, side), lambda s: (s, 0, 0)),
            pl.BlockSpec((2 * side, 2 * side), lambda s: (0, 0), pipeline_mode=pl.Buffered(1)),
            pl.BlockSpec((2 * side, 2 * side), lambda s: (0, 0), pipeline_mode=pl.Buffered(1)),
        ],
        out_specs=pl.BlockSpec((1, modes, 2, side, side), lambda s: (s, 0, 0, 0, 0)),
        out_shape=jax.ShapeDtypeStruct((slots, modes, 2, side, side), jnp.bfloat16),
        scratch_shapes=[pltpu.VMEM((modes, side, 2 * side), jnp.float32)],
        compiler_params=pltpu.CompilerParams(vmem_limit_bytes=64 * 1024 * 1024),
        cost_estimate=pl.CostEstimate(
            flops=slots * modes * 4 * (2 * side) ** 2 * side,
            bytes_accessed=slots * (modes + 3) * 2 * side * side * 4,
            transcendentals=slots * side * side,
        ),
    )(patch, all_modes, amplitudes, left, right)


def backward_kernel(block_ref, count_ref, corr_ref, probe_ref, patch_ref, left_ref, right_ref, grad_ref, *part):
    side = patch_ref.shape[-1]
    modes = probe_ref.shape[0]
    slot = pl.program_id(0)
    if part:
        part_ref = part[0]

        @pl.when(slot == 0)
        def _():
            part_ref[...] = jnp.zeros(part_ref.shape, part_ref.dtype)

    live = (slot < count_ref[0]).astype(jnp.float32)
    obj_real = patch_ref[0, 0]
    obj_imag = patch_ref[0, 1]

    def one_mode(mode, carry):
        grad_real, grad_imag = carry
        stacked = jnp.concatenate([corr_ref[0, mode, 0], corr_ref[0, mode, 1]], axis=0)
        half = jnp.dot(left_ref[...], stacked, preferred_element_type=jnp.float32).astype(jnp.bfloat16)
        wide = jnp.concatenate([half[:side], half[side:]], axis=1)
        back = jnp.dot(wide, right_ref[...], preferred_element_type=jnp.float32) * live
        back_real = back[:, :side]
        back_imag = back[:, side:]
        probe_real = probe_ref[mode, 0]
        probe_imag = probe_ref[mode, 1]
        if part:
            part_ref[mode, 0] += obj_real * back_real + obj_imag * back_imag
            part_ref[mode, 1] += obj_real * back_imag - obj_imag * back_real

        grad_real = grad_real + (probe_real * back_real + probe_imag * back_imag)
        grad_imag = grad_imag + (probe_real * back_imag - probe_imag * back_real)
        return grad_real, grad_imag

    zeros = jnp.zeros((side, side), jnp.float32)
    grad_real, grad_imag = lax.fori_loop(0, modes, one_mode, (zeros, zeros))
    grad_ref[0, 0] = grad_real
    grad_ref[0, 1] = grad_imag


def backward_gradients(correction, all_modes, patch, block, count, block_modes, inverse_table, with_partial):
    slots, modes, _, side, _ = correction.shape
    left = complex_table(inverse_table, False)
    right = complex_table(inverse_table, True)
    out_specs = [pl.BlockSpec((1, 2, side, side), lambda s, b, n: (s, 0, 0, 0))]
    out_shape = [jax.ShapeDtypeStruct((slots, 2, side, side), jnp.float32)]
    if with_partial:
        out_specs.append(pl.BlockSpec((block_modes, 2, side, side), lambda s, b, n: (0, 0, 0, 0)))
        out_shape.append(jax.ShapeDtypeStruct((block_modes, 2, side, side), jnp.float32))
    grid_spec = pltpu.PrefetchScalarGridSpec(
        num_scalar_prefetch=2,
        grid=(slots,),
        in_specs=[
            pl.BlockSpec((1, block_modes, 2, side, side), lambda s, b, n: (s, b[0], 0, 0, 0)),
            pl.BlockSpec((block_modes, 2, side, side), lambda s, b, n: (b[0], 0, 0, 0), pipeline_mode=pl.Buffered(1)),
            pl.BlockSpec((1, 2, side, side), lambda s, b, n: (s, 0, 0, 0)),
            pl.BlockSpec((2 * side, 2 * side), lambda s, b, n: (0, 0), pipeline_mode=pl.Buffered(1)),
            pl.BlockSpec((2 * side, 2 * side), lambda s, b, n: (0, 0), pipeline_mode=pl.Buffered(1)),
        ],
        out_specs=out_specs,
    )
    return pl.pallas_call(
        backward_kernel,
        grid_spec=grid_spec,
        out_shape=out_shape,
        compiler_params=pltpu.CompilerParams(
            vmem_limit_bytes=64 * 1024 * 1024, dimension_semantics=("arbitrary",)
        ),
        cost_estimate=pl.CostEstimate(
            flops=slots * block_modes * 4 * (2 * side) ** 2 * side,
            bytes_accessed=slots * (block_modes + 4) * 2 * side * side * 4,
            transcendentals=0,
        ),
    )(
        jnp.reshape(block, (1,)).astype(jnp.int32),
        jnp.reshape(count, (1,)).astype(jnp.int32),
        correction,
        all_modes,
        patch,
        left,
        right,
    )


def shards(object_tiles, probe_modes, amplitudes, offsets, counts):
    side = probe_modes.shape[-1]
    tile_side = object_tiles.shape[-1]
    slots = offsets.shape[1]
    own_modes = probe_modes.shape[0]
    count = lax.axis_size("scan")
    core = lax.axis_index("scan") % 2
    sent = lax.dynamic_index_in_dim(probe_modes, core, 0, keepdims=False)
    pairs = [(s * 2 + m, (s ^ 2) * 2 + 1 - m) for s in range(count) for m in range(2)]
    got = lax.ppermute(sent, ("scan", "mode"), pairs)
    other = lax.dynamic_index_in_dim(probe_modes, 1 - core, 0, keepdims=False)
    mate = lax.ppermute(other, "mode", [(0, 1), (1, 0)])
    partner_modes = jnp.stack([jnp.where(core == 0, got, mate), jnp.where(core == 0, mate, got)])
    component = lax.axis_index("mode")
    all_modes = jnp.where(
        component == 0,
        jnp.concatenate([probe_modes, partner_modes], axis=0),
        jnp.concatenate([partner_modes, probe_modes], axis=0),
    )
    modes_here = all_modes.shape[0]
    own_tile = object_tiles[0]
    east_tile = from_behind(own_tile, "scan", -1)
    south_tile = from_behind(own_tile, "scan", -GCOLS)
    far_corner = lax.ppermute(
        own_tile, "scan", [(s, s - GCOLS - 1) for s in range(count) if (s - GCOLS - 1) % 2 == 1 and s >= GCOLS + 1]
        + [(s, s - GCOLS - 1 + count) for s in range(count) if (s - GCOLS - 1) % 2 == 1 and s < GCOLS + 1]
    )
    near_corner = lax.ppermute(south_tile, "scan", [(s, s - 1) for s in range(count) if s % 2 == 1])
    corner_tile = jnp.where(lax.axis_index("scan") % 2 == 0, near_corner, far_corner)
    upper_band = jnp.concatenate([own_tile, east_tile], axis=2)
    lower_band = jnp.concatenate([south_tile, corner_tile], axis=2)
    extended = jnp.concatenate([upper_band, lower_band], axis=1)
    slot_offsets = offsets[0]
    windows = jnp.stack(
        [
            lax.dynamic_slice(
                extended,
                (0, slot_offsets[slot_id, 0] - 1, slot_offsets[slot_id, 1] - 1),
                (2, side + 2, side + 2),
            )
            for slot_id in range(slots)
        ]
    )
    patch = windows[:, :, 1:-1, 1:-1]
    grad_y = (windows[:, :, 2:, 1:-1] - windows[:, :, :-2, 1:-1]) * 0.5
    grad_x = (windows[:, :, 1:-1, 2:] - windows[:, :, 1:-1, :-2]) * 0.5
    obj_real = patch[:, 0][:, None]
    obj_imag = patch[:, 1][:, None]
    probe_real = all_modes[:, 0][None]
    probe_imag = all_modes[:, 1][None]
    forward_table = dft_tables(side, -1.0)
    inverse_table = dft_tables(side, 1.0)
    correction = forward_correction(patch, all_modes, amplitudes[0], forward_table)
    own_grad, probe_partial = backward_gradients(
        correction, all_modes, patch, component, counts[0], own_modes, inverse_table, True
    )
    (partner_grad,) = backward_gradients(
        correction, all_modes, patch, 1 - component, counts[0], own_modes, inverse_table, False
    )
    whole_grad = own_grad + partner_grad
    position_y = jnp.sum(whole_grad * grad_y, axis=(1, 2, 3))
    position_x = jnp.sum(whole_grad * grad_x, axis=(1, 2, 3))
    positions = jnp.stack([position_y, position_x], axis=1) / side
    mine = lax.dynamic_slice_in_dim(whole_grad, component, 1, axis=1)
    gradient_plane = jnp.zeros((2 * tile_side, 2 * tile_side), jnp.float32)
    for slot_id in range(slots):
        start = (slot_offsets[slot_id, 0], slot_offsets[slot_id, 1])
        current = lax.dynamic_slice(gradient_plane, start, (side, side))
        gradient_plane = lax.dynamic_update_slice(gradient_plane, current + mine[slot_id, 0], start)
    received_east = from_behind(gradient_plane[:tile_side, tile_side:], "scan", 1)
    received_south = from_behind(gradient_plane[tile_side:, :tile_side], "scan", GCOLS)
    received_corner = from_behind(gradient_plane[tile_side:, tile_side:], "scan", GCOLS + 1)
    probe_grad, positions, (received_east, received_south, received_corner) = scan_all_reduce(
        probe_partial, positions, (received_east, received_south, received_corner)
    )
    total_grad = (
        gradient_plane[:tile_side, :tile_side] + received_east + received_south + received_corner
    )
    return (total_grad[None, None], probe_grad, positions[None])


def solution(mesh):
    return jax.shard_map(
        shards,
        mesh=mesh,
        in_specs=(
            P("scan", None, None, None),
            P("mode", None, None, None),
            P("scan", None, None, None),
            P("scan", None, None),
            P("scan"),
        ),
        out_specs=(
            P("scan", "mode", None, None),
            P("mode", None, None, None),
            P("scan", None, None),
        ),
        check_vma=False,
    )
```

```python
import math

import jax
import jax.numpy as jnp
from jax import lax
from jax.experimental import pallas as pl
from jax.experimental.pallas import tpu as pltpu
from jax.sharding import PartitionSpec as P

GCOLS = 8
CORE = (1, 2)
ZLO = (2, 2)
YAX = (4, 4)
XAX = (16, 4)


amp_floor = 1.0


def from_behind(value, axis, steps):
    count = lax.axis_size(axis)
    pairs = [(source, (source + steps) % count) for source in range(count)]
    return lax.ppermute(value, axis, pairs)


def sub_shift(value, sub, shift):
    stride, size = sub
    count = lax.axis_size("scan")
    pairs = []
    for source in range(count):
        coord = (source // stride) % size
        pairs.append((source, source + (((coord + shift) % size) - coord) * stride))
    return lax.ppermute(value, "scan", pairs)


def sub_coord(sub):
    stride, size = sub
    return (lax.axis_index("scan") // stride) % size


def pair_reduce_scatter(data, sub):
    coord = sub_coord(sub)
    half = data.shape[0] // 2
    mine = lax.dynamic_slice_in_dim(data, coord * half, half, axis=0)
    other = lax.dynamic_slice_in_dim(data, (1 - coord) * half, half, axis=0)
    return mine + sub_shift(other, sub, 1)


def pair_all_gather(data, sub):
    coord = sub_coord(sub)
    got = sub_shift(data, sub, 1)
    first = jnp.where(coord == 0, data, got)
    second = jnp.where(coord == 0, got, data)
    return jnp.concatenate([first, second], axis=0)


def direct_reduce_scatter(data, sub):
    size = sub[1]
    coord = sub_coord(sub)
    chunks = data.reshape(size, data.shape[0] // size, -1)
    total = chunks[coord]
    for shift in sorted(range(1, size), key=lambda k: -min(k, size - k)):
        total = total + sub_shift(chunks[(coord + shift) % size], sub, shift)
    return total


def direct_all_gather(data, sub):
    size = sub[1]
    coord = sub_coord(sub)
    out = jnp.zeros((size,) + data.shape, data.dtype)
    out = lax.dynamic_update_index_in_dim(out, data, coord, 0)
    for shift in sorted(range(1, size), key=lambda k: -min(k, size - k)):
        got = sub_shift(data, sub, shift)
        out = lax.dynamic_update_index_in_dim(out, got, (coord - shift) % size, 0)
    return out.reshape(size * data.shape[0], -1)


def ring_reduce_scatter(data, sub):
    size = sub[1]
    coord = sub_coord(sub)
    rows = data.shape[0] // (2 * size)
    fwd = data[: rows * size].reshape(size, rows, -1)
    bwd = data[rows * size :].reshape(size, rows, -1)
    part_f = fwd[(coord - 1) % size]
    part_b = bwd[(coord + 1) % size]
    for step in range(size - 1):
        got_f = sub_shift(part_f, sub, 1)
        got_b = sub_shift(part_b, sub, -1)
        part_f = got_f + fwd[(coord - step - 2) % size]
        part_b = got_b + bwd[(coord + step + 2) % size]
    return jnp.concatenate([part_f, part_b], axis=0)


def ring_all_gather(data, sub):
    size = sub[1]
    coord = sub_coord(sub)
    rows = data.shape[0] // 2
    piece_f = data[:rows]
    piece_b = data[rows:]
    out_f = jnp.zeros((size, rows, data.shape[1]), data.dtype)
    out_b = jnp.zeros((size, rows, data.shape[1]), data.dtype)
    out_f = lax.dynamic_update_index_in_dim(out_f, piece_f, coord, 0)
    out_b = lax.dynamic_update_index_in_dim(out_b, piece_b, coord, 0)
    for step in range(size - 1):
        piece_f = sub_shift(piece_f, sub, 1)
        piece_b = sub_shift(piece_b, sub, -1)
        out_f = lax.dynamic_update_index_in_dim(out_f, piece_f, (coord - step - 1) % size, 0)
        out_b = lax.dynamic_update_index_in_dim(out_b, piece_b, (coord + step + 1) % size, 0)
    return jnp.concatenate([out_f.reshape(size * rows, -1), out_b.reshape(size * rows, -1)], axis=0)


def scan_all_reduce(value, early, tied):
    shape = value.shape
    data = value.reshape(-1, shape[-1])
    data = pair_reduce_scatter(data, CORE)
    data = direct_reduce_scatter(data, XAX)
    data = direct_reduce_scatter(data, YAX)
    data = data + sub_shift(data, ZLO, 1)
    data, early, tied = lax.optimization_barrier((data, early, tied))
    data = direct_all_gather(data, YAX)
    data = direct_all_gather(data, XAX)
    data = pair_all_gather(data, CORE)
    return data.reshape(shape), early, tied


def dft_tables(length_side, direction_sign):
    index_row = jnp.arange(length_side, dtype=jnp.int32)
    product = index_row[:, None] * index_row[None, :] % length_side
    angles = product.astype(jnp.float32) * (2.0 * math.pi / length_side)
    scale_factor = 1.0 / math.sqrt(length_side)
    real_part = jnp.cos(angles) * scale_factor
    imag_part = direction_sign * jnp.sin(angles) * scale_factor
    matrix_table = jnp.stack(
        [jnp.stack([real_part, -imag_part]), jnp.stack([imag_part, real_part])]
    )
    return matrix_table.astype(jnp.bfloat16)


def transform(field, matrix_table):
    first_section = jnp.einsum(
        "dcpq,bcqk->bdpk", matrix_table, field, preferred_element_type=jnp.float32
    ).astype(jnp.bfloat16)
    return jnp.einsum(
        "bcpq,dcqk->bdpk", first_section, matrix_table, preferred_element_type=jnp.float32
    )


def complex_table(matrix_table, transposed):
    if transposed:
        rows = [jnp.concatenate([matrix_table[0, c], matrix_table[1, c]], axis=1) for c in range(2)]
    else:
        rows = [jnp.concatenate([matrix_table[d, 0], matrix_table[d, 1]], axis=1) for d in range(2)]
    return jnp.concatenate(rows, axis=0)


def forward_kernel(patch_ref, probe_ref, amp_ref, left_ref, right_ref, out_ref, far_ref):
    side = patch_ref.shape[-1]
    modes = probe_ref.shape[0]
    obj_real = patch_ref[0, 0]
    obj_imag = patch_ref[0, 1]

    def one_mode(mode, intensity):
        probe_real = probe_ref[mode, 0]
        probe_imag = probe_ref[mode, 1]
        exit_real = (obj_real * probe_real - obj_imag * probe_imag).astype(jnp.bfloat16)
        exit_imag = (obj_real * probe_imag + obj_imag * probe_real).astype(jnp.bfloat16)
        stacked = jnp.concatenate([exit_real, exit_imag], axis=0)
        half = jnp.dot(left_ref[...], stacked, preferred_element_type=jnp.float32).astype(jnp.bfloat16)
        wide = jnp.concatenate([half[:side], half[side:]], axis=1)
        far = jnp.dot(wide, right_ref[...], preferred_element_type=jnp.float32)
        far_ref[mode] = far
        return intensity + far[:, :side] * far[:, :side] + far[:, side:] * far[:, side:]

    intensity = lax.fori_loop(0, modes, one_mode, jnp.zeros((side, side), jnp.float32))
    ratio = amp_ref[0] / jnp.maximum(jnp.sqrt(intensity), amp_floor) - 1.0

    def store(mode, carry):
        far = far_ref[mode]
        out_ref[0, mode, 0] = (far[:, :side] * ratio).astype(jnp.bfloat16)
        out_ref[0, mode, 1] = (far[:, side:] * ratio).astype(jnp.bfloat16)
        return carry

    lax.fori_loop(0, modes, store, 0)


def forward_correction(patch, all_modes, amplitudes, forward_table):
    slots, _, side, _ = patch.shape
    modes = all_modes.shape[0]
    left = complex_table(forward_table, False)
    right = complex_table(forward_table, True)
    return pl.pallas_call(
        forward_kernel,
        grid=(slots,),
        in_specs=[
            pl.BlockSpec((1, 2, side, side), lambda s: (s, 0, 0, 0)),
            pl.BlockSpec((modes, 2, side, side), lambda s: (0, 0, 0, 0), pipeline_mode=pl.Buffered(1)),
            pl.BlockSpec((1, side, side), lambda s: (s, 0, 0)),
            pl.BlockSpec((2 * side, 2 * side), lambda s: (0, 0), pipeline_mode=pl.Buffered(1)),
            pl.BlockSpec((2 * side, 2 * side), lambda s: (0, 0), pipeline_mode=pl.Buffered(1)),
        ],
        out_specs=pl.BlockSpec((1, modes, 2, side, side), lambda s: (s, 0, 0, 0, 0)),
        out_shape=jax.ShapeDtypeStruct((slots, modes, 2, side, side), jnp.bfloat16),
        scratch_shapes=[pltpu.VMEM((modes, side, 2 * side), jnp.float32)],
        compiler_params=pltpu.CompilerParams(vmem_limit_bytes=64 * 1024 * 1024),
        cost_estimate=pl.CostEstimate(
            flops=slots * modes * 4 * (2 * side) ** 2 * side,
            bytes_accessed=slots * (modes + 3) * 2 * side * side * 4,
            transcendentals=slots * side * side,
        ),
    )(patch, all_modes, amplitudes, left, right)


def backward_kernel(block_ref, count_ref, corr_ref, probe_ref, patch_ref, left_ref, right_ref, grad_ref, *part):
    side = patch_ref.shape[-1]
    modes = probe_ref.shape[0]
    slot = pl.program_id(0)
    if part:
        part_ref = part[0]

        @pl.when(slot == 0)
        def _():
            part_ref[...] = jnp.zeros(part_ref.shape, part_ref.dtype)

    live = (slot < count_ref[0]).astype(jnp.float32)
    obj_real = patch_ref[0, 0]
    obj_imag = patch_ref[0, 1]

    def one_mode(mode, carry):
        grad_real, grad_imag = carry
        stacked = jnp.concatenate([corr_ref[0, mode, 0], corr_ref[0, mode, 1]], axis=0)
        half = jnp.dot(left_ref[...], stacked, preferred_element_type=jnp.float32).astype(jnp.bfloat16)
        wide = jnp.concatenate([half[:side], half[side:]], axis=1)
        back = jnp.dot(wide, right_ref[...], preferred_element_type=jnp.float32) * live
        back_real = back[:, :side]
        back_imag = back[:, side:]
        probe_real = probe_ref[mode, 0]
        probe_imag = probe_ref[mode, 1]
        if part:
            part_ref[mode, 0] += obj_real * back_real + obj_imag * back_imag
            part_ref[mode, 1] += obj_real * back_imag - obj_imag * back_real

        grad_real = grad_real + (probe_real * back_real + probe_imag * back_imag)
        grad_imag = grad_imag + (probe_real * back_imag - probe_imag * back_real)
        return grad_real, grad_imag

    zeros = jnp.zeros((side, side), jnp.float32)
    grad_real, grad_imag = lax.fori_loop(0, modes, one_mode, (zeros, zeros))
    grad_ref[0, 0] = grad_real
    grad_ref[0, 1] = grad_imag


def backward_gradients(correction, all_modes, patch, block, count, block_modes, inverse_table, with_partial):
    slots, modes, _, side, _ = correction.shape
    left = complex_table(inverse_table, False)
    right = complex_table(inverse_table, True)
    out_specs = [pl.BlockSpec((1, 2, side, side), lambda s, b, n: (s, 0, 0, 0))]
    out_shape = [jax.ShapeDtypeStruct((slots, 2, side, side), jnp.float32)]
    if with_partial:
        out_specs.append(pl.BlockSpec((block_modes, 2, side, side), lambda s, b, n: (0, 0, 0, 0)))
        out_shape.append(jax.ShapeDtypeStruct((block_modes, 2, side, side), jnp.float32))
    grid_spec = pltpu.PrefetchScalarGridSpec(
        num_scalar_prefetch=2,
        grid=(slots,),
        in_specs=[
            pl.BlockSpec((1, block_modes, 2, side, side), lambda s, b, n: (s, b[0], 0, 0, 0)),
            pl.BlockSpec((block_modes, 2, side, side), lambda s, b, n: (b[0], 0, 0, 0), pipeline_mode=pl.Buffered(1)),
            pl.BlockSpec((1, 2, side, side), lambda s, b, n: (s, 0, 0, 0)),
            pl.BlockSpec((2 * side, 2 * side), lambda s, b, n: (0, 0), pipeline_mode=pl.Buffered(1)),
            pl.BlockSpec((2 * side, 2 * side), lambda s, b, n: (0, 0), pipeline_mode=pl.Buffered(1)),
        ],
        out_specs=out_specs,
    )
    return pl.pallas_call(
        backward_kernel,
        grid_spec=grid_spec,
        out_shape=out_shape,
        compiler_params=pltpu.CompilerParams(
            vmem_limit_bytes=64 * 1024 * 1024, dimension_semantics=("arbitrary",)
        ),
        cost_estimate=pl.CostEstimate(
            flops=slots * block_modes * 4 * (2 * side) ** 2 * side,
            bytes_accessed=slots * (block_modes + 4) * 2 * side * side * 4,
            transcendentals=0,
        ),
    )(
        jnp.reshape(block, (1,)).astype(jnp.int32),
        jnp.reshape(count, (1,)).astype(jnp.int32),
        correction,
        all_modes,
        patch,
        left,
        right,
    )


def shards(object_tiles, probe_modes, amplitudes, offsets, counts):
    side = probe_modes.shape[-1]
    tile_side = object_tiles.shape[-1]
    slots = offsets.shape[1]
    own_modes = probe_modes.shape[0]
    count = lax.axis_size("scan")
    core = lax.axis_index("scan") % 2
    sent = lax.dynamic_index_in_dim(probe_modes, core, 0, keepdims=False)
    pairs = [(s * 2 + m, (s ^ 2) * 2 + 1 - m) for s in range(count) for m in range(2)]
    got = lax.ppermute(sent, ("scan", "mode"), pairs)
    other = lax.dynamic_index_in_dim(probe_modes, 1 - core, 0, keepdims=False)
    mate = lax.ppermute(other, "mode", [(0, 1), (1, 0)])
    partner_modes = jnp.stack([jnp.where(core == 0, got, mate), jnp.where(core == 0, mate, got)])
    component = lax.axis_index("mode")
    all_modes = jnp.where(
        component == 0,
        jnp.concatenate([probe_modes, partner_modes], axis=0),
        jnp.concatenate([partner_modes, probe_modes], axis=0),
    )
    modes_here = all_modes.shape[0]
    own_tile = object_tiles[0]
    east_tile = from_behind(own_tile, "scan", -1)
    south_tile = from_behind(own_tile, "scan", -GCOLS)
    far_corner = lax.ppermute(
        own_tile, "scan", [(s, s - GCOLS - 1) for s in range(count) if (s - GCOLS - 1) % 2 == 1 and s >= GCOLS + 1]
        + [(s, s - GCOLS - 1 + count) for s in range(count) if (s - GCOLS - 1) % 2 == 1 and s < GCOLS + 1]
    )
    near_corner = lax.ppermute(south_tile, "scan", [(s, s - 1) for s in range(count) if s % 2 == 1])
    corner_tile = jnp.where(lax.axis_index("scan") % 2 == 0, near_corner, far_corner)
    upper_band = jnp.concatenate([own_tile, east_tile], axis=2)
    lower_band = jnp.concatenate([south_tile, corner_tile], axis=2)
    extended = jnp.concatenate([upper_band, lower_band], axis=1)
    slot_offsets = offsets[0]
    windows = jnp.stack(
        [
            lax.dynamic_slice(
                extended,
                (0, slot_offsets[slot_id, 0] - 1, slot_offsets[slot_id, 1] - 1),
                (2, side + 2, side + 2),
            )
            for slot_id in range(slots)
        ]
    )
    patch = windows[:, :, 1:-1, 1:-1]
    grad_y = (windows[:, :, 2:, 1:-1] - windows[:, :, :-2, 1:-1]) * 0.5
    grad_x = (windows[:, :, 1:-1, 2:] - windows[:, :, 1:-1, :-2]) * 0.5
    obj_real = patch[:, 0][:, None]
    obj_imag = patch[:, 1][:, None]
    probe_real = all_modes[:, 0][None]
    probe_imag = all_modes[:, 1][None]
    forward_table = dft_tables(side, -1.0)
    inverse_table = dft_tables(side, 1.0)
    correction = forward_correction(patch, all_modes, amplitudes[0], forward_table)
    own_grad, probe_partial = backward_gradients(
        correction, all_modes, patch, component, counts[0], own_modes, inverse_table, True
    )
    (partner_grad,) = backward_gradients(
        correction, all_modes, patch, 1 - component, counts[0], own_modes, inverse_table, False
    )
    whole_grad = own_grad + partner_grad
    position_y = jnp.sum(whole_grad * grad_y, axis=(1, 2, 3))
    position_x = jnp.sum(whole_grad * grad_x, axis=(1, 2, 3))
    positions = jnp.stack([position_y, position_x], axis=1) / side
    mine = lax.dynamic_slice_in_dim(whole_grad, component, 1, axis=1)
    gradient_plane = jnp.zeros((2 * tile_side, 2 * tile_side), jnp.float32)
    for slot_id in range(slots):
        start = (slot_offsets[slot_id, 0], slot_offsets[slot_id, 1])
        current = lax.dynamic_slice(gradient_plane, start, (side, side))
        gradient_plane = lax.dynamic_update_slice(gradient_plane, current + mine[slot_id, 0], start)
    received_east = from_behind(gradient_plane[:tile_side, tile_side:], "scan", 1)
    received_south = from_behind(gradient_plane[tile_side:, :tile_side], "scan", GCOLS)
    received_corner = from_behind(gradient_plane[tile_side:, tile_side:], "scan", GCOLS + 1)
    probe_grad, positions, (received_east, received_south, received_corner) = scan_all_reduce(
        probe_partial, positions, (received_east, received_south, received_corner)
    )
    total_grad = (
        gradient_plane[:tile_side, :tile_side] + received_east + received_south + received_corner
    )
    return (total_grad[None, None], probe_grad, positions[None])


def solution(mesh):
    return jax.shard_map(
        shards,
        mesh=mesh,
        in_specs=(
            P("scan", None, None, None),
            P("mode", None, None, None),
            P("scan", None, None, None),
            P("scan", None, None),
            P("scan"),
        ),
        out_specs=(
            P("scan", "mode", None, None),
            P("mode", None, None, None),
            P("scan", None, None),
        ),
        check_vma=False,
    )
```

```python
import math

import jax
import jax.numpy as jnp
from jax import lax
from jax.experimental import pallas as pl
from jax.experimental.pallas import tpu as pltpu
from jax.sharding import PartitionSpec as P

GCOLS = 8
CORE = (1, 2)
ZLO = (2, 2)
YAX = (4, 4)
XAX = (16, 4)


amp_floor = 1.0


def from_behind(value, axis, steps):
    count = lax.axis_size(axis)
    pairs = [(source, (source + steps) % count) for source in range(count)]
    return lax.ppermute(value, axis, pairs)


def sub_shift(value, sub, shift):
    stride, size = sub
    count = lax.axis_size("scan")
    pairs = []
    for source in range(count):
        coord = (source // stride) % size
        pairs.append((source, source + (((coord + shift) % size) - coord) * stride))
    return lax.ppermute(value, "scan", pairs)


def sub_coord(sub):
    stride, size = sub
    return (lax.axis_index("scan") // stride) % size


def pair_reduce_scatter(data, sub):
    coord = sub_coord(sub)
    half = data.shape[0] // 2
    mine = lax.dynamic_slice_in_dim(data, coord * half, half, axis=0)
    other = lax.dynamic_slice_in_dim(data, (1 - coord) * half, half, axis=0)
    return mine + sub_shift(other, sub, 1)


def pair_all_gather(data, sub):
    coord = sub_coord(sub)
    got = sub_shift(data, sub, 1)
    first = jnp.where(coord == 0, data, got)
    second = jnp.where(coord == 0, got, data)
    return jnp.concatenate([first, second], axis=0)


def direct_reduce_scatter(data, sub):
    size = sub[1]
    coord = sub_coord(sub)
    chunks = data.reshape(size, data.shape[0] // size, -1)
    total = chunks[coord]
    for shift in range(1, size):
        total = total + sub_shift(chunks[(coord + shift) % size], sub, shift)
    return total


def direct_all_gather(data, sub):
    size = sub[1]
    coord = sub_coord(sub)
    out = jnp.zeros((size,) + data.shape, data.dtype)
    out = lax.dynamic_update_index_in_dim(out, data, coord, 0)
    for shift in range(1, size):
        got = sub_shift(data, sub, shift)
        out = lax.dynamic_update_index_in_dim(out, got, (coord - shift) % size, 0)
    return out.reshape(size * data.shape[0], -1)


def ring_reduce_scatter(data, sub):
    size = sub[1]
    coord = sub_coord(sub)
    rows = data.shape[0] // (2 * size)
    fwd = data[: rows * size].reshape(size, rows, -1)
    bwd = data[rows * size :].reshape(size, rows, -1)
    part_f = fwd[(coord - 1) % size]
    part_b = bwd[(coord + 1) % size]
    for step in range(size - 1):
        got_f = sub_shift(part_f, sub, 1)
        got_b = sub_shift(part_b, sub, -1)
        part_f = got_f + fwd[(coord - step - 2) % size]
        part_b = got_b + bwd[(coord + step + 2) % size]
    return jnp.concatenate([part_f, part_b], axis=0)


def ring_all_gather(data, sub):
    size = sub[1]
    coord = sub_coord(sub)
    rows = data.shape[0] // 2
    piece_f = data[:rows]
    piece_b = data[rows:]
    out_f = jnp.zeros((size, rows, data.shape[1]), data.dtype)
    out_b = jnp.zeros((size, rows, data.shape[1]), data.dtype)
    out_f = lax.dynamic_update_index_in_dim(out_f, piece_f, coord, 0)
    out_b = lax.dynamic_update_index_in_dim(out_b, piece_b, coord, 0)
    for step in range(size - 1):
        piece_f = sub_shift(piece_f, sub, 1)
        piece_b = sub_shift(piece_b, sub, -1)
        out_f = lax.dynamic_update_index_in_dim(out_f, piece_f, (coord - step - 1) % size, 0)
        out_b = lax.dynamic_update_index_in_dim(out_b, piece_b, (coord + step + 1) % size, 0)
    return jnp.concatenate([out_f.reshape(size * rows, -1), out_b.reshape(size * rows, -1)], axis=0)


def scan_all_reduce(value, early, tied):
    shape = value.shape
    data = value.reshape(-1, shape[-1])
    data = pair_reduce_scatter(data, CORE)
    data = direct_reduce_scatter(data, XAX)
    data = direct_reduce_scatter(data, YAX)
    data, early, tied = lax.optimization_barrier((data, early, tied))
    data = data + sub_shift(data, ZLO, 1)
    data = direct_all_gather(data, YAX)
    data = direct_all_gather(data, XAX)
    data = pair_all_gather(data, CORE)
    return data.reshape(shape), early, tied


def dft_tables(length_side, direction_sign):
    index_row = jnp.arange(length_side, dtype=jnp.int32)
    product = index_row[:, None] * index_row[None, :] % length_side
    angles = product.astype(jnp.float32) * (2.0 * math.pi / length_side)
    scale_factor = 1.0 / math.sqrt(length_side)
    real_part = jnp.cos(angles) * scale_factor
    imag_part = direction_sign * jnp.sin(angles) * scale_factor
    matrix_table = jnp.stack(
        [jnp.stack([real_part, -imag_part]), jnp.stack([imag_part, real_part])]
    )
    return matrix_table.astype(jnp.bfloat16)


def transform(field, matrix_table):
    first_section = jnp.einsum(
        "dcpq,bcqk->bdpk", matrix_table, field, preferred_element_type=jnp.float32
    ).astype(jnp.bfloat16)
    return jnp.einsum(
        "bcpq,dcqk->bdpk", first_section, matrix_table, preferred_element_type=jnp.float32
    )


def complex_table(matrix_table, transposed):
    if transposed:
        rows = [jnp.concatenate([matrix_table[0, c], matrix_table[1, c]], axis=1) for c in range(2)]
    else:
        rows = [jnp.concatenate([matrix_table[d, 0], matrix_table[d, 1]], axis=1) for d in range(2)]
    return jnp.concatenate(rows, axis=0)


def forward_kernel(patch_ref, probe_ref, amp_ref, left_ref, right_ref, out_ref, far_ref):
    side = patch_ref.shape[-1]
    modes = probe_ref.shape[0]
    obj_real = patch_ref[0, 0]
    obj_imag = patch_ref[0, 1]

    def one_mode(mode, intensity):
        probe_real = probe_ref[mode, 0]
        probe_imag = probe_ref[mode, 1]
        exit_real = (obj_real * probe_real - obj_imag * probe_imag).astype(jnp.bfloat16)
        exit_imag = (obj_real * probe_imag + obj_imag * probe_real).astype(jnp.bfloat16)
        stacked = jnp.concatenate([exit_real, exit_imag], axis=0)
        half = jnp.dot(left_ref[...], stacked, preferred_element_type=jnp.float32).astype(jnp.bfloat16)
        wide = jnp.concatenate([half[:side], half[side:]], axis=1)
        far = jnp.dot(wide, right_ref[...], preferred_element_type=jnp.float32)
        far_ref[mode] = far
        return intensity + far[:, :side] * far[:, :side] + far[:, side:] * far[:, side:]

    intensity = lax.fori_loop(0, modes, one_mode, jnp.zeros((side, side), jnp.float32))
    ratio = amp_ref[0] / jnp.maximum(jnp.sqrt(intensity), amp_floor) - 1.0

    def store(mode, carry):
        far = far_ref[mode]
        out_ref[0, mode, 0] = (far[:, :side] * ratio).astype(jnp.bfloat16)
        out_ref[0, mode, 1] = (far[:, side:] * ratio).astype(jnp.bfloat16)
        return carry

    lax.fori_loop(0, modes, store, 0)


def forward_correction(patch, all_modes, amplitudes, forward_table):
    slots, _, side, _ = patch.shape
    modes = all_modes.shape[0]
    left = complex_table(forward_table, False)
    right = complex_table(forward_table, True)
    return pl.pallas_call(
        forward_kernel,
        grid=(slots,),
        in_specs=[
            pl.BlockSpec((1, 2, side, side), lambda s: (s, 0, 0, 0)),
            pl.BlockSpec((modes, 2, side, side), lambda s: (0, 0, 0, 0), pipeline_mode=pl.Buffered(1)),
            pl.BlockSpec((1, side, side), lambda s: (s, 0, 0)),
            pl.BlockSpec((2 * side, 2 * side), lambda s: (0, 0), pipeline_mode=pl.Buffered(1)),
            pl.BlockSpec((2 * side, 2 * side), lambda s: (0, 0), pipeline_mode=pl.Buffered(1)),
        ],
        out_specs=pl.BlockSpec((1, modes, 2, side, side), lambda s: (s, 0, 0, 0, 0)),
        out_shape=jax.ShapeDtypeStruct((slots, modes, 2, side, side), jnp.bfloat16),
        scratch_shapes=[pltpu.VMEM((modes, side, 2 * side), jnp.float32)],
        compiler_params=pltpu.CompilerParams(vmem_limit_bytes=64 * 1024 * 1024),
        cost_estimate=pl.CostEstimate(
            flops=slots * modes * 4 * (2 * side) ** 2 * side,
            bytes_accessed=slots * (modes + 3) * 2 * side * side * 4,
            transcendentals=slots * side * side,
        ),
    )(patch, all_modes, amplitudes, left, right)


def backward_kernel(block_ref, count_ref, corr_ref, probe_ref, patch_ref, left_ref, right_ref, grad_ref, *part):
    side = patch_ref.shape[-1]
    modes = probe_ref.shape[0]
    slot = pl.program_id(0)
    if part:
        part_ref = part[0]

        @pl.when(slot == 0)
        def _():
            part_ref[...] = jnp.zeros(part_ref.shape, part_ref.dtype)

    live = (slot < count_ref[0]).astype(jnp.float32)
    obj_real = patch_ref[0, 0]
    obj_imag = patch_ref[0, 1]

    def one_mode(mode, carry):
        grad_real, grad_imag = carry
        stacked = jnp.concatenate([corr_ref[0, mode, 0], corr_ref[0, mode, 1]], axis=0)
        half = jnp.dot(left_ref[...], stacked, preferred_element_type=jnp.float32).astype(jnp.bfloat16)
        wide = jnp.concatenate([half[:side], half[side:]], axis=1)
        back = jnp.dot(wide, right_ref[...], preferred_element_type=jnp.float32) * live
        back_real = back[:, :side]
        back_imag = back[:, side:]
        probe_real = probe_ref[mode, 0]
        probe_imag = probe_ref[mode, 1]
        if part:
            part_ref[mode, 0] += obj_real * back_real + obj_imag * back_imag
            part_ref[mode, 1] += obj_real * back_imag - obj_imag * back_real

        grad_real = grad_real + (probe_real * back_real + probe_imag * back_imag)
        grad_imag = grad_imag + (probe_real * back_imag - probe_imag * back_real)
        return grad_real, grad_imag

    zeros = jnp.zeros((side, side), jnp.float32)
    grad_real, grad_imag = lax.fori_loop(0, modes, one_mode, (zeros, zeros))
    grad_ref[0, 0] = grad_real
    grad_ref[0, 1] = grad_imag


def backward_gradients(correction, all_modes, patch, block, count, block_modes, inverse_table, with_partial):
    slots, modes, _, side, _ = correction.shape
    left = complex_table(inverse_table, False)
    right = complex_table(inverse_table, True)
    out_specs = [pl.BlockSpec((1, 2, side, side), lambda s, b, n: (s, 0, 0, 0))]
    out_shape = [jax.ShapeDtypeStruct((slots, 2, side, side), jnp.float32)]
    if with_partial:
        out_specs.append(pl.BlockSpec((block_modes, 2, side, side), lambda s, b, n: (0, 0, 0, 0)))
        out_shape.append(jax.ShapeDtypeStruct((block_modes, 2, side, side), jnp.float32))
    grid_spec = pltpu.PrefetchScalarGridSpec(
        num_scalar_prefetch=2,
        grid=(slots,),
        in_specs=[
            pl.BlockSpec((1, block_modes, 2, side, side), lambda s, b, n: (s, b[0], 0, 0, 0)),
            pl.BlockSpec((block_modes, 2, side, side), lambda s, b, n: (b[0], 0, 0, 0), pipeline_mode=pl.Buffered(1)),
            pl.BlockSpec((1, 2, side, side), lambda s, b, n: (s, 0, 0, 0)),
            pl.BlockSpec((2 * side, 2 * side), lambda s, b, n: (0, 0), pipeline_mode=pl.Buffered(1)),
            pl.BlockSpec((2 * side, 2 * side), lambda s, b, n: (0, 0), pipeline_mode=pl.Buffered(1)),
        ],
        out_specs=out_specs,
    )
    return pl.pallas_call(
        backward_kernel,
        grid_spec=grid_spec,
        out_shape=out_shape,
        compiler_params=pltpu.CompilerParams(
            vmem_limit_bytes=64 * 1024 * 1024, dimension_semantics=("arbitrary",)
        ),
        cost_estimate=pl.CostEstimate(
            flops=slots * block_modes * 4 * (2 * side) ** 2 * side,
            bytes_accessed=slots * (block_modes + 4) * 2 * side * side * 4,
            transcendentals=0,
        ),
    )(
        jnp.reshape(block, (1,)).astype(jnp.int32),
        jnp.reshape(count, (1,)).astype(jnp.int32),
        correction,
        all_modes,
        patch,
        left,
        right,
    )


def shards(object_tiles, probe_modes, amplitudes, offsets, counts):
    side = probe_modes.shape[-1]
    tile_side = object_tiles.shape[-1]
    slots = offsets.shape[1]
    own_modes = probe_modes.shape[0]
    count = lax.axis_size("scan")
    core = lax.axis_index("scan") % 2
    sent = lax.dynamic_index_in_dim(probe_modes, core, 0, keepdims=False)
    pairs = [(s * 2 + m, (s ^ 2) * 2 + 1 - m) for s in range(count) for m in range(2)]
    got = lax.ppermute(sent, ("scan", "mode"), pairs)
    other = lax.dynamic_index_in_dim(probe_modes, 1 - core, 0, keepdims=False)
    mate = lax.ppermute(other, "mode", [(0, 1), (1, 0)])
    partner_modes = jnp.stack([jnp.where(core == 0, got, mate), jnp.where(core == 0, mate, got)])
    component = lax.axis_index("mode")
    all_modes = jnp.where(
        component == 0,
        jnp.concatenate([probe_modes, partner_modes], axis=0),
        jnp.concatenate([partner_modes, probe_modes], axis=0),
    )
    modes_here = all_modes.shape[0]
    own_tile = object_tiles[0]
    east_tile = from_behind(own_tile, "scan", -1)
    south_tile = from_behind(own_tile, "scan", -GCOLS)
    far_corner = lax.ppermute(
        own_tile, "scan", [(s, s - GCOLS - 1) for s in range(count) if (s - GCOLS - 1) % 2 == 1 and s >= GCOLS + 1]
        + [(s, s - GCOLS - 1 + count) for s in range(count) if (s - GCOLS - 1) % 2 == 1 and s < GCOLS + 1]
    )
    near_corner = lax.ppermute(south_tile, "scan", [(s, s - 1) for s in range(count) if s % 2 == 1])
    corner_tile = jnp.where(lax.axis_index("scan") % 2 == 0, near_corner, far_corner)
    upper_band = jnp.concatenate([own_tile, east_tile], axis=2)
    lower_band = jnp.concatenate([south_tile, corner_tile], axis=2)
    extended = jnp.concatenate([upper_band, lower_band], axis=1)
    slot_offsets = offsets[0]
    windows = jnp.stack(
        [
            lax.dynamic_slice(
                extended,
                (0, slot_offsets[slot_id, 0] - 1, slot_offsets[slot_id, 1] - 1),
                (2, side + 2, side + 2),
            )
            for slot_id in range(slots)
        ]
    )
    patch = windows[:, :, 1:-1, 1:-1]
    grad_y = (windows[:, :, 2:, 1:-1] - windows[:, :, :-2, 1:-1]) * 0.5
    grad_x = (windows[:, :, 1:-1, 2:] - windows[:, :, 1:-1, :-2]) * 0.5
    obj_real = patch[:, 0][:, None]
    obj_imag = patch[:, 1][:, None]
    probe_real = all_modes[:, 0][None]
    probe_imag = all_modes[:, 1][None]
    forward_table = dft_tables(side, -1.0)
    inverse_table = dft_tables(side, 1.0)
    correction = forward_correction(patch, all_modes, amplitudes[0], forward_table)
    own_grad, probe_partial = backward_gradients(
        correction, all_modes, patch, component, counts[0], own_modes, inverse_table, True
    )
    (partner_grad,) = backward_gradients(
        correction, all_modes, patch, 1 - component, counts[0], own_modes, inverse_table, False
    )
    whole_grad = own_grad + partner_grad
    position_y = jnp.sum(whole_grad * grad_y, axis=(1, 2, 3))
    position_x = jnp.sum(whole_grad * grad_x, axis=(1, 2, 3))
    positions = jnp.stack([position_y, position_x], axis=1) / side
    mine = lax.dynamic_slice_in_dim(whole_grad, component, 1, axis=1)
    gradient_plane = jnp.zeros((2 * tile_side, 2 * tile_side), jnp.float32)
    for slot_id in range(slots):
        start = (slot_offsets[slot_id, 0], slot_offsets[slot_id, 1])
        current = lax.dynamic_slice(gradient_plane, start, (side, side))
        gradient_plane = lax.dynamic_update_slice(gradient_plane, current + mine[slot_id, 0], start)
    received_east = from_behind(gradient_plane[:tile_side, tile_side:], "scan", 1)
    received_south = from_behind(gradient_plane[tile_side:, :tile_side], "scan", GCOLS)
    received_corner = from_behind(gradient_plane[tile_side:, tile_side:], "scan", GCOLS + 1)
    probe_grad, positions, (received_east, received_south, received_corner) = scan_all_reduce(
        probe_partial, positions, (received_east, received_south, received_corner)
    )
    total_grad = (
        gradient_plane[:tile_side, :tile_side] + received_east + received_south + received_corner
    )
    return (total_grad[None, None], probe_grad, positions[None])


def solution(mesh):
    return jax.shard_map(
        shards,
        mesh=mesh,
        in_specs=(
            P("scan", None, None, None),
            P("mode", None, None, None),
            P("scan", None, None, None),
            P("scan", None, None),
            P("scan"),
        ),
        out_specs=(
            P("scan", "mode", None, None),
            P("mode", None, None, None),
            P("scan", None, None),
        ),
        check_vma=False,
    )
```
